512 devices in a mesh: sta: 32 (over z_lo, y), src: 16 (over z_hi, x, core).
Axes of the slice: x: 4, y: 4, z: 16 (z_hi: 2, z_lo: 8; z = z_hi * 8 + z_lo), core: 2. Of those that a mesh axis runs over, the one named last changes fastest.
Arguments:
- green_real: bfloat16 [4096, 32768], P('sta', 'src'), may hold values from -0.2541165 to 0.2541165
- green_imag: bfloat16 [4096, 32768], P('sta', 'src'), may hold values from -0.2541165 to 0.2541165
- station_vec: float32 [2, 32, 4096], P(None, 'src', 'sta'), may hold values from -6 to 6
- source_vec: float32 [2, 32, 32768], P(None, 'sta', 'src'), may hold values from -6 to 6
- search_dir: float32 [2, 32, 32768], P(None, 'sta', 'src'), may hold values from -6 to 6
- solution: float32 [2, 32, 32768], P(None, 'sta', 'src'), may hold values from -6 to 6
- alpha_now: float32 [32], replicated, may hold values from 0.5 to 2
- rho_bar: float32 [32], replicated, may hold values from 0.5 to 2
- phi_bar: float32 [32], replicated, may hold values from 0.5 to 2
Outputs:
- station_out: float32 [2, 32, 4096], P(None, 'src', 'sta')
- source_out: float32 [2, 32, 32768], P(None, 'sta', 'src')
- search_out: float32 [2, 32, 32768], P(None, 'sta', 'src')
- solution_out: float32 [2, 32, 32768], P(None, 'sta', 'src')
- alpha_out: float32 [32], replicated
- rho_bar_out: float32 [32], replicated
- phi_bar_out: float32 [32], replicated
The draws below stay inside these ranges and needn't reach their ends.
All inputs are finite; a program needn't handle non-finite values.
Results may differ from the reference program's by a relative error of at most 0.019.
Values may be sent and summed in bfloat16 or wider, within the bound.
A program may use at most 64 MiB of HBM per device.

```python
import math
import jax
import jax.numpy as jnp
from jax import lax

EVENTS = 32
ITERS = 3
ROWS = 4096
COLS = 32768


def green_scales(key):
    row_pos = jnp.arange(ROWS, dtype=jnp.float32) / ROWS
    col_pos = jnp.arange(COLS, dtype=jnp.float32) / COLS
    row_rough = jax.random.uniform(jax.random.fold_in(key, 11), (ROWS,), jnp.float32)
    col_rough = jax.random.uniform(jax.random.fold_in(key, 12), (COLS,), jnp.float32)
    row_scale = jnp.exp(math.log(3.0) * row_pos + math.log(10.0) * row_rough)
    col_scale = jnp.exp(math.log(3.0) * col_pos + math.log(10.0) * col_rough)
    return (row_scale, col_scale)


def green_entries(key, which):
    row_scale, col_scale = green_scales(key)
    entry_key = jax.random.fold_in(key, which)
    values = jax.random.truncated_normal(entry_key, -4.0, 4.0, (ROWS, COLS), jnp.float32)
    factor = 1.0 / (78.3 * math.sqrt(COLS))
    return (values * row_scale[:, None] * col_scale[None, :] * factor).astype(jnp.bfloat16)


def draw_green_real(key, part):
    return green_entries(key, 21)


def draw_green_imag(key, part):
    return green_entries(key, 22)


def raised(values, own_key, source, target, shards_of, factor):
    def block_of(position):
        return (jnp.arange(values.shape[position]) // (values.shape[position] // shards_of)).reshape((-1,) + (1,) * (values.ndim - 1 - position))

    near = jax.random.permutation(own_key, shards_of)[block_of(target)]
    second = (block_of(target) + shards_of // 2) % shards_of
    return jnp.where((block_of(source) == near) | (block_of(source) == second), factor * values, values)


def steps_of(own_key, dims, split, least, largest):
    factor_of = 1.0
    for dim, shards_of in split:
        steps = jax.random.uniform(jax.random.fold_in(jax.random.fold_in(own_key, 6), dim), (shards_of,), jnp.float32, least / len(split), largest / len(split))
        factor_of = factor_of * jnp.repeat(jnp.exp(steps), dims[dim] // shards_of).reshape((-1,) + (1,) * (len(dims) - 1 - dim))
    return factor_of


def centred(own_key, dims, scale, reach, shards=(), kind=jnp.bfloat16):
    array = jax.random.normal(own_key, dims, jnp.float32) * scale
    if len(shards) > 0:
        array = steps_of(own_key, dims, shards, -0.22, 0.18) * array
    return jnp.clip(array, min=-reach, max=reach).astype(kind)


def noise_with(key, dims, width, bound, split, heavy, kind=jnp.bfloat16):
    array = width * jax.random.normal(key, dims, jnp.float32)
    if split:
        array = array * steps_of(key, dims, split, -0.22, 0.18)
    return jnp.clip(raised(array, jax.random.fold_in(key, 3), *heavy), -bound, bound).astype(kind)


def setup_inputs(seed: int = 0) -> dict:
    streams_of = jax.random.split(jax.random.key(seed), 10)
    return {
        "green_real": draw_green_real(jax.random.fold_in(streams_of[9], 71), 0),
        "green_imag": draw_green_imag(jax.random.fold_in(streams_of[9], 71), 0),
        "station_vec": noise_with(streams_of[2], (2, EVENTS, ROWS), 1.0, 6.0, ((1, 16), (2, 32)), (2, 1, 32, 2.75), jnp.float32),
        "source_vec": noise_with(streams_of[3], (2, EVENTS, COLS), 1.0, 6.0, ((1, 32), (2, 16)), (2, 1, 32, 2.75), jnp.float32),
        "search_dir": centred(streams_of[4], (2, EVENTS, COLS), 1.0, 6.0, ((1, 32), (2, 16)), jnp.float32),
        "solution": centred(streams_of[5], (2, EVENTS, COLS), 1.0, 6.0, ((1, 32), (2, 16)), jnp.float32),
        "alpha_now": jnp.clip(jnp.exp(jax.random.uniform(streams_of[6], (EVENTS,), jnp.float32, math.log(0.5), math.log(2.0))), 0.5, 2.0),
        "rho_bar": jnp.clip(jax.random.uniform(streams_of[7], (EVENTS,), jnp.float32, 0.5, 2.0), 0.5, 2.0),
        "phi_bar": jnp.clip(jnp.exp(jax.random.uniform(streams_of[8], (EVENTS,), jnp.float32, math.log(0.5), math.log(2.0))), 0.5, 2.0),
    }


epsilon = 1e-06

def forward_apply(green_real, green_imag, pair):
    contract = (((1,), (1,)), ((), ()))
    real_real = lax.dot_general(pair[0], green_real, contract, preferred_element_type=jnp.float32)
    imag_imag = lax.dot_general(pair[1], green_imag, contract, preferred_element_type=jnp.float32)
    real_imag = lax.dot_general(pair[0], green_imag, contract, preferred_element_type=jnp.float32)
    imag_real = lax.dot_general(pair[1], green_real, contract, preferred_element_type=jnp.float32)
    return jnp.stack((real_real - imag_imag, imag_real + real_imag))

def adjoint_apply(green_real, green_imag, pair):
    contract = (((1,), (0,)), ((), ()))
    real_real = lax.dot_general(pair[0], green_real, contract, preferred_element_type=jnp.float32)
    imag_imag = lax.dot_general(pair[1], green_imag, contract, preferred_element_type=jnp.float32)
    imag_real = lax.dot_general(pair[1], green_real, contract, preferred_element_type=jnp.float32)
    real_imag = lax.dot_general(pair[0], green_imag, contract, preferred_element_type=jnp.float32)
    return jnp.stack((real_real + imag_imag, imag_real - real_imag))

def rotate(alpha_now, beta_now, rho_bar, phi_bar):
    rho_new = jnp.sqrt(rho_bar * rho_bar + beta_now * beta_now)
    cosine = rho_bar / rho_new
    sine_val = beta_now / rho_new
    theta_val = sine_val * alpha_now
    phi_val = cosine * phi_bar
    return (-cosine * alpha_now, sine_val * phi_bar, phi_val / rho_new, theta_val / rho_new)

def reference(green_real, green_imag, station_vec, source_vec, search_dir, solution, alpha_now, rho_bar, phi_bar):
    ratio = COLS / ROWS
    for iteration in range(ITERS):
        image = forward_apply(green_real, green_imag, source_vec.astype(jnp.bfloat16))
        station_vec = image - alpha_now[None, :, None] * station_vec
        beta_now = jnp.sqrt(lax.optimization_barrier(jnp.sum(station_vec * station_vec, axis=(0, 2))) / ROWS + epsilon)
        station_vec = station_vec / beta_now[None, :, None]
        back = adjoint_apply(green_real, green_imag, station_vec.astype(jnp.bfloat16))
        source_vec = ratio * back - beta_now[None, :, None] * source_vec
        alpha_now = jnp.sqrt(lax.optimization_barrier(jnp.sum(source_vec * source_vec, axis=(0, 2))) / COLS + epsilon)
        source_vec = source_vec / alpha_now[None, :, None]
        rho_bar, phi_bar, step_sol, step_dir = rotate(alpha_now, beta_now, rho_bar, phi_bar)
        solution = solution + step_sol[None, :, None] * search_dir
        search_dir = source_vec - step_dir[None, :, None] * search_dir
    return (station_vec, source_vec, search_dir, solution, alpha_now, rho_bar, phi_bar)
```

```python
import functools

import jax
import jax.numpy as jnp
from jax import lax
from jax.experimental import pallas as pl
from jax.experimental.pallas import tpu as pltpu
from jax.sharding import PartitionSpec as P

ITERS = 3
EPS = 1e-06
MESH = pl.DeviceIdType.MESH
F32 = jnp.float32
BF16 = jnp.bfloat16
LANES = 128
PART = 8


class Grid:
    def __init__(self, ny, nq, nhalf, nzh, nx, ncore):
        self.ny, self.nq, self.nhalf = ny, nq, nhalf
        self.nzh, self.nx, self.ncore = nzh, nx, ncore
        self.nz = nq * nhalf
        self.nxc = nx * ncore
        self.groups = 2 * self.nz // PART
        self.per = self.nz // self.groups


FULL = Grid(4, 4, 2, 2, 4, 2)


def kernel(grid, rows_total, cols_total, *refs):
    (green_re, green_im, station_ref, source_ref, search_ref, sol_ref,
     alpha_ref, rho_ref, phi_ref,
     station_out, source_out, search_out, sol_out, alpha_out, rho_out, phi_out,
     gmat, first, first_rows, vall, a1_out, a1_in, a2_in, af_out, af_in, ag_in,
     b1_out, b1_in, b2_out, b2_in, b3_out, b3_in,
     uhat, unorm, coef,
     load_sem, first_send, first_recv, send, recv) = refs
    ny, nq, nxc, groups, per = grid.ny, grid.nq, grid.nxc, grid.groups, grid.per
    width = source_ref.shape[-1] // nq
    half_rows = ny // 2
    ratio = cols_total / rows_total

    sta = lax.axis_index("sta")
    src = lax.axis_index("src")
    y = lax.rem(sta, ny)
    z = lax.div(sta, ny)
    quad = lax.rem(z, nq)
    zhalf = lax.div(z, nq)
    zh = lax.div(src, nxc)
    xc = lax.rem(src, nxc)
    core = lax.rem(xc, 2)

    def device(dz=None, dy=None, sta_to=None, src_to=None):
        return {"sta": sta if sta_to is None else sta_to, "src": src if src_to is None else src_to}

    def y_peer(d):
        return lax.rem(y + d, ny)

    def sta_of(z_at, y_at):
        return z_at * ny + y_at

    y_order = sorted(range(1, ny), key=lambda d: -min(d, ny - d))
    peers = []
    for d in range(1, ny):
        peers.append(device(sta_to=sta_of(z, y_peer(d))))
    for d in range(1, grid.nz):
        peers.append(device(sta_to=sta_of(lax.rem(z + d, grid.nz), y)))
    for d in range(1, nxc):
        peers.append(device(src_to=zh * nxc + lax.rem(xc + d, nxc)))
    other = (1 - zh) * nxc + xc - core
    for c in range(2):
        peers.append(device(src_to=other + c))
    barrier = pltpu.get_barrier_semaphore()
    for peer in peers:
        pl.semaphore_signal(barrier, inc=1, device_id=peer, device_id_type=MESH)

    rows_half = green_re.shape[0]
    loads = [
        pltpu.make_async_copy(green_re, gmat.at[pl.ds(0, rows_half)], load_sem.at[0]),
        pltpu.make_async_copy(green_im, gmat.at[pl.ds(rows_half, rows_half)], load_sem.at[1]),
    ]
    for load in loads:
        load.start()

    own = source_ref[:, 0, :]
    pieces = [own[p : p + 1, q * width : (q + 1) * width] for p in range(2) for q in range(nq)]
    first[z] = jnp.concatenate(pieces, axis=0).astype(BF16)

    sends = []

    def remote(src_at, dst_at, send_sem, recv_sem, to):
        copy = pltpu.make_async_remote_copy(
            src_ref=src_at, dst_ref=dst_at, send_sem=send_sem, recv_sem=recv_sem,
            device_id=to, device_id_type=MESH)
        copy.start()

    def wait_bytes(ref, sem):
        pltpu.make_async_copy(ref, ref, sem).wait()

    def is_re(shape):
        return lax.broadcasted_iota(jnp.int32, shape, len(shape) - 2) < per

    def swap(a):
        return pltpu.roll(a, per, a.ndim - 2)

    def encode(total):
        high = total.astype(BF16).astype(F32)
        return jnp.where(is_re(total.shape), high, total - high)

    def decode(pair):
        return pair + swap(pair)

    def lanes(a):
        return jnp.broadcast_to(a, a.shape[:-1] + (LANES,))

    def event_of(k, shape):
        zl = lax.rem(lax.broadcasted_iota(jnp.int32, shape, 1), per)
        return (k * per + zl) * ny + lax.broadcasted_iota(jnp.int32, shape, 0)

    n_events = alpha_ref.shape[-1]

    def spread(ref, k):
        shape = (ny, PART, n_events)
        lane = lax.broadcasted_iota(jnp.int32, shape, 2)
        row = jnp.broadcast_to(ref[...].reshape(1, 1, n_events), shape)
        return lanes(jnp.sum(jnp.where(lane == event_of(k, shape), row, 0.0), axis=-1, keepdims=True))

    alpha = [spread(alpha_ref, k) for k in range(groups)]
    rho = [spread(rho_ref, k) for k in range(groups)]
    phi = [spread(phi_ref, k) for k in range(groups)]

    search_out[...] = search_ref[...]
    sol_out[...] = sol_ref[...]

    for load in loads:
        load.wait()
    pl.semaphore_wait(barrier, len(peers))

    for d in range(1, grid.nz):
        remote(first.at[z], first.at[z], first_send, first_recv,
               device(sta_to=sta_of(lax.rem(z + d, grid.nz), y)))
    wait_bytes(first.at[pl.ds(0, grid.nz - 1)], first_recv)
    for k in range(groups):
        for e in range(per):
            block = first[k * per + e].astype(F32)
            for p in range(2):
                for q in range(nq):
                    first_rows[k, q, p * per + e : p * per + e + 1, :] = block[p * nq + q : p * nq + q + 1, :]
        vall[0, k, y, :, :, 0:width] = first_rows[k].astype(BF16)

    def share_y(t, k):
        for d in y_order:
            remote(vall.at[t, k, y], vall.at[t, k, y], send.at[t, k, 6], recv.at[t, k, 6],
                   device(sta_to=sta_of(z, y_peer(d))))

    for k in range(groups):
        share_y(0, k)

    def columns(t, k, q):
        return vall[t, k, :, q, :, 0:width].astype(F32)

    def beta_squares(t, k):
        return decode(vall[t, k, :, 0, :, width:].astype(F32))

    def root(total, count):
        return jnp.sqrt(total * (1.0 / count) + EPS)

    def squares_of(values):
        total = jnp.sum(values[0] * values[0], axis=-1, keepdims=True)
        for value in values[1:]:
            total += jnp.sum(value * value, axis=-1, keepdims=True)
        return lanes(total + swap(lanes(total))[..., 0:1])

    contract = (((1,), (1,)), ((), ()))

    def stage_a1(t, k):
        wait_bytes(vall.at[t, k, pl.ds(0, ny - 1)], recv.at[t, k, 6])
        values = [columns(t, k, q) for q in range(nq)]
        last = t == ITERS
        buf_out, buf_in = (af_out.at[k], af_in.at[k]) if last else (a1_out.at[t, k], a1_in.at[t, k])
        if t == 0:
            scalars = jnp.zeros((ny, PART, LANES), F32)
        else:
            scalars = encode(squares_of(values))
        if last:
            message = scalars
        else:
            product = jnp.zeros((ny * PART, 2 * rows_half), F32)
            for q in range(nq):
                left = values[q].reshape(ny * PART, width).astype(BF16)
                product += lax.dot_general(
                    left, gmat[:, q * width : (q + 1) * width], contract, preferred_element_type=F32)
            product = product.reshape(ny, PART, 2 * rows_half)
            turned = swap(product[..., rows_half:])
            image = product[..., :rows_half] + jnp.where(is_re(turned.shape), -turned, turned)
            if t == 0:
                shape = image.shape
                event = event_of(k, shape)
                part_re = is_re(shape)
                per_src = station_ref.shape[1]
                for n in range(per_src):
                    mine = event == src * per_src + n
                    both = jnp.where(part_re, jnp.broadcast_to(station_ref[0, n : n + 1, :][None], shape),
                                     jnp.broadcast_to(station_ref[1, n : n + 1, :][None], shape))
                    image -= jnp.where(mine, alpha[k] * both, 0.0)
            message = jnp.concatenate([image, scalars], axis=-1)
        message = message.astype(BF16)
        for c in range(2):
            buf_out[c] = message[c * half_rows : (c + 1) * half_rows]
        buf_in[xc] = buf_out[core]
        for d in range(1, nxc):
            to = lax.rem(xc + d, nxc)
            remote(buf_out.at[lax.rem(to, 2)], buf_in.at[xc], send.at[t, k, 0], recv.at[t, k, 0],
                   device(src_to=zh * nxc + to))

    def stage_a2(t, k):
        last = t == ITERS
        buf_in, buf_next = (af_in.at[k], ag_in.at[k]) if last else (a1_in.at[t, k], a2_in.at[t, k])
        wait_bytes(buf_in.at[pl.ds(0, nxc - 1)], recv.at[t, k, 0])
        total = buf_in[0].astype(F32)
        for i in range(1, nxc):
            total += buf_in[i].astype(F32)
        scalars = encode(decode(total[..., -LANES:]))
        message = scalars if last else jnp.concatenate([total[..., :rows_half], scalars], axis=-1)
        buf_next[zh * 2 + core] = message.astype(BF16)
        here = buf_next.at[zh * 2 + core]
        for to in (other + core, other + 1 - core, src + 1 - 2 * core):
            remote(here, here, send.at[t, k, 1], recv.at[t, k, 1], device(src_to=to))

    def summed(t, k):
        last = t == ITERS
        buf = ag_in.at[k] if last else a2_in.at[t, k]
        wait_bytes(buf.at[pl.ds(0, 3)], recv.at[t, k, 1])
        halves = [buf[c].astype(F32) + buf[2 + c].astype(F32) for c in range(2)]
        return jnp.concatenate(halves, axis=0)

    def stage_a3(t, k):
        total = summed(t, k)
        vector = total[..., :rows_half]
        if t > 0:
            alpha[k] = root(decode(total[..., -LANES:]), cols_total)
            beta = root(beta_squares(t, k), rows_total)
            vector = vector / alpha[k] - alpha[k] * (uhat[k] / beta)
        uhat[k] = vector
        scalars = encode(squares_of([vector])).astype(BF16)
        turned = swap(vector)
        left = jnp.concatenate([vector, jnp.where(is_re(turned.shape), turned, -turned)], axis=-1)
        left = left.reshape(ny * PART, 2 * rows_half).astype(BF16)
        for q in range(nq):
            back = jnp.dot(left, gmat[:, q * width : (q + 1) * width], preferred_element_type=F32)
            b1_out[t, k, :, q, :, 0:width] = back.reshape(ny, PART, width).astype(BF16)
            b1_out[t, k, :, q, :, width:] = scalars
        for d in y_order:
            remote(b1_out.at[t, k, y_peer(d)], b1_in.at[t, k, y], send.at[t, k, 2], recv.at[t, k, 2],
                   device(sta_to=sta_of(z, y_peer(d))))

    def stage_b2(t, k):
        wait_bytes(b1_in.at[t, k, pl.ds(0, ny - 1)], recv.at[t, k, 2])
        total = b1_out[t, k, y].astype(F32)
        for d in range(1, ny):
            total += b1_in[t, k, y_peer(d)].astype(F32)
        b2_out[t, k, :, :, 0:width] = total[..., :width].astype(BF16)
        b2_out[t, k, :, :, width:] = encode(decode(total[..., width:])).astype(BF16)
        for d in range(1, nq):
            to = lax.rem(quad + d, nq)
            remote(b2_out.at[t, k, to], b2_in.at[t, k, quad], send.at[t, k, 3], recv.at[t, k, 3],
                   device(sta_to=sta_of(zhalf * nq + to, y)))

    def stage_b3(t, k):
        wait_bytes(b2_in.at[t, k, pl.ds(0, nq - 1)], recv.at[t, k, 3])
        total = b2_out[t, k, quad].astype(F32)
        for d in range(1, nq):
            total += b2_in[t, k, lax.rem(quad + d, nq)].astype(F32)
        b3_out[t, k, :, 0:width] = total[:, :width].astype(BF16)
        b3_out[t, k, :, width:] = encode(decode(total[:, width:])).astype(BF16)
        remote(b3_out.at[t, k], b3_in.at[t, k], send.at[t, k, 4], recv.at[t, k, 4],
               device(sta_to=sta_of((1 - zhalf) * nq + quad, y)))

    def stage_b4(t, k):
        wait_bytes(b3_in.at[t, k], recv.at[t, k, 4])
        total = b3_out[t, k].astype(F32) + b3_in[t, k].astype(F32)
        squares = decode(total[:, width:])
        beta = root(squares, rows_total)[:, 0:1]
        before = vall[t, k, y, quad, :, 0:width].astype(F32)
        if t > 0:
            before = before / coef[k, 0, y][:, 0:1]
        after = total[:, :width] * (ratio / beta) - beta * before
        vall[t + 1, k, y, quad, :, 0:width] = after.astype(BF16)
        vall[t + 1, k, y, quad, :, width:] = encode(squares).astype(BF16)
        here = vall.at[t + 1, k, y, quad]
        for d in range(1, nq):
            to = lax.rem(quad + d, nq)
            remote(here, here, send.at[t, k, 5], recv.at[t, k, 5],
                   device(sta_to=sta_of(zhalf * nq + to, y)))

    def stage_b5(t, k):
        wait_bytes(vall.at[t + 1, k, y, pl.ds(0, nq - 1)], recv.at[t, k, 5])
        share_y(t + 1, k)

    mine_k = lax.div(z, per)
    mine_row = lax.rem(z, per)

    def rotate(t, k):
        beta = root(beta_squares(t, k), rows_total)
        rho_new = jnp.sqrt(rho[k] * rho[k] + beta * beta)
        cosine = rho[k] / rho_new
        sine = beta / rho_new
        coef[k, 0] = alpha[k]
        coef[k, 1] = cosine * phi[k] / rho_new
        coef[k, 2] = sine * alpha[k] / rho_new
        rho[k] = -cosine * alpha[k]
        phi[k] = sine * phi[k]

    def step(t):
        def scalar(i):
            return coef[mine_k, i, y, pl.ds(mine_row, 1), :][:, 0:1]

        alpha_own, step_sol, step_dir = scalar(0), scalar(1), scalar(2)
        block = vall[t, mine_k, y].astype(F32)[:, :, 0:width]
        row = lax.broadcasted_iota(jnp.int32, block.shape, 1)
        for p in range(2):
            picked = jnp.sum(jnp.where(row == p * per + mine_row, block, 0.0), axis=1, keepdims=True)
            vector = jnp.concatenate([picked[q] for q in range(nq)], axis=-1) / alpha_own
            before = search_out[p]
            sol_out[p] = sol_out[p] + step_sol * before
            search_out[p] = vector - step_dir * before
            if t == ITERS:
                source_out[p] = vector

    for t in range(ITERS):
        for k in range(groups):
            stage_a1(t, k)
        for k in range(groups):
            stage_a2(t, k)
        for k in range(groups):
            stage_a3(t, k)
        if t > 0:
            for k in range(groups):
                rotate(t, k)
            step(t)
        for stage in (stage_b2, stage_b3, stage_b4, stage_b5):
            for k in range(groups):
                stage(t, k)
    for k in range(groups):
        stage_a1(ITERS, k)
    for k in range(groups):
        unorm[k] = uhat[k] / root(beta_squares(ITERS, k), rows_total)
    per_src = station_ref.shape[1]
    for n in range(per_src):
        event = src * per_src + n
        at_y, at_z = lax.rem(event, ny), lax.div(event, ny)
        for p in range(2):
            station_out[p, n : n + 1, :] = unorm[
                lax.div(at_z, per), at_y, pl.ds(p * per + lax.rem(at_z, per), 1), :]
    for k in range(groups):
        stage_a2(ITERS, k)
    for k in range(groups):
        alpha[k] = root(decode(summed(ITERS, k)), cols_total)
        rotate(ITERS, k)
    step(ITERS)

    def collect(values):
        shape = (ny, PART, n_events)
        lane = lax.broadcasted_iota(jnp.int32, shape, 2)
        total = jnp.zeros((1, n_events), F32)
        for k in range(groups):
            keep = (lane == event_of(k, shape)) & is_re(shape)
            kept = jnp.where(keep, values[k][..., 0:1], 0.0).reshape(ny * PART, n_events)
            total += jnp.sum(kept, axis=0, keepdims=True)
        return total

    alpha_out[...] = collect(alpha)
    rho_out[...] = collect(rho)
    phi_out[...] = collect(phi)

    wait_bytes(first.at[pl.ds(0, grid.nz - 1)], first_send)
    for k in range(groups):
        for t in range(ITERS + 1):
            last = t == ITERS
            wait_bytes((af_in.at[k] if last else a1_in.at[t, k]).at[pl.ds(0, nxc - 1)], send.at[t, k, 0])
            buf = ag_in.at[k] if last else a2_in.at[t, k]
            wait_bytes(buf.at[pl.ds(0, 3)], send.at[t, k, 1])
            wait_bytes(vall.at[t, k, pl.ds(0, ny - 1)], send.at[t, k, 6])
            if not last:
                wait_bytes(b1_in.at[t, k, pl.ds(0, ny - 1)], send.at[t, k, 2])
                wait_bytes(b2_in.at[t, k, pl.ds(0, nq - 1)], send.at[t, k, 3])
                wait_bytes(b3_in.at[t, k], send.at[t, k, 4])
                wait_bytes(vall.at[t, k, 0, pl.ds(0, nq - 1)], send.at[t, k, 5])


def shards(grid, *args):
    green_real, source = args[0], args[3]
    rows = green_real.shape[0]
    rows_total = rows * lax.axis_size("sta")
    cols_total = green_real.shape[1] * lax.axis_size("src")
    ny, nq, groups = grid.ny, grid.nq, grid.groups
    width = green_real.shape[1] // nq
    padded = width + LANES
    n_events = args[6].shape[0]
    args = list(args[:6]) + [a.reshape(1, n_events) for a in args[6:]]
    vmem = pl.BlockSpec(memory_space=pltpu.VMEM)
    half = ny // 2
    message = rows + LANES

    def buf(*shape, kind=BF16):
        return pltpu.VMEM(shape, kind)

    scratch = [
        buf(2 * rows, green_real.shape[1]),
        buf(grid.nz, 2 * nq, width),
        buf(groups, nq, PART, width, kind=F32),
        buf(ITERS + 1, groups, ny, nq, PART, padded),
        buf(ITERS, groups, 2, half, PART, message),
        buf(ITERS, groups, grid.nxc, half, PART, message),
        buf(ITERS, groups, 4, half, PART, message),
        buf(groups, 2, half, PART, LANES),
        buf(groups, grid.nxc, half, PART, LANES),
        buf(groups, 4, half, PART, LANES),
        buf(ITERS, groups, ny, nq, PART, padded),
        buf(ITERS, groups, ny, nq, PART, padded),
        buf(ITERS, groups, nq, PART, padded),
        buf(ITERS, groups, nq, PART, padded),
        buf(ITERS, groups, PART, padded),
        buf(ITERS, groups, PART, padded),
        buf(groups, ny, PART, rows, kind=F32),
        buf(groups, ny, PART, rows, kind=F32),
        buf(groups, 3, ny, PART, LANES, kind=F32),
        pltpu.SemaphoreType.DMA((2,)),
        pltpu.SemaphoreType.DMA,
        pltpu.SemaphoreType.DMA,
        pltpu.SemaphoreType.DMA((ITERS + 1, groups, 7)),
        pltpu.SemaphoreType.DMA((ITERS + 1, groups, 7)),
    ]
    shapes = [args[2].shape, source.shape, source.shape, source.shape] + [(1, n_events)] * 3
    outs = pl.pallas_call(
        functools.partial(kernel, grid, rows_total, cols_total),
        out_shape=[jax.ShapeDtypeStruct(shape, F32) for shape in shapes],
        in_specs=[pl.BlockSpec(memory_space=pl.ANY)] * 2 + [vmem] * 7,
        out_specs=[vmem] * 7,
        scratch_shapes=scratch,
        compiler_params=pltpu.CompilerParams(
            collective_id=0, has_side_effects=True, vmem_limit_bytes=40 * 1024 * 1024),
        name="lsqr",
    )(*args)
    return tuple(outs[:4]) + tuple(a.reshape(n_events) for a in outs[4:])


def build(mesh, grid):
    placed = (
        P("sta", "src"),
        P("sta", "src"),
        P(None, "src", "sta"),
        P(None, "sta", "src"),
        P(None, "sta", "src"),
        P(None, "sta", "src"),
        P(),
        P(),
        P(),
    )
    return jax.shard_map(
        functools.partial(shards, grid),
        mesh=mesh,
        in_specs=placed,
        out_specs=placed[2:],
        check_vma=False,
    )


def solution(mesh):
    return build(mesh, FULL)
```

```python
import functools

import jax
import jax.numpy as jnp
from jax import lax
from jax.experimental import pallas as pl
from jax.experimental.pallas import tpu as pltpu
from jax.sharding import PartitionSpec as P

ITERS = 3
EPS = 1e-06
MESH = pl.DeviceIdType.MESH
F32 = jnp.float32
BF16 = jnp.bfloat16
LANES = 128
PART = 8


class Grid:
    def __init__(self, ny, nq, nhalf, nzh, nx, ncore):
        self.ny, self.nq, self.nhalf = ny, nq, nhalf
        self.nzh, self.nx, self.ncore = nzh, nx, ncore
        self.nz = nq * nhalf
        self.nxc = nx * ncore
        self.groups = 2 * self.nz // PART
        self.per = self.nz // self.groups


FULL = Grid(4, 4, 2, 2, 4, 2)


def kernel(grid, rows_total, cols_total, *refs):
    (green_re, green_im, station_in, source_in, search_in, sol_in, alpha_in, rho_in, phi_in,
     station_out, source_out, search_out, sol_out, alpha_out, rho_out, phi_out,
     station_ref, source_ref, alpha_ref, rho_ref, phi_ref,
     gmat, first, first_rows, vall, a1_out, a1_in, a2_in, fs1, fs2,
     b1_out, b1_in, b2_out, b2_in, b3_out, b3_in,
     uhat, unorm, coef, load_sem, first_send, first_recv, send, recv) = refs
    ny, nq, nxc, groups, per = grid.ny, grid.nq, grid.nxc, grid.groups, grid.per
    n_src = grid.nzh * nxc
    width = source_ref.shape[-1] // nq
    rows_half = gmat.shape[1] // 2
    half_rows = ny // 2
    ratio = cols_total / rows_total
    S_A1, S_A2, S_B2, S_B3, S_B5, S_B1 = 0, 1, 2, 3, 4, 5
    S_B4 = S_B1 + nq

    sta = lax.axis_index("sta")
    src = lax.axis_index("src")
    y = lax.rem(sta, ny)
    z = lax.div(sta, ny)
    quad = lax.rem(z, nq)
    zhalf = lax.div(z, nq)
    zh = lax.div(src, nxc)
    xc = lax.rem(src, nxc)
    core = lax.rem(xc, 2)

    def at_sta(z_at, y_at):
        return {"sta": z_at * ny + y_at, "src": src}

    def at_src(src_to):
        return {"sta": sta, "src": src_to}

    def y_peer(d):
        return lax.rem(y + d, ny)

    def by_distance(i, far_first):
        sign = -1 if far_first else 1
        table = [sorted(range(nq), key=lambda q: sign * abs(q - p))[i] for p in range(nq)]
        value = jnp.int32(table[0])
        for p in range(1, nq):
            value = jnp.where(quad == p, table[p], value)
        return value

    y_order = sorted(range(1, ny), key=lambda d: -min(d, ny - d))
    peers = []
    for d in range(1, grid.nz):
        peers.append(at_sta(lax.rem(z + d, grid.nz), y))
    for d in range(1, ny):
        for e in range(nq):
            peers.append(at_sta(zhalf * nq + lax.rem(quad + e, nq), y_peer(d)))
    for d in range(1, n_src):
        peers.append(at_src(lax.rem(src + d, n_src)))
    barrier = pltpu.get_barrier_semaphore()
    for peer in peers:
        pl.semaphore_signal(barrier, inc=1, device_id=peer, device_id_type=MESH)

    loads = [
        pltpu.make_async_copy(a, b, load_sem.at[i])
        for i, (a, b) in enumerate((
            (source_in, source_ref), (station_in, station_ref), (alpha_in, alpha_ref), (rho_in, rho_ref),
            (phi_in, phi_ref), (search_in, search_out), (sol_in, sol_out)))
    ]
    g_loads = []
    for q in range(nq):
        cut = pl.ds(q * width, width)
        for p, green in enumerate((green_re, green_im)):
            g_loads.append(pltpu.make_async_copy(
                green.at[:, cut], gmat.at[q, pl.ds(p * rows_half, rows_half)],
                load_sem.at[len(loads) + 2 * q + p]))
    for load in loads + g_loads:
        load.start()
    for load in loads:
        load.wait()

    pieces = [source_ref[p, :, q * width : (q + 1) * width] for p in range(2) for q in range(nq)]
    first[z] = jnp.concatenate(pieces, axis=0).astype(BF16)

    def remote(src_at, dst_at, send_sem, recv_sem, to):
        pltpu.make_async_remote_copy(
            src_ref=src_at, dst_ref=dst_at, send_sem=send_sem, recv_sem=recv_sem,
            device_id=to, device_id_type=MESH).start()

    def wait_bytes(ref, sem):
        pltpu.make_async_copy(ref, ref, sem).wait()

    def is_re(shape):
        return lax.broadcasted_iota(jnp.int32, shape, len(shape) - 2) < per

    def swap(a):
        return pltpu.roll(a, per, a.ndim - 2)

    def encode(total):
        high = total.astype(BF16).astype(F32)
        return jnp.where(is_re(total.shape), high, total - high)

    def decode(pair):
        return pair + swap(pair)

    def lanes(a):
        return jnp.broadcast_to(a, a.shape[:-1] + (LANES,))

    def event_of(k, shape):
        zl = lax.rem(lax.broadcasted_iota(jnp.int32, shape, 1), per)
        return (k * per + zl) * ny + lax.broadcasted_iota(jnp.int32, shape, 0)

    n_events = alpha_ref.shape[-1]

    def spread(ref, k):
        shape = (ny, PART, n_events)
        lane = lax.broadcasted_iota(jnp.int32, shape, 2)
        row = jnp.broadcast_to(ref[...].reshape(1, 1, n_events), shape)
        return lanes(jnp.sum(jnp.where(lane == event_of(k, shape), row, 0.0), axis=-1, keepdims=True))

    alpha = [spread(alpha_ref, k) for k in range(groups)]
    rho = [spread(rho_ref, k) for k in range(groups)]
    phi = [spread(phi_ref, k) for k in range(groups)]

    pl.semaphore_wait(barrier, len(peers))

    for d in range(grid.nz - 1, 0, -1):
        remote(first.at[z], first.at[z], first_send, first_recv, at_sta(lax.rem(z + d, grid.nz), y))
    for load in g_loads:
        load.wait()
    wait_bytes(first.at[pl.ds(0, grid.nz - 1)], first_recv)

    def share_y(t, k, q):
        here = vall.at[t, k, y, q]
        for d in y_order:
            remote(here, here, send.at[t, k, S_B5], recv.at[t, k, S_B5], at_sta(z, y_peer(d)))

    for k in range(groups):
        for e in range(per):
            block = first[k * per + e].astype(F32)
            for p in range(2):
                for q in range(nq):
                    first_rows[k, q, p * per + e : p * per + e + 1, :] = block[p * nq + q : p * nq + q + 1, :]
        vall[0, k, y, :, :, 0:width] = first_rows[k].astype(BF16)
        for q in range(nq):
            share_y(0, k, q)

    def columns(t, k, q):
        return vall[t, k, :, q, :, 0:width].astype(F32)

    def beta_squares(t, k):
        return decode(vall[t, k, :, 0, :, width:].astype(F32))

    def root(total, count):
        return jnp.sqrt(total * (1.0 / count) + EPS)

    def squares_of(values):
        total = jnp.sum(values[0] * values[0], axis=-1, keepdims=True)
        for value in values[1:]:
            total += jnp.sum(value * value, axis=-1, keepdims=True)
        total = lanes(total)
        return total + swap(total)

    contract = (((1,), (1,)), ((), ()))

    def stage_a1(t, k):
        wait_bytes(vall.at[t, k, pl.ds(0, ny - 1)], recv.at[t, k, S_B5])
        values = [columns(t, k, q) for q in range(nq)]
        product = jnp.zeros((ny * PART, 2 * rows_half), F32)
        for q in range(nq):
            left = values[q].reshape(ny * PART, width).astype(BF16)
            product += lax.dot_general(left, gmat[q], contract, preferred_element_type=F32)
        product = product.reshape(ny, PART, 2 * rows_half)
        turned = swap(product[..., rows_half:])
        image = product[..., :rows_half] + jnp.where(is_re(turned.shape), -turned, turned)
        if t == 0:
            scalars = jnp.zeros((ny, PART, LANES), F32)
            shape = image.shape
            event = event_of(k, shape)
            part_re = is_re(shape)
            per_src = station_ref.shape[1]
            for n in range(per_src):
                both = jnp.where(part_re, jnp.broadcast_to(station_ref[0, n : n + 1, :][None], shape),
                                 jnp.broadcast_to(station_ref[1, n : n + 1, :][None], shape))
                image -= jnp.where(event == src * per_src + n, alpha[k] * both, 0.0)
        else:
            scalars = encode(squares_of(values))
        message = jnp.concatenate([image, scalars], axis=-1).astype(BF16)
        for c in range(2):
            a1_out[t, k, c] = message[c * half_rows : (c + 1) * half_rows]
        a1_in[t, k, xc] = a1_out[t, k, core]
        for d in range(1, nxc):
            to = lax.rem(xc + d, nxc)
            remote(a1_out.at[t, k, lax.rem(to, 2)], a1_in.at[t, k, xc], send.at[t, k, S_A1], recv.at[t, k, S_A1],
                   at_src(zh * nxc + to))

    other = (1 - zh) * nxc + xc - core

    def stage_a2(t, k):
        wait_bytes(a1_in.at[t, k, pl.ds(0, nxc - 1)], recv.at[t, k, S_A1])
        total = a1_in[t, k, 0].astype(F32)
        for i in range(1, nxc):
            total += a1_in[t, k, i].astype(F32)
        scalars = encode(decode(total[..., rows_half:]))
        a2_in[t, k, zh * 2 + core] = jnp.concatenate([total[..., :rows_half], scalars], axis=-1).astype(BF16)
        here = a2_in.at[t, k, zh * 2 + core]
        for to in (other + core, other + 1 - core, src + 1 - 2 * core):
            remote(here, here, send.at[t, k, S_A2], recv.at[t, k, S_A2], at_src(to))

    def stage_a3(t, k):
        wait_bytes(a2_in.at[t, k, pl.ds(0, 3)], recv.at[t, k, S_A2])
        total = jnp.concatenate(
            [a2_in[t, k, c].astype(F32) + a2_in[t, k, 2 + c].astype(F32) for c in range(2)], axis=0)
        vector = total[..., :rows_half]
        if t > 0:
            alpha[k] = root(decode(total[..., rows_half:]), cols_total)
            beta = root(beta_squares(t, k), rows_total)
            vector = vector / alpha[k] - alpha[k] * (uhat[k] / beta)
        uhat[k] = vector
        scalars = encode(squares_of([vector])).astype(BF16)
        turned = swap(vector)
        left = jnp.concatenate([vector, jnp.where(is_re(turned.shape), turned, -turned)], axis=-1)
        left = left.reshape(ny * PART, 2 * rows_half).astype(BF16)
        for i in range(nq):
            q = by_distance(i, True)
            back = jnp.dot(left, gmat[q], preferred_element_type=F32)
            b1_out[t, k, :, q, :, 0:width] = back.reshape(ny, PART, width).astype(BF16)
            b1_out[t, k, :, q, :, width:] = scalars
            for d in y_order:
                remote(b1_out.at[t, k, y_peer(d), q], b1_in.at[t, k, q, y], send.at[t, k, S_B1],
                       recv.at[t, k, S_B1 + q], at_sta(z, y_peer(d)))

    def stage_b2(t, k):
        for i in range(nq):
            q = by_distance(i, True)
            wait_bytes(b1_in.at[t, k, q, pl.ds(0, ny - 1)], recv.at[t, k, S_B1 + q])
            total = b1_out[t, k, y, q].astype(F32)
            for d in range(1, ny):
                total += b1_in[t, k, q, y_peer(d)].astype(F32)
            b2_out[t, k, q, :, 0:width] = total[..., :width].astype(BF16)
            b2_out[t, k, q, :, width:] = encode(decode(total[..., width:])).astype(BF16)
            if i < nq - 1:
                remote(b2_out.at[t, k, q], b2_in.at[t, k, quad], send.at[t, k, S_B2], recv.at[t, k, S_B2],
                       at_sta(zhalf * nq + q, y))

    def stage_b3(t, k):
        wait_bytes(b2_in.at[t, k, pl.ds(0, nq - 1)], recv.at[t, k, S_B2])
        total = b2_out[t, k, quad].astype(F32)
        for d in range(1, nq):
            total += b2_in[t, k, lax.rem(quad + d, nq)].astype(F32)
        b3_out[t, k, :, 0:width] = total[:, :width].astype(BF16)
        b3_out[t, k, :, width:] = encode(decode(total[:, width:])).astype(BF16)
        remote(b3_out.at[t, k], b3_in.at[t, k], send.at[t, k, S_B3], recv.at[t, k, S_B3],
               at_sta((1 - zhalf) * nq + quad, y))

    def stage_b4(t, k):
        wait_bytes(b3_in.at[t, k], recv.at[t, k, S_B3])
        total = b3_out[t, k].astype(F32) + b3_in[t, k].astype(F32)
        squares = decode(total[:, width:])
        beta = root(squares, rows_total)[:, 0:1]
        before = vall[t, k, y, quad, :, 0:width].astype(F32)
        if t > 0:
            before = before / coef[k, 0, y][:, 0:1]
        after = total[:, :width] * (ratio / beta) - beta * before
        after = after.astype(BF16)
        if t == ITERS - 1:
            after32 = after.astype(F32)
            lane = lax.broadcasted_iota(jnp.int32, squares.shape, 1)
            slot = y * nq + quad
            fs1[k, slot] = jnp.where(lane < LANES // 2, squares_of([after32]), squares)
            for d in range(ny - 1, -1, -1):
                for e in range(nq):
                    if d or e:
                        remote(fs1.at[k, slot], fs1.at[k, slot], send.at[t + 1, k, 0], recv.at[t + 1, k, 0],
                               at_sta(zhalf * nq + lax.rem(quad + e, nq), y_peer(d)))
        vall[t + 1, k, y, quad, :, 0:width] = after
        vall[t + 1, k, y, quad, :, width:] = encode(squares).astype(BF16)
        here = vall.at[t + 1, k, y, quad]
        for i in range(nq - 1):
            to = by_distance(i, True)
            remote(here, here, send.at[t, k, S_B4], recv.at[t, k, S_B4 + quad], at_sta(zhalf * nq + to, y))
        if t < ITERS - 1:
            share_y(t + 1, k, quad)

    def stage_b5(t, k):
        for i in range(1, nq):
            q = by_distance(i, False)
            wait_bytes(vall.at[t + 1, k, y, q], recv.at[t, k, S_B4 + q])
            if t < ITERS - 1:
                share_y(t + 1, k, q)

    mine_k = lax.div(z, per)
    mine_row = lax.rem(z, per)

    def rotate(k, beta):
        rho_new = jnp.sqrt(rho[k] * rho[k] + beta * beta)
        cosine = rho[k] / rho_new
        sine = beta / rho_new
        coef[k, 0] = alpha[k]
        coef[k, 1] = cosine * phi[k] / rho_new
        coef[k, 2] = sine * alpha[k] / rho_new
        rho[k] = -cosine * alpha[k]
        phi[k] = sine * phi[k]

    def own_rows(t):
        block = vall[t, mine_k, y].astype(F32)[:, :, 0:width]
        row = lax.broadcasted_iota(jnp.int32, block.shape, 1)
        result = []
        for p in range(2):
            picked = jnp.sum(jnp.where(row == p * per + mine_row, block, 0.0), axis=1, keepdims=True)
            result.append(jnp.concatenate([picked[q] for q in range(nq)], axis=-1))
        return result

    def step(t, rows):
        def scalar(i):
            return coef[mine_k, i, y, pl.ds(mine_row, 1), :][:, 0:1]

        alpha_own, step_sol, step_dir = scalar(0), scalar(1), scalar(2)
        for p in range(2):
            vector = rows[p] / alpha_own
            before = search_out[p]
            sol_out[p] = sol_out[p] + step_sol * before
            search_out[p] = vector - step_dir * before
            if t == ITERS:
                source_out[p] = vector

    for t in range(ITERS):
        for k in range(groups):
            stage_a1(t, k)
        for k in range(groups):
            stage_a2(t, k)
        for k in range(groups):
            stage_a3(t, k)
        if t > 0:
            for k in range(groups):
                rotate(k, root(beta_squares(t, k), rows_total))
            step(t, own_rows(t))
        for stage in (stage_b2, stage_b3, stage_b4, stage_b5):
            for k in range(groups):
                stage(t, k)

    row = lax.broadcasted_iota(jnp.int32, (PART, LANES), 0)
    lane = lax.broadcasted_iota(jnp.int32, (PART, LANES), 1)
    seg = LANES // ny
    squares = jnp.zeros((PART, LANES), F32)
    betas = []
    for k in range(groups):
        wait_bytes(fs1.at[k, pl.ds(0, ny * nq - 1)], recv.at[ITERS, k, 0])
        beta_rows = []
        for i in range(ny):
            total = fs1[k, i * nq]
            beta_rows.append(lanes(total[:, LANES // 2 : LANES // 2 + 1]))
            for q in range(1, nq):
                total += fs1[k, i * nq + q]
            squares = jnp.where((lax.div(lane, seg) == i) & (lax.div(row, per) == k), lanes(total[:, 0:1]), squares)
        betas.append(root(jnp.stack(beta_rows), rows_total))
    fs2[src] = squares
    for d in range(1, n_src):
        remote(fs2.at[src], fs2.at[src], send.at[ITERS, 0, 1], recv.at[ITERS, 0, 1],
               at_src(lax.rem(src + d, n_src)))

    for k in range(groups):
        unorm[k] = uhat[k] / betas[k]
    per_src = station_ref.shape[1]
    for n in range(per_src):
        event = src * per_src + n
        at_y, at_z = lax.rem(event, ny), lax.div(event, ny)
        for p in range(2):
            station_out[p, n : n + 1, :] = unorm[
                lax.div(at_z, per), at_y, pl.ds(p * per + lax.rem(at_z, per), 1), :]
    last_rows = own_rows(ITERS)

    wait_bytes(fs2.at[pl.ds(0, n_src - 1)], recv.at[ITERS, 0, 1])
    squares = fs2[0]
    for i in range(1, n_src):
        squares += fs2[i]
    for k in range(groups):
        kept = jnp.where(lax.div(row, per) == k, squares, 0.0)
        kept = kept + swap(kept)
        alpha[k] = root(jnp.stack([lanes(kept[:, i * seg : i * seg + 1]) for i in range(ny)]), cols_total)
        rotate(k, betas[k])
    step(ITERS, last_rows)

    def collect(values):
        shape = (ny, PART, n_events)
        lane = lax.broadcasted_iota(jnp.int32, shape, 2)
        total = jnp.zeros((1, n_events), F32)
        for k in range(groups):
            keep = (lane == event_of(k, shape)) & is_re(shape)
            kept = jnp.where(keep, values[k][..., 0:1], 0.0).reshape(ny * PART, n_events)
            total += jnp.sum(kept, axis=0, keepdims=True)
        return total

    alpha_out[...] = collect(alpha)
    rho_out[...] = collect(rho)
    phi_out[...] = collect(phi)

    wait_bytes(first.at[pl.ds(0, grid.nz - 1)], first_send)
    wait_bytes(fs2.at[pl.ds(0, n_src - 1)], send.at[ITERS, 0, 1])
    for k in range(groups):
        wait_bytes(fs1.at[k, pl.ds(0, ny * nq - 1)], send.at[ITERS, k, 0])
        for t in range(ITERS):
            wait_bytes(a1_in.at[t, k, pl.ds(0, nxc - 1)], send.at[t, k, S_A1])
            wait_bytes(a2_in.at[t, k, pl.ds(0, 3)], send.at[t, k, S_A2])
            wait_bytes(vall.at[t, k, pl.ds(0, ny - 1)], send.at[t, k, S_B5])
            wait_bytes(b1_out.at[t, k, pl.ds(0, ny - 1)], send.at[t, k, S_B1])
            wait_bytes(b2_in.at[t, k, pl.ds(0, nq - 1)], send.at[t, k, S_B2])
            wait_bytes(b3_in.at[t, k], send.at[t, k, S_B3])
            wait_bytes(vall.at[t, k, 0, pl.ds(0, nq - 1)], send.at[t, k, S_B4])


def deliver(n, *refs):
    copies = [pltpu.make_async_copy(refs[i], refs[n + i], refs[2 * n].at[i]) for i in range(n)]
    for copy in copies:
        copy.start()
    for copy in copies:
        copy.wait()


def shards(grid, *args):
    green_real, station, source = args[0], args[2], args[3]
    rows = green_real.shape[0]
    rows_total = rows * lax.axis_size("sta")
    cols_total = green_real.shape[1] * lax.axis_size("src")
    ny, nq, groups = grid.ny, grid.nq, grid.groups
    width = green_real.shape[1] // nq
    padded = width + LANES
    n_events = args[6].shape[0]
    args = list(args[:6]) + [a.reshape(1, n_events) for a in args[6:]]
    vmem = pl.BlockSpec(memory_space=pltpu.VMEM)
    hbm = pl.BlockSpec(memory_space=pltpu.HBM)
    half = ny // 2
    message = rows + LANES

    def buf(*shape, kind=BF16):
        return pltpu.VMEM(shape, kind)

    scratch = [
        buf(*station.shape, kind=F32),
        buf(*source.shape, kind=F32),
        buf(1, n_events, kind=F32),
        buf(1, n_events, kind=F32),
        buf(1, n_events, kind=F32),
        buf(nq, 2 * rows, width),
        buf(grid.nz, 2 * nq, width),
        buf(groups, nq, PART, width, kind=F32),
        buf(ITERS + 1, groups, ny, nq, PART, padded),
        buf(ITERS, groups, 2, half, PART, message),
        buf(ITERS, groups, grid.nxc, half, PART, message),
        buf(ITERS, groups, 4, half, PART, message),
        buf(groups, ny * nq, PART, LANES, kind=F32),
        buf(grid.nzh * grid.nxc, PART, LANES, kind=F32),
        buf(ITERS, groups, ny, nq, PART, padded),
        buf(ITERS, groups, nq, ny, PART, padded),
        buf(ITERS, groups, nq, PART, padded),
        buf(ITERS, groups, nq, PART, padded),
        buf(ITERS, groups, PART, padded),
        buf(ITERS, groups, PART, padded),
        buf(groups, ny, PART, rows, kind=F32),
        buf(groups, ny, PART, rows, kind=F32),
        buf(groups, 3, ny, PART, LANES, kind=F32),
        pltpu.SemaphoreType.DMA((7 + 2 * nq,)),
        pltpu.SemaphoreType.DMA,
        pltpu.SemaphoreType.DMA,
        pltpu.SemaphoreType.DMA((ITERS + 1, groups, 5 + 2 * nq)),
        pltpu.SemaphoreType.DMA((ITERS + 1, groups, 5 + 2 * nq)),
    ]
    shapes = [station.shape, source.shape, source.shape, source.shape] + [(1, n_events)] * 3
    shapes = [jax.ShapeDtypeStruct(shape, F32) for shape in shapes]
    outs = pl.pallas_call(
        functools.partial(kernel, grid, rows_total, cols_total),
        out_shape=shapes,
        in_specs=[hbm] * 9,
        out_specs=[vmem] * 7,
        scratch_shapes=scratch,
        compiler_params=pltpu.CompilerParams(
            collective_id=0, has_side_effects=True),
        name="lsqr",
    )(*args)
    outs = pl.pallas_call(
        functools.partial(deliver, len(outs)),
        out_shape=shapes,
        in_specs=[vmem] * 7,
        out_specs=[hbm] * 7,
        scratch_shapes=[pltpu.SemaphoreType.DMA((7,))],
        name="deliver",
    )(*outs)
    return tuple(outs[:4]) + tuple(a.reshape(n_events) for a in outs[4:])


def build(mesh, grid):
    placed = (
        P("sta", "src"),
        P("sta", "src"),
        P(None, "src", "sta"),
        P(None, "sta", "src"),
        P(None, "sta", "src"),
        P(None, "sta", "src"),
        P(),
        P(),
        P(),
    )
    return jax.shard_map(
        functools.partial(shards, grid),
        mesh=mesh,
        in_specs=placed,
        out_specs=placed[2:],
        check_vma=False,
    )


def solution(mesh):
    return build(mesh, FULL)
```

```python
import functools

import jax
import jax.numpy as jnp
from jax import lax
from jax.experimental import pallas as pl
from jax.experimental.pallas import tpu as pltpu
from jax.sharding import PartitionSpec as P

ITERS = 3
EPS = 1e-06
MESH = pl.DeviceIdType.MESH
F32 = jnp.float32
BF16 = jnp.bfloat16
LANES = 128
PART = 8


class Grid:
    def __init__(self, ny, nq, nhalf, nzh, nx, ncore):
        self.ny, self.nq, self.nhalf = ny, nq, nhalf
        self.nzh, self.nx, self.ncore = nzh, nx, ncore
        self.nz = nq * nhalf
        self.nxc = nx * ncore
        self.groups = 2 * self.nz // PART
        self.per = self.nz // self.groups


FULL = Grid(4, 4, 2, 2, 4, 2)


def kernel(grid, rows_total, cols_total, *refs):
    (green_re, green_im, station_in, source_in, search_in, sol_in, alpha_in, rho_in, phi_in,
     station_out, source_out, search_out, sol_out, alpha_out, rho_out, phi_out,
     station_ref, source_ref, alpha_ref, rho_ref, phi_ref,
     gmat, first, first_rows, vall, a1_out, a1_in, a2_in, fs1, fs2,
     b1_out, b1_in, b1s_out, b1s_in, b2_out, b2_in, b3_out, b3_in, beta_sq,
     uhat, unorm, coef, load_sem, first_send, first_recv, send, recv) = refs
    ny, nq, nxc, groups, per = grid.ny, grid.nq, grid.nxc, grid.groups, grid.per
    n_src = grid.nzh * nxc
    width = source_ref.shape[-1] // nq
    rows_half = gmat.shape[1] // 2
    half_rows = ny // 2
    ratio = cols_total / rows_total
    S_A1, S_A2, S_B2, S_B3, S_B5, S_B1S, S_B5S, S_B1 = 0, 1, 2, 3, 4, 5, 6, 7
    S_B4 = S_B1 + nq

    sta = lax.axis_index("sta")
    src = lax.axis_index("src")
    y = lax.rem(sta, ny)
    z = lax.div(sta, ny)
    quad = lax.rem(z, nq)
    zhalf = lax.div(z, nq)
    zh = lax.div(src, nxc)
    xc = lax.rem(src, nxc)
    core = lax.rem(xc, 2)

    def at_sta(z_at, y_at):
        return {"sta": z_at * ny + y_at, "src": src}

    def at_src(src_to):
        return {"sta": sta, "src": src_to}

    def y_peer(d):
        return lax.rem(y + d, ny)

    def by_distance(i, far_first):
        sign = -1 if far_first else 1
        table = [sorted(range(nq), key=lambda q: sign * abs(q - p))[i] for p in range(nq)]
        value = jnp.int32(table[0])
        for p in range(1, nq):
            value = jnp.where(quad == p, table[p], value)
        return value

    y_order = sorted(range(1, ny), key=lambda d: -min(d, ny - d))
    peers = []
    for d in range(1, grid.nz):
        peers.append(at_sta(lax.rem(z + d, grid.nz), y))
    for d in range(1, ny):
        for e in range(nq):
            peers.append(at_sta(zhalf * nq + lax.rem(quad + e, nq), y_peer(d)))
    for d in range(1, n_src):
        peers.append(at_src(lax.rem(src + d, n_src)))
    barrier = pltpu.get_barrier_semaphore()
    for peer in peers:
        pl.semaphore_signal(barrier, inc=1, device_id=peer, device_id_type=MESH)

    loads = [
        pltpu.make_async_copy(a, b, load_sem.at[i])
        for i, (a, b) in enumerate((
            (source_in, source_ref), (station_in, station_ref), (alpha_in, alpha_ref), (rho_in, rho_ref),
            (phi_in, phi_ref), (search_in, search_out), (sol_in, sol_out)))
    ]
    g_loads = []
    for q in range(nq):
        cut = pl.ds(q * width, width)
        for p, green in enumerate((green_re, green_im)):
            g_loads.append(pltpu.make_async_copy(
                green.at[:, cut], gmat.at[q, pl.ds(p * rows_half, rows_half)],
                load_sem.at[len(loads) + 2 * q + p]))
    for load in loads + g_loads:
        load.start()
    for load in loads:
        load.wait()

    pieces = [source_ref[p, :, q * width : (q + 1) * width] for p in range(2) for q in range(nq)]
    first[z] = jnp.concatenate(pieces, axis=0).astype(BF16)

    def remote(src_at, dst_at, send_sem, recv_sem, to):
        pltpu.make_async_remote_copy(
            src_ref=src_at, dst_ref=dst_at, send_sem=send_sem, recv_sem=recv_sem,
            device_id=to, device_id_type=MESH).start()

    def wait_bytes(ref, sem):
        pltpu.make_async_copy(ref, ref, sem).wait()

    def is_re(shape):
        return lax.broadcasted_iota(jnp.int32, shape, len(shape) - 2) < per

    def swap(a):
        return pltpu.roll(a, per, a.ndim - 2)

    def encode(total):
        high = total.astype(BF16).astype(F32)
        return jnp.where(is_re(total.shape), high, total - high)

    def decode(pair):
        return pair + swap(pair)

    def lanes(a):
        return jnp.broadcast_to(a, a.shape[:-1] + (LANES,))

    def event_of(k, shape):
        zl = lax.rem(lax.broadcasted_iota(jnp.int32, shape, 1), per)
        return (k * per + zl) * ny + lax.broadcasted_iota(jnp.int32, shape, 0)

    n_events = alpha_ref.shape[-1]

    def spread(ref, k):
        shape = (ny, PART, n_events)
        lane = lax.broadcasted_iota(jnp.int32, shape, 2)
        row = jnp.broadcast_to(ref[...].reshape(1, 1, n_events), shape)
        return lanes(jnp.sum(jnp.where(lane == event_of(k, shape), row, 0.0), axis=-1, keepdims=True))

    alpha = [spread(alpha_ref, k) for k in range(groups)]
    rho = [spread(rho_ref, k) for k in range(groups)]
    phi = [spread(phi_ref, k) for k in range(groups)]

    pl.semaphore_wait(barrier, len(peers))

    for d in range(grid.nz - 1, 0, -1):
        remote(first.at[z], first.at[z], first_send, first_recv, at_sta(lax.rem(z + d, grid.nz), y))
    for load in g_loads:
        load.wait()
    wait_bytes(first.at[pl.ds(0, grid.nz - 1)], first_recv)

    def share_y(t, k, q):
        here = vall.at[t, k, y, q]
        for d in y_order:
            remote(here, here, send.at[t, k, S_B5], recv.at[t, k, S_B5], at_sta(z, y_peer(d)))

    for k in range(groups):
        for e in range(per):
            block = first[k * per + e].astype(F32)
            for p in range(2):
                for q in range(nq):
                    first_rows[k, q, p * per + e : p * per + e + 1, :] = block[p * nq + q : p * nq + q + 1, :]
        vall[0, k, y] = first_rows[k].astype(BF16)
        for q in range(nq):
            share_y(0, k, q)

    def columns(t, k, q):
        return vall[t, k, :, q].astype(F32)

    def beta_squares(t, k):
        return beta_sq[t, k]

    def root(total, count):
        return jnp.sqrt(total * (1.0 / count) + EPS)

    def squares_of(values):
        total = jnp.sum(values[0] * values[0], axis=-1, keepdims=True)
        for value in values[1:]:
            total += jnp.sum(value * value, axis=-1, keepdims=True)
        total = lanes(total)
        return total + swap(total)

    seg_a = LANES // half_rows

    def pack(chunks):
        tile = chunks[0]
        lane = lax.broadcasted_iota(jnp.int32, tile.shape, 1)
        for i in range(1, half_rows):
            tile = jnp.where(lane >= i * seg_a, chunks[i], tile)
        return tile

    def unpack(tile):
        return [lanes(tile[:, i * seg_a : i * seg_a + 1]) for i in range(half_rows)]

    contract = (((1,), (1,)), ((), ()))

    def stage_a1(t, k):
        wait_bytes(vall.at[t, k, pl.ds(0, ny - 1)], recv.at[t, k, S_B5])
        values = [columns(t, k, q) for q in range(nq)]
        product = jnp.zeros((ny * PART, 2 * rows_half), F32)
        for q in range(nq):
            left = values[q].reshape(ny * PART, width).astype(BF16)
            product += lax.dot_general(left, gmat[q], contract, preferred_element_type=F32)
        product = product.reshape(ny, PART, 2 * rows_half)
        turned = swap(product[..., rows_half:])
        image = product[..., :rows_half] + jnp.where(is_re(turned.shape), -turned, turned)
        if t == 0:
            scalars = jnp.zeros((ny, PART, LANES), F32)
            shape = image.shape
            event = event_of(k, shape)
            part_re = is_re(shape)
            per_src = station_ref.shape[1]
            for n in range(per_src):
                both = jnp.where(part_re, jnp.broadcast_to(station_ref[0, n : n + 1, :][None], shape),
                                 jnp.broadcast_to(station_ref[1, n : n + 1, :][None], shape))
                image -= jnp.where(event == src * per_src + n, alpha[k] * both, 0.0)
        else:
            scalars = encode(squares_of(values))
        message = image.astype(BF16)
        for c in range(2):
            cut = slice(c * half_rows, (c + 1) * half_rows)
            a1_out[t, k, c, 0:half_rows] = message[cut]
            a1_out[t, k, c, half_rows] = pack(scalars[cut]).astype(BF16)
        a1_in[t, k, xc] = a1_out[t, k, core]
        for d in range(1, nxc):
            to = lax.rem(xc + d, nxc)
            remote(a1_out.at[t, k, lax.rem(to, 2)], a1_in.at[t, k, xc], send.at[t, k, S_A1], recv.at[t, k, S_A1],
                   at_src(zh * nxc + to))

    other = (1 - zh) * nxc + xc - core

    def stage_a2(t, k):
        wait_bytes(a1_in.at[t, k, pl.ds(0, nxc - 1)], recv.at[t, k, S_A1])
        total = a1_in[t, k, 0].astype(F32)
        for i in range(1, nxc):
            total += a1_in[t, k, i].astype(F32)
        a2_in[t, k, zh * 2 + core, 0:half_rows] = total[0:half_rows].astype(BF16)
        a2_in[t, k, zh * 2 + core, half_rows] = encode(decode(total[half_rows])).astype(BF16)
        here = a2_in.at[t, k, zh * 2 + core]
        for to in (other + core, other + 1 - core, src + 1 - 2 * core):
            remote(here, here, send.at[t, k, S_A2], recv.at[t, k, S_A2], at_src(to))

    def stage_a3(t, k):
        wait_bytes(a2_in.at[t, k, pl.ds(0, 3)], recv.at[t, k, S_A2])
        totals = [a2_in[t, k, c].astype(F32) + a2_in[t, k, 2 + c].astype(F32) for c in range(2)]
        vector = jnp.concatenate([total[0:half_rows] for total in totals], axis=0)
        if t > 0:
            squares = [decode(total[half_rows]) for total in totals]
            alpha[k] = root(jnp.stack(unpack(squares[0]) + unpack(squares[1])), cols_total)
            wait_bytes(beta_sq.at[t, k, pl.ds(0, ny - 1)], recv.at[t, k, S_B5S])
            beta = root(beta_squares(t, k), rows_total)
            vector = vector / alpha[k] - alpha[k] * (uhat[k] / beta)
        uhat[k] = vector
        b1s_out[t, k] = squares_of([vector])
        turned = swap(vector)
        left = jnp.concatenate([vector, jnp.where(is_re(turned.shape), turned, -turned)], axis=-1)
        left = left.reshape(ny * PART, 2 * rows_half).astype(BF16)
        for i in range(nq):
            q = by_distance(i, True)
            back = jnp.dot(left, gmat[q], preferred_element_type=F32)
            b1_out[t, k, :, q] = back.reshape(ny, PART, width).astype(BF16)
            if i == 0:
                for d in y_order:
                    remote(b1s_out.at[t, k, y_peer(d)], b1s_in.at[t, k, y], send.at[t, k, S_B1S],
                           recv.at[t, k, S_B1S], at_sta(z, y_peer(d)))
            for d in y_order:
                remote(b1_out.at[t, k, y_peer(d), q], b1_in.at[t, k, q, y], send.at[t, k, S_B1],
                       recv.at[t, k, S_B1 + q], at_sta(z, y_peer(d)))

    def stage_b2(t, k):
        wait_bytes(b1s_in.at[t, k, pl.ds(0, ny - 1)], recv.at[t, k, S_B1S])
        squares = b1s_out[t, k, y]
        for d in range(1, ny):
            squares += b1s_in[t, k, y_peer(d)]
        squares = encode(squares).astype(BF16)
        for i in range(nq):
            q = by_distance(i, True)
            wait_bytes(b1_in.at[t, k, q, pl.ds(0, ny - 1)], recv.at[t, k, S_B1 + q])
            total = b1_out[t, k, y, q].astype(F32)
            for d in range(1, ny):
                total += b1_in[t, k, q, y_peer(d)].astype(F32)
            b2_out[t, k, q, :, 0:width] = total.astype(BF16)
            b2_out[t, k, q, :, width:] = squares
            if i < nq - 1:
                remote(b2_out.at[t, k, q], b2_in.at[t, k, quad], send.at[t, k, S_B2], recv.at[t, k, S_B2],
                       at_sta(zhalf * nq + q, y))

    def stage_b3(t, k):
        wait_bytes(b2_in.at[t, k, pl.ds(0, nq - 1)], recv.at[t, k, S_B2])
        b2_in[t, k, quad] = b2_out[t, k, quad]
        total = b2_in[t, k, 0].astype(F32)
        for i in range(1, nq):
            total += b2_in[t, k, i].astype(F32)
        b3_out[t, k, :, 0:width] = total[:, :width].astype(BF16)
        b3_out[t, k, :, width:] = encode(decode(total[:, width:])).astype(BF16)
        remote(b3_out.at[t, k], b3_in.at[t, k], send.at[t, k, S_B3], recv.at[t, k, S_B3],
               at_sta((1 - zhalf) * nq + quad, y))

    def stage_b4(t, k):
        wait_bytes(b3_in.at[t, k], recv.at[t, k, S_B3])
        total = b3_out[t, k].astype(F32) + b3_in[t, k].astype(F32)
        squares = decode(total[:, width:])
        beta = root(squares, rows_total)[:, 0:1]
        before = vall[t, k, y, quad].astype(F32)
        if t > 0:
            before = before / coef[k, 0, y][:, 0:1]
        after = total[:, :width] * (ratio / beta) - beta * before
        after = after.astype(BF16)
        if t == ITERS - 1:
            after32 = after.astype(F32)
            lane = lax.broadcasted_iota(jnp.int32, squares.shape, 1)
            slot = y * nq + quad
            fs1[k, slot] = jnp.where(lane < LANES // 2, squares_of([after32]), squares)
            for d in range(ny - 1, -1, -1):
                for e in range(nq):
                    if d or e:
                        remote(fs1.at[k, slot], fs1.at[k, slot], send.at[t + 1, k, 0], recv.at[t + 1, k, 0],
                               at_sta(zhalf * nq + lax.rem(quad + e, nq), y_peer(d)))
        vall[t + 1, k, y, quad] = after
        here = vall.at[t + 1, k, y, quad]
        for i in range(nq - 1):
            to = by_distance(i, True)
            remote(here, here, send.at[t, k, S_B4], recv.at[t, k, S_B4 + quad], at_sta(zhalf * nq + to, y))
        if t < ITERS - 1:
            share_y(t + 1, k, quad)
            beta_sq[t + 1, k, y] = squares
            for d in y_order:
                remote(beta_sq.at[t + 1, k, y], beta_sq.at[t + 1, k, y], send.at[t + 1, k, S_B5S],
                       recv.at[t + 1, k, S_B5S], at_sta(z, y_peer(d)))

    def stage_b5(t, k):
        for i in range(1, nq):
            q = by_distance(i, False)
            wait_bytes(vall.at[t + 1, k, y, q], recv.at[t, k, S_B4 + q])
            if t < ITERS - 1:
                share_y(t + 1, k, q)

    mine_k = lax.div(z, per)
    mine_row = lax.rem(z, per)

    def rotate(k, beta):
        rho_new = jnp.sqrt(rho[k] * rho[k] + beta * beta)
        cosine = rho[k] / rho_new
        sine = beta / rho_new
        coef[k, 0] = alpha[k]
        coef[k, 1] = cosine * phi[k] / rho_new
        coef[k, 2] = sine * alpha[k] / rho_new
        rho[k] = -cosine * alpha[k]
        phi[k] = sine * phi[k]

    def own_rows(t):
        block = vall[t, mine_k, y].astype(F32)
        row = lax.broadcasted_iota(jnp.int32, block.shape, 1)
        result = []
        for p in range(2):
            picked = jnp.sum(jnp.where(row == p * per + mine_row, block, 0.0), axis=1, keepdims=True)
            result.append(jnp.concatenate([picked[q] for q in range(nq)], axis=-1))
        return result

    def step(t, rows):
        def scalar(i):
            return coef[mine_k, i, y, pl.ds(mine_row, 1), :][:, 0:1]

        alpha_own, step_sol, step_dir = scalar(0), scalar(1), scalar(2)
        for p in range(2):
            vector = rows[p] / alpha_own
            before = search_out[p]
            sol_out[p] = sol_out[p] + step_sol * before
            search_out[p] = vector - step_dir * before
            if t == ITERS:
                source_out[p] = vector

    for t in range(ITERS):
        for k in range(groups):
            stage_a1(t, k)
        for k in range(groups):
            stage_a2(t, k)
        for k in range(groups):
            stage_a3(t, k)
        if t > 0:
            for k in range(groups):
                rotate(k, root(beta_squares(t, k), rows_total))
            step(t, own_rows(t))
        for stage in (stage_b2, stage_b3, stage_b4, stage_b5):
            for k in range(groups):
                stage(t, k)

    row = lax.broadcasted_iota(jnp.int32, (PART, LANES), 0)
    lane = lax.broadcasted_iota(jnp.int32, (PART, LANES), 1)
    seg = LANES // ny
    squares = jnp.zeros((PART, LANES), F32)
    betas = []
    for k in range(groups):
        wait_bytes(fs1.at[k, pl.ds(0, ny * nq - 1)], recv.at[ITERS, k, 0])
        beta_rows = []
        for i in range(ny):
            total = fs1[k, i * nq]
            beta_rows.append(lanes(total[:, LANES // 2 : LANES // 2 + 1]))
            for q in range(1, nq):
                total += fs1[k, i * nq + q]
            squares = jnp.where((lax.div(lane, seg) == i) & (lax.div(row, per) == k), lanes(total[:, 0:1]), squares)
        betas.append(root(jnp.stack(beta_rows), rows_total))
    fs2[src] = squares
    for d in range(1, n_src):
        remote(fs2.at[src], fs2.at[src], send.at[ITERS, 0, 1], recv.at[ITERS, 0, 1],
               at_src(lax.rem(src + d, n_src)))

    for k in range(groups):
        unorm[k] = uhat[k] / betas[k]
    per_src = station_ref.shape[1]
    for n in range(per_src):
        event = src * per_src + n
        at_y, at_z = lax.rem(event, ny), lax.div(event, ny)
        for p in range(2):
            station_out[p, n : n + 1, :] = unorm[
                lax.div(at_z, per), at_y, pl.ds(p * per + lax.rem(at_z, per), 1), :]
    last_rows = own_rows(ITERS)

    wait_bytes(fs2.at[pl.ds(0, n_src - 1)], recv.at[ITERS, 0, 1])
    squares = fs2[0]
    for i in range(1, n_src):
        squares += fs2[i]
    for k in range(groups):
        kept = jnp.where(lax.div(row, per) == k, squares, 0.0)
        kept = kept + swap(kept)
        alpha[k] = root(jnp.stack([lanes(kept[:, i * seg : i * seg + 1]) for i in range(ny)]), cols_total)
        rotate(k, betas[k])
    step(ITERS, last_rows)

    def collect(values):
        shape = (ny, PART, n_events)
        lane = lax.broadcasted_iota(jnp.int32, shape, 2)
        total = jnp.zeros((1, n_events), F32)
        for k in range(groups):
            keep = (lane == event_of(k, shape)) & is_re(shape)
            kept = jnp.where(keep, values[k][..., 0:1], 0.0).reshape(ny * PART, n_events)
            total += jnp.sum(kept, axis=0, keepdims=True)
        return total

    alpha_out[...] = collect(alpha)
    rho_out[...] = collect(rho)
    phi_out[...] = collect(phi)

    wait_bytes(first.at[pl.ds(0, grid.nz - 1)], first_send)
    wait_bytes(fs2.at[pl.ds(0, n_src - 1)], send.at[ITERS, 0, 1])
    for k in range(groups):
        wait_bytes(fs1.at[k, pl.ds(0, ny * nq - 1)], send.at[ITERS, k, 0])
        for t in range(ITERS):
            wait_bytes(a1_in.at[t, k, pl.ds(0, nxc - 1)], send.at[t, k, S_A1])
            wait_bytes(a2_in.at[t, k, pl.ds(0, 3)], send.at[t, k, S_A2])
            wait_bytes(vall.at[t, k, pl.ds(0, ny - 1)], send.at[t, k, S_B5])
            wait_bytes(b1_out.at[t, k, pl.ds(0, ny - 1)], send.at[t, k, S_B1])
            wait_bytes(b2_in.at[t, k, pl.ds(0, nq - 1)], send.at[t, k, S_B2])
            wait_bytes(b3_in.at[t, k], send.at[t, k, S_B3])
            wait_bytes(vall.at[t, k, 0, pl.ds(0, nq - 1)], send.at[t, k, S_B4])
            wait_bytes(b1s_in.at[t, k, pl.ds(0, ny - 1)], send.at[t, k, S_B1S])
            if t > 0:
                wait_bytes(beta_sq.at[t, k, pl.ds(0, ny - 1)], send.at[t, k, S_B5S])


def deliver(n, *refs):
    copies = [pltpu.make_async_copy(refs[i], refs[n + i], refs[2 * n].at[i]) for i in range(n)]
    for copy in copies:
        copy.start()
    for copy in copies:
        copy.wait()


def shards(grid, *args):
    green_real, station, source = args[0], args[2], args[3]
    rows = green_real.shape[0]
    rows_total = rows * lax.axis_size("sta")
    cols_total = green_real.shape[1] * lax.axis_size("src")
    ny, nq, groups = grid.ny, grid.nq, grid.groups
    width = green_real.shape[1] // nq
    padded = width + LANES
    n_events = args[6].shape[0]
    args = list(args[:6]) + [a.reshape(1, n_events) for a in args[6:]]
    vmem = pl.BlockSpec(memory_space=pltpu.VMEM)
    hbm = pl.BlockSpec(memory_space=pltpu.HBM)
    half = ny // 2

    def buf(*shape, kind=BF16):
        return pltpu.VMEM(shape, kind)

    scratch = [
        buf(*station.shape, kind=F32),
        buf(*source.shape, kind=F32),
        buf(1, n_events, kind=F32),
        buf(1, n_events, kind=F32),
        buf(1, n_events, kind=F32),
        buf(nq, 2 * rows, width),
        buf(grid.nz, 2 * nq, width),
        buf(groups, nq, PART, width, kind=F32),
        buf(ITERS + 1, groups, ny, nq, PART, width),
        buf(ITERS, groups, 2, half + 1, PART, LANES),
        buf(ITERS, groups, grid.nxc, half + 1, PART, LANES),
        buf(ITERS, groups, 4, half + 1, PART, LANES),
        buf(groups, ny * nq, PART, LANES, kind=F32),
        buf(grid.nzh * grid.nxc, PART, LANES, kind=F32),
        buf(ITERS, groups, ny, nq, PART, width),
        buf(ITERS, groups, nq, ny, PART, width),
        buf(ITERS, groups, ny, PART, LANES, kind=F32),
        buf(ITERS, groups, ny, PART, LANES, kind=F32),
        buf(ITERS, groups, nq, PART, padded),
        buf(ITERS, groups, nq, PART, padded),
        buf(ITERS, groups, PART, padded),
        buf(ITERS, groups, PART, padded),
        buf(ITERS, groups, ny, PART, LANES, kind=F32),
        buf(groups, ny, PART, rows, kind=F32),
        buf(groups, ny, PART, rows, kind=F32),
        buf(groups, 3, ny, PART, LANES, kind=F32),
        pltpu.SemaphoreType.DMA((7 + 2 * nq,)),
        pltpu.SemaphoreType.DMA,
        pltpu.SemaphoreType.DMA,
        pltpu.SemaphoreType.DMA((ITERS + 1, groups, 7 + 2 * nq)),
        pltpu.SemaphoreType.DMA((ITERS + 1, groups, 7 + 2 * nq)),
    ]
    shapes = [station.shape, source.shape, source.shape, source.shape] + [(1, n_events)] * 3
    shapes = [jax.ShapeDtypeStruct(shape, F32) for shape in shapes]
    outs = pl.pallas_call(
        functools.partial(kernel, grid, rows_total, cols_total),
        out_shape=shapes,
        in_specs=[hbm] * 9,
        out_specs=[vmem] * 7,
        scratch_shapes=scratch,
        compiler_params=pltpu.CompilerParams(
            collective_id=0, has_side_effects=True),
        name="lsqr",
    )(*args)
    outs = pl.pallas_call(
        functools.partial(deliver, len(outs)),
        out_shape=shapes,
        in_specs=[vmem] * 7,
        out_specs=[hbm] * 7,
        scratch_shapes=[pltpu.SemaphoreType.DMA((7,))],
        name="deliver",
    )(*outs)
    return tuple(outs[:4]) + tuple(a.reshape(n_events) for a in outs[4:])


def build(mesh, grid):
    placed = (
        P("sta", "src"),
        P("sta", "src"),
        P(None, "src", "sta"),
        P(None, "sta", "src"),
        P(None, "sta", "src"),
        P(None, "sta", "src"),
        P(),
        P(),
        P(),
    )
    return jax.shard_map(
        functools.partial(shards, grid),
        mesh=mesh,
        in_specs=placed,
        out_specs=placed[2:],
        check_vma=False,
    )


def solution(mesh):
    return build(mesh, FULL)
```

```python
import functools

import jax
import jax.numpy as jnp
from jax import lax
from jax.experimental import pallas as pl
from jax.experimental.pallas import tpu as pltpu
from jax.sharding import PartitionSpec as P

ITERS = 3
EPS = 1e-06
MESH = pl.DeviceIdType.MESH
F32 = jnp.float32
BF16 = jnp.bfloat16
LANES = 128
PART = 8


class Grid:
    def __init__(self, ny, nq, nhalf, nzh, nx, ncore):
        self.ny, self.nq, self.nhalf = ny, nq, nhalf
        self.nzh, self.nx, self.ncore = nzh, nx, ncore
        self.nz = nq * nhalf
        self.nxc = nx * ncore
        self.groups = 2 * self.nz // PART
        self.per = self.nz // self.groups


FULL = Grid(4, 4, 2, 2, 4, 2)


def kernel(grid, rows_total, cols_total, *refs):
    (green_re, green_im, station_in, source_in, search_in, sol_in, alpha_in, rho_in, phi_in,
     station_out, source_out, search_out, sol_out, alpha_out, rho_out, phi_out,
     station_ref, source_ref, alpha_ref, rho_ref, phi_ref,
     gmat, first, first_rows, vall, a1_out, a1_in, a2_in, fs1, fs2,
     b1_out, b1_in, b3_out, b3_in, beta_sq,
     uhat, unorm, coef, load_sem, first_send, first_recv, send, recv) = refs
    ny, nq, nxc, groups, per = grid.ny, grid.nq, grid.nxc, grid.groups, grid.per
    n_src = grid.nzh * nxc
    width = source_ref.shape[-1] // nq
    rows_half = gmat.shape[1] // 2
    half_rows = ny // 2
    ratio = cols_total / rows_total
    S_A1, S_A2, S_B1, S_B3, S_V, S_BETA, S_LAST = range(7)
    n_own = ny * nq

    sta = lax.axis_index("sta")
    src = lax.axis_index("src")
    y = lax.rem(sta, ny)
    z = lax.div(sta, ny)
    quad = lax.rem(z, nq)
    zhalf = lax.div(z, nq)
    zh = lax.div(src, nxc)
    xc = lax.rem(src, nxc)
    core = lax.rem(xc, 2)

    def at_sta(z_at, y_at):
        return {"sta": z_at * ny + y_at, "src": src}

    def at_src(src_to):
        return {"sta": sta, "src": src_to}

    def y_peer(d):
        return lax.rem(y + d, ny)

    def by_distance(i, far_first):
        sign = -1 if far_first else 1
        table = [sorted(range(nq), key=lambda q: sign * abs(q - p))[i] for p in range(nq)]
        value = jnp.int32(table[0])
        for p in range(1, nq):
            value = jnp.where(quad == p, table[p], value)
        return value

    y_order = sorted(range(1, ny), key=lambda d: -min(d, ny - d))
    peers = []
    for d in range(1, grid.nz):
        peers.append(at_sta(lax.rem(z + d, grid.nz), y))
    for d in range(1, ny):
        for e in range(nq):
            peers.append(at_sta(zhalf * nq + lax.rem(quad + e, nq), y_peer(d)))
    for d in range(1, n_src):
        peers.append(at_src(lax.rem(src + d, n_src)))
    barrier = pltpu.get_barrier_semaphore()
    for peer in peers:
        pl.semaphore_signal(barrier, inc=1, device_id=peer, device_id_type=MESH)

    loads = [
        pltpu.make_async_copy(a, b, load_sem.at[i])
        for i, (a, b) in enumerate((
            (source_in, source_ref), (station_in, station_ref), (alpha_in, alpha_ref), (rho_in, rho_ref),
            (phi_in, phi_ref), (search_in, search_out), (sol_in, sol_out)))
    ]
    g_loads = []
    for q in range(nq):
        cut = pl.ds(q * width, width)
        for p, green in enumerate((green_re, green_im)):
            g_loads.append(pltpu.make_async_copy(
                green.at[:, cut], gmat.at[q, pl.ds(p * rows_half, rows_half)],
                load_sem.at[len(loads) + 2 * q + p]))
    for load in loads + g_loads:
        load.start()
    for load in loads:
        load.wait()

    pieces = [source_ref[p, :, q * width : (q + 1) * width] for p in range(2) for q in range(nq)]
    first[z] = jnp.concatenate(pieces, axis=0).astype(BF16)

    def remote(src_at, dst_at, send_sem, recv_sem, to):
        pltpu.make_async_remote_copy(
            src_ref=src_at, dst_ref=dst_at, send_sem=send_sem, recv_sem=recv_sem,
            device_id=to, device_id_type=MESH).start()

    def wait_bytes(ref, sem):
        pltpu.make_async_copy(ref, ref, sem).wait()

    def is_re(shape):
        return lax.broadcasted_iota(jnp.int32, shape, len(shape) - 2) < per

    def swap(a):
        return pltpu.roll(a, per, a.ndim - 2)

    def encode(total):
        high = total.astype(BF16).astype(F32)
        return jnp.where(is_re(total.shape), high, total - high)

    def decode(pair):
        return pair + swap(pair)

    def lanes(a):
        return jnp.broadcast_to(a, a.shape[:-1] + (LANES,))

    def event_of(k, shape):
        zl = lax.rem(lax.broadcasted_iota(jnp.int32, shape, 1), per)
        return (k * per + zl) * ny + lax.broadcasted_iota(jnp.int32, shape, 0)

    n_events = alpha_ref.shape[-1]

    def spread(ref, k):
        shape = (ny, PART, n_events)
        lane = lax.broadcasted_iota(jnp.int32, shape, 2)
        row = jnp.broadcast_to(ref[...].reshape(1, 1, n_events), shape)
        return lanes(jnp.sum(jnp.where(lane == event_of(k, shape), row, 0.0), axis=-1, keepdims=True))

    alpha = [spread(alpha_ref, k) for k in range(groups)]
    rho = [spread(rho_ref, k) for k in range(groups)]
    phi = [spread(phi_ref, k) for k in range(groups)]

    pl.semaphore_wait(barrier, len(peers))

    for d in range(grid.nz - 1, 0, -1):
        remote(first.at[z], first.at[z], first_send, first_recv, at_sta(lax.rem(z + d, grid.nz), y))
    for load in g_loads:
        load.wait()
    wait_bytes(first.at[pl.ds(0, grid.nz - 1)], first_recv)

    for k in range(groups):
        for e in range(per):
            block = first[k * per + e].astype(F32)
            for p in range(2):
                for q in range(nq):
                    first_rows[k, q, p * per + e : p * per + e + 1, :] = block[p * nq + q : p * nq + q + 1, :]
        mine = pl.ds(y * nq, nq)
        vall[0, k, mine] = first_rows[k].astype(BF16)
        for d in y_order:
            remote(vall.at[0, k, mine], vall.at[0, k, mine], send.at[0, k, S_V], recv.at[0, k, S_V],
                   at_sta(z, y_peer(d)))

    def blocks_in(t):
        return n_own - (nq if t == 0 else 1)

    def columns(t, k, q):
        return jnp.stack([vall[t, k, i * nq + q].astype(F32) for i in range(ny)])

    def beta_squares(t, k):
        return beta_sq[t, k]

    def root(total, count):
        return jnp.sqrt(total * (1.0 / count) + EPS)

    def squares_of(values):
        total = jnp.sum(values[0] * values[0], axis=-1, keepdims=True)
        for value in values[1:]:
            total += jnp.sum(value * value, axis=-1, keepdims=True)
        total = lanes(total)
        return total + swap(total)

    seg_a = LANES // half_rows

    def pack(chunks):
        tile = chunks[0]
        lane = lax.broadcasted_iota(jnp.int32, tile.shape, 1)
        for i in range(1, half_rows):
            tile = jnp.where(lane >= i * seg_a, chunks[i], tile)
        return tile

    def unpack(tile):
        return [lanes(tile[:, i * seg_a : i * seg_a + 1]) for i in range(half_rows)]

    contract = (((1,), (1,)), ((), ()))

    slot = y * nq + quad

    def stage_a1(t, k):
        wait_bytes(vall.at[t, k, pl.ds(0, blocks_in(t))], recv.at[t, k, S_V])
        values = [columns(t, k, q) for q in range(nq)]
        product = jnp.zeros((ny * PART, 2 * rows_half), F32)
        for q in range(nq):
            left = values[q].reshape(ny * PART, width).astype(BF16)
            product += lax.dot_general(left, gmat[q], contract, preferred_element_type=F32)
        product = product.reshape(ny, PART, 2 * rows_half)
        turned = swap(product[..., rows_half:])
        image = product[..., :rows_half] + jnp.where(is_re(turned.shape), -turned, turned)
        if t == 0:
            scalars = jnp.zeros((ny, PART, LANES), F32)
            shape = image.shape
            event = event_of(k, shape)
            part_re = is_re(shape)
            per_src = station_ref.shape[1]
            for n in range(per_src):
                both = jnp.where(part_re, jnp.broadcast_to(station_ref[0, n : n + 1, :][None], shape),
                                 jnp.broadcast_to(station_ref[1, n : n + 1, :][None], shape))
                image -= jnp.where(event == src * per_src + n, alpha[k] * both, 0.0)
        else:
            scalars = encode(squares_of(values))
        message = image.astype(BF16)
        for c in range(2):
            cut = slice(c * half_rows, (c + 1) * half_rows)
            a1_out[t, k, c, 0:half_rows] = message[cut]
            a1_out[t, k, c, half_rows] = pack(scalars[cut]).astype(BF16)
        a1_in[t, k, xc] = a1_out[t, k, core]
        for d in range(1, nxc):
            to = lax.rem(xc + d, nxc)
            remote(a1_out.at[t, k, lax.rem(to, 2)], a1_in.at[t, k, xc], send.at[t, k, S_A1], recv.at[t, k, S_A1],
                   at_src(zh * nxc + to))

    other = (1 - zh) * nxc + xc - core

    def stage_a2(t, k):
        wait_bytes(a1_in.at[t, k, pl.ds(0, nxc - 1)], recv.at[t, k, S_A1])
        total = a1_in[t, k, 0].astype(F32)
        for i in range(1, nxc):
            total += a1_in[t, k, i].astype(F32)
        a2_in[t, k, zh * 2 + core, 0:half_rows] = total[0:half_rows].astype(BF16)
        a2_in[t, k, zh * 2 + core, half_rows] = encode(decode(total[half_rows])).astype(BF16)
        here = a2_in.at[t, k, zh * 2 + core]
        for to in (other + core, other + 1 - core, src + 1 - 2 * core):
            remote(here, here, send.at[t, k, S_A2], recv.at[t, k, S_A2], at_src(to))

    def stage_a3(t, k):
        wait_bytes(a2_in.at[t, k, pl.ds(0, 3)], recv.at[t, k, S_A2])
        totals = [a2_in[t, k, c].astype(F32) + a2_in[t, k, 2 + c].astype(F32) for c in range(2)]
        vector = jnp.concatenate([total[0:half_rows] for total in totals], axis=0)
        if t > 0:
            squares = [decode(total[half_rows]) for total in totals]
            alpha[k] = root(jnp.stack(unpack(squares[0]) + unpack(squares[1])), cols_total)
            wait_bytes(beta_sq.at[t, k, pl.ds(0, ny - 1)], recv.at[t, k, S_BETA])
            beta = root(beta_squares(t, k), rows_total)
            vector = vector / alpha[k] - alpha[k] * (uhat[k] / beta)
        uhat[k] = vector
        scalars = encode(squares_of([vector])).astype(BF16)
        turned = swap(vector)
        left = jnp.concatenate([vector, jnp.where(is_re(turned.shape), turned, -turned)], axis=-1)
        left = left.reshape(ny * PART, 2 * rows_half).astype(BF16)
        for i in range(nq):
            q = by_distance(i, True)
            back = jnp.dot(left, gmat[q], preferred_element_type=F32)
            b1_out[t, k, q, :, :, 0:width] = back.reshape(ny, PART, width).astype(BF16)
            b1_out[t, k, q, :, :, width:] = scalars
            if i < nq - 1:
                remote(b1_out.at[t, k, q, y], b1_in.at[t, k, slot], send.at[t, k, S_B1], recv.at[t, k, S_B1],
                       at_sta(zhalf * nq + q, y))
            for d in y_order:
                remote(b1_out.at[t, k, q, y_peer(d)], b1_in.at[t, k, slot], send.at[t, k, S_B1],
                       recv.at[t, k, S_B1], at_sta(zhalf * nq + q, y_peer(d)))

    def stage_b3(t, k):
        b1_in[t, k, slot] = b1_out[t, k, quad, y]
        wait_bytes(b1_in.at[t, k, pl.ds(0, n_own - 1)], recv.at[t, k, S_B1])
        total = b1_in[t, k, 0].astype(F32)
        for i in range(1, n_own):
            total += b1_in[t, k, i].astype(F32)
        b3_out[t, k, :, 0:width] = total[:, :width].astype(BF16)
        b3_out[t, k, :, width:] = encode(decode(total[:, width:])).astype(BF16)
        remote(b3_out.at[t, k], b3_in.at[t, k], send.at[t, k, S_B3], recv.at[t, k, S_B3],
               at_sta((1 - zhalf) * nq + quad, y))

    def to_half(ref, send_sem, recv_sem):
        for i in range(nq):
            q = by_distance(i, True)
            for d in y_order + [0]:
                if d or i < nq - 1:
                    remote(ref, ref, send_sem, recv_sem, at_sta(zhalf * nq + q, y_peer(d)))

    def stage_b4(t, k):
        before = vall[t, k, slot].astype(F32)
        if t > 0:
            before = before / coef[k, 0, y][:, 0:1]
        wait_bytes(b3_in.at[t, k], recv.at[t, k, S_B3])
        total = b3_out[t, k].astype(F32) + b3_in[t, k].astype(F32)
        squares = decode(total[:, width:])
        beta = root(squares, rows_total)[:, 0:1]
        after = total[:, :width] * (ratio / beta) - beta * before
        after = after.astype(BF16)
        vall[t + 1, k, slot] = after
        here = vall.at[t + 1, k, slot]
        if t < ITERS - 1:
            to_half(here, send.at[t + 1, k, S_V], recv.at[t + 1, k, S_V])
            beta_sq[t + 1, k, y] = squares
            for d in y_order:
                remote(beta_sq.at[t + 1, k, y], beta_sq.at[t + 1, k, y], send.at[t + 1, k, S_BETA],
                       recv.at[t + 1, k, S_BETA], at_sta(z, y_peer(d)))
        else:
            lane = lax.broadcasted_iota(jnp.int32, squares.shape, 1)
            fs1[k, slot] = jnp.where(lane < LANES // 2, squares_of([after.astype(F32)]), squares)
            to_half(fs1.at[k, slot], send.at[t + 1, k, 0], recv.at[t + 1, k, 0])
            for i in range(nq - 1):
                to = by_distance(i, True)
                remote(here, here, send.at[t, k, S_LAST], recv.at[t, k, S_LAST], at_sta(zhalf * nq + to, y))

    mine_k = lax.div(z, per)
    mine_row = lax.rem(z, per)

    def rotate(k, beta):
        rho_new = jnp.sqrt(rho[k] * rho[k] + beta * beta)
        cosine = rho[k] / rho_new
        sine = beta / rho_new
        coef[k, 0] = alpha[k]
        coef[k, 1] = cosine * phi[k] / rho_new
        coef[k, 2] = sine * alpha[k] / rho_new
        rho[k] = -cosine * alpha[k]
        phi[k] = sine * phi[k]

    def own_rows(t):
        block = vall[t, mine_k, pl.ds(y * nq, nq)].astype(F32)
        row = lax.broadcasted_iota(jnp.int32, block.shape, 1)
        result = []
        for p in range(2):
            picked = jnp.sum(jnp.where(row == p * per + mine_row, block, 0.0), axis=1, keepdims=True)
            result.append(jnp.concatenate([picked[q] for q in range(nq)], axis=-1))
        return result

    def step(t, rows):
        def scalar(i):
            return coef[mine_k, i, y, pl.ds(mine_row, 1), :][:, 0:1]

        alpha_own, step_sol, step_dir = scalar(0), scalar(1), scalar(2)
        for p in range(2):
            vector = rows[p] / alpha_own
            before = search_out[p]
            sol_out[p] = sol_out[p] + step_sol * before
            search_out[p] = vector - step_dir * before
            if t == ITERS:
                source_out[p] = vector

    for t in range(ITERS):
        for k in range(groups):
            stage_a1(t, k)
        for k in range(groups):
            stage_a2(t, k)
        for k in range(groups):
            stage_a3(t, k)
        if t > 0:
            for k in range(groups):
                rotate(k, root(beta_squares(t, k), rows_total))
            step(t, own_rows(t))
        for stage in (stage_b3, stage_b4):
            for k in range(groups):
                stage(t, k)

    row = lax.broadcasted_iota(jnp.int32, (PART, LANES), 0)
    lane = lax.broadcasted_iota(jnp.int32, (PART, LANES), 1)
    seg = LANES // ny
    squares = jnp.zeros((PART, LANES), F32)
    betas = []
    for k in range(groups):
        wait_bytes(fs1.at[k, pl.ds(0, ny * nq - 1)], recv.at[ITERS, k, 0])
        beta_rows = []
        for i in range(ny):
            total = fs1[k, i * nq]
            beta_rows.append(lanes(total[:, LANES // 2 : LANES // 2 + 1]))
            for q in range(1, nq):
                total += fs1[k, i * nq + q]
            squares = jnp.where((lax.div(lane, seg) == i) & (lax.div(row, per) == k), lanes(total[:, 0:1]), squares)
        betas.append(root(jnp.stack(beta_rows), rows_total))
    fs2[src] = squares
    for d in range(1, n_src):
        remote(fs2.at[src], fs2.at[src], send.at[ITERS, 0, 1], recv.at[ITERS, 0, 1],
               at_src(lax.rem(src + d, n_src)))

    for k in range(groups):
        unorm[k] = uhat[k] / betas[k]
    per_src = station_ref.shape[1]
    for n in range(per_src):
        event = src * per_src + n
        at_y, at_z = lax.rem(event, ny), lax.div(event, ny)
        for p in range(2):
            station_out[p, n : n + 1, :] = unorm[
                lax.div(at_z, per), at_y, pl.ds(p * per + lax.rem(at_z, per), 1), :]
    for k in range(groups):
        wait_bytes(vall.at[ITERS, k, pl.ds(0, nq - 1)], recv.at[ITERS - 1, k, S_LAST])
    last_rows = own_rows(ITERS)

    wait_bytes(fs2.at[pl.ds(0, n_src - 1)], recv.at[ITERS, 0, 1])
    squares = fs2[0]
    for i in range(1, n_src):
        squares += fs2[i]
    for k in range(groups):
        kept = jnp.where(lax.div(row, per) == k, squares, 0.0)
        kept = kept + swap(kept)
        alpha[k] = root(jnp.stack([lanes(kept[:, i * seg : i * seg + 1]) for i in range(ny)]), cols_total)
        rotate(k, betas[k])
    step(ITERS, last_rows)

    def collect(values):
        shape = (ny, PART, n_events)
        lane = lax.broadcasted_iota(jnp.int32, shape, 2)
        total = jnp.zeros((1, n_events), F32)
        for k in range(groups):
            keep = (lane == event_of(k, shape)) & is_re(shape)
            kept = jnp.where(keep, values[k][..., 0:1], 0.0).reshape(ny * PART, n_events)
            total += jnp.sum(kept, axis=0, keepdims=True)
        return total

    alpha_out[...] = collect(alpha)
    rho_out[...] = collect(rho)
    phi_out[...] = collect(phi)

    wait_bytes(first.at[pl.ds(0, grid.nz - 1)], first_send)
    wait_bytes(fs2.at[pl.ds(0, n_src - 1)], send.at[ITERS, 0, 1])
    for k in range(groups):
        wait_bytes(fs1.at[k, pl.ds(0, ny * nq - 1)], send.at[ITERS, k, 0])
        for t in range(ITERS):
            wait_bytes(a1_in.at[t, k, pl.ds(0, nxc - 1)], send.at[t, k, S_A1])
            wait_bytes(a2_in.at[t, k, pl.ds(0, 3)], send.at[t, k, S_A2])
            wait_bytes(vall.at[t, k, pl.ds(0, blocks_in(t))], send.at[t, k, S_V])
            wait_bytes(b1_in.at[t, k, pl.ds(0, n_own - 1)], send.at[t, k, S_B1])
            wait_bytes(b3_in.at[t, k], send.at[t, k, S_B3])
            if t > 0:
                wait_bytes(beta_sq.at[t, k, pl.ds(0, ny - 1)], send.at[t, k, S_BETA])
        wait_bytes(vall.at[ITERS, k, pl.ds(0, nq - 1)], send.at[ITERS - 1, k, S_LAST])


def deliver(n, *refs):
    copies = [pltpu.make_async_copy(refs[i], refs[n + i], refs[2 * n].at[i]) for i in range(n)]
    for copy in copies:
        copy.start()
    for copy in copies:
        copy.wait()


def shards(grid, *args):
    green_real, station, source = args[0], args[2], args[3]
    rows = green_real.shape[0]
    rows_total = rows * lax.axis_size("sta")
    cols_total = green_real.shape[1] * lax.axis_size("src")
    ny, nq, groups = grid.ny, grid.nq, grid.groups
    width = green_real.shape[1] // nq
    padded = width + LANES
    n_events = args[6].shape[0]
    args = list(args[:6]) + [a.reshape(1, n_events) for a in args[6:]]
    vmem = pl.BlockSpec(memory_space=pltpu.VMEM)
    hbm = pl.BlockSpec(memory_space=pltpu.HBM)
    half = ny // 2

    def buf(*shape, kind=BF16):
        return pltpu.VMEM(shape, kind)

    scratch = [
        buf(*station.shape, kind=F32),
        buf(*source.shape, kind=F32),
        buf(1, n_events, kind=F32),
        buf(1, n_events, kind=F32),
        buf(1, n_events, kind=F32),
        buf(nq, 2 * rows, width),
        buf(grid.nz, 2 * nq, width),
        buf(groups, nq, PART, width, kind=F32),
        buf(ITERS + 1, groups, ny * nq, PART, width),
        buf(ITERS, groups, 2, half + 1, PART, LANES),
        buf(ITERS, groups, grid.nxc, half + 1, PART, LANES),
        buf(ITERS, groups, 4, half + 1, PART, LANES),
        buf(groups, ny * nq, PART, LANES, kind=F32),
        buf(grid.nzh * grid.nxc, PART, LANES, kind=F32),
        buf(ITERS, groups, nq, ny, PART, padded),
        buf(ITERS, groups, ny * nq, PART, padded),
        buf(ITERS, groups, PART, padded),
        buf(ITERS, groups, PART, padded),
        buf(ITERS, groups, ny, PART, LANES, kind=F32),
        buf(groups, ny, PART, rows, kind=F32),
        buf(groups, ny, PART, rows, kind=F32),
        buf(groups, 3, ny, PART, LANES, kind=F32),
        pltpu.SemaphoreType.DMA((7 + 2 * nq,)),
        pltpu.SemaphoreType.DMA,
        pltpu.SemaphoreType.DMA,
        pltpu.SemaphoreType.DMA((ITERS + 1, groups, 7)),
        pltpu.SemaphoreType.DMA((ITERS + 1, groups, 7)),
    ]
    shapes = [station.shape, source.shape, source.shape, source.shape] + [(1, n_events)] * 3
    shapes = [jax.ShapeDtypeStruct(shape, F32) for shape in shapes]
    outs = pl.pallas_call(
        functools.partial(kernel, grid, rows_total, cols_total),
        out_shape=shapes,
        in_specs=[hbm] * 9,
        out_specs=[vmem] * 7,
        scratch_shapes=scratch,
        compiler_params=pltpu.CompilerParams(
            collective_id=0, has_side_effects=True),
        name="lsqr",
    )(*args)
    outs = pl.pallas_call(
        functools.partial(deliver, len(outs)),
        out_shape=shapes,
        in_specs=[vmem] * 7,
        out_specs=[hbm] * 7,
        scratch_shapes=[pltpu.SemaphoreType.DMA((7,))],
        name="deliver",
    )(*outs)
    return tuple(outs[:4]) + tuple(a.reshape(n_events) for a in outs[4:])


def build(mesh, grid):
    placed = (
        P("sta", "src"),
        P("sta", "src"),
        P(None, "src", "sta"),
        P(None, "sta", "src"),
        P(None, "sta", "src"),
        P(None, "sta", "src"),
        P(),
        P(),
        P(),
    )
    return jax.shard_map(
        functools.partial(shards, grid),
        mesh=mesh,
        in_specs=placed,
        out_specs=placed[2:],
        check_vma=False,
    )


def solution(mesh):
    return build(mesh, FULL)
```

```python
import functools

import jax
import jax.numpy as jnp
from jax import lax
from jax.experimental import pallas as pl
from jax.experimental.pallas import tpu as pltpu
from jax.sharding import PartitionSpec as P

ITERS = 3
EPS = 1e-06
MESH = pl.DeviceIdType.MESH
F32 = jnp.float32
BF16 = jnp.bfloat16
LANES = 128
PART = 8


class Grid:
    def __init__(self, ny, nq, nhalf, nzh, nx, ncore):
        self.ny, self.nq, self.nhalf = ny, nq, nhalf
        self.nzh, self.nx, self.ncore = nzh, nx, ncore
        self.nz = nq * nhalf
        self.nxc = nx * ncore
        self.groups = 2 * self.nz // PART
        self.per = self.nz // self.groups


FULL = Grid(4, 4, 2, 2, 4, 2)


def kernel(grid, rows_total, cols_total, *refs):
    (green_re, green_im, station_in, source_in, search_in, sol_in, alpha_in, rho_in, phi_in,
     station_out, source_out, search_out, sol_out, alpha_out, rho_out, phi_out,
     station_ref, source_ref, alpha_ref, rho_ref, phi_ref,
     gmat, first, first_rows, vall, a1_in, a2_in, fs1, fs2,
     b1_out, b1_in, by_out, by_in, bq_in, b3_out, b3_in, beta_sq,
     uhat, unorm, coef, load_sem, first_send, first_recv, send, recv) = refs
    ny, nq, nxc, groups, per = grid.ny, grid.nq, grid.nxc, grid.groups, grid.per
    n_src = grid.nzh * nxc
    width = source_ref.shape[-1] // nq
    rows_half = gmat.shape[1] // 2
    ratio = cols_total / rows_total
    S_A1, S_A2, S_B1, S_B3, S_V, S_BETA, S_LAST, S_BY, S_BQ = range(9)
    n_own = ny * nq

    sta = lax.axis_index("sta")
    src = lax.axis_index("src")
    y = lax.rem(sta, ny)
    z = lax.div(sta, ny)
    quad = lax.rem(z, nq)
    zhalf = lax.div(z, nq)
    zh = lax.div(src, nxc)
    xc = lax.rem(src, nxc)

    def at_sta(z_at, y_at):
        return {"sta": z_at * ny + y_at, "src": src}

    def at_src(src_to):
        return {"sta": sta, "src": src_to}

    def y_peer(d):
        return lax.rem(y + d, ny)

    def by_distance(i, far_first):
        sign = -1 if far_first else 1
        table = [sorted(range(nq), key=lambda q: sign * abs(q - p))[i] for p in range(nq)]
        value = jnp.int32(table[0])
        for p in range(1, nq):
            value = jnp.where(quad == p, table[p], value)
        return value

    y_order = sorted(range(1, ny), key=lambda d: -min(d, ny - d))
    peers = []
    for d in range(1, grid.nz):
        peers.append(at_sta(lax.rem(z + d, grid.nz), y))
    for d in range(1, ny):
        for e in range(nq):
            peers.append(at_sta(zhalf * nq + lax.rem(quad + e, nq), y_peer(d)))
    for d in range(1, n_src):
        peers.append(at_src(lax.rem(src + d, n_src)))
    barrier = pltpu.get_barrier_semaphore()
    for peer in peers:
        pl.semaphore_signal(barrier, inc=1, device_id=peer, device_id_type=MESH)

    loads = [
        pltpu.make_async_copy(a, b, load_sem.at[i])
        for i, (a, b) in enumerate((
            (source_in, source_ref), (station_in, station_ref), (alpha_in, alpha_ref), (rho_in, rho_ref),
            (phi_in, phi_ref), (search_in, search_out), (sol_in, sol_out)))
    ]
    g_loads = []
    for q in range(nq):
        cut = pl.ds(q * width, width)
        for p, green in enumerate((green_re, green_im)):
            g_loads.append(pltpu.make_async_copy(
                green.at[:, cut], gmat.at[q, pl.ds(p * rows_half, rows_half)],
                load_sem.at[len(loads) + 2 * q + p]))
    for load in loads + g_loads:
        load.start()
    for load in loads:
        load.wait()

    pieces = [source_ref[p, :, q * width : (q + 1) * width] for p in range(2) for q in range(nq)]
    first[z] = jnp.concatenate(pieces, axis=0).astype(BF16)

    def remote(src_at, dst_at, send_sem, recv_sem, to):
        pltpu.make_async_remote_copy(
            src_ref=src_at, dst_ref=dst_at, send_sem=send_sem, recv_sem=recv_sem,
            device_id=to, device_id_type=MESH).start()

    def wait_bytes(ref, sem):
        pltpu.make_async_copy(ref, ref, sem).wait()

    def is_re(shape):
        return lax.broadcasted_iota(jnp.int32, shape, len(shape) - 2) < per

    def swap(a):
        return pltpu.roll(a, per, a.ndim - 2)

    def encode(total):
        high = total.astype(BF16).astype(F32)
        return jnp.where(is_re(total.shape), high, total - high)

    def decode(pair):
        return pair + swap(pair)

    def lanes(a):
        return jnp.broadcast_to(a, a.shape[:-1] + (LANES,))

    def event_of(k, shape):
        zl = lax.rem(lax.broadcasted_iota(jnp.int32, shape, 1), per)
        return (k * per + zl) * ny + lax.broadcasted_iota(jnp.int32, shape, 0)

    n_events = alpha_ref.shape[-1]

    def spread(ref, k):
        shape = (ny, PART, n_events)
        lane = lax.broadcasted_iota(jnp.int32, shape, 2)
        row = jnp.broadcast_to(ref[...].reshape(1, 1, n_events), shape)
        return lanes(jnp.sum(jnp.where(lane == event_of(k, shape), row, 0.0), axis=-1, keepdims=True))

    alpha = [spread(alpha_ref, k) for k in range(groups)]
    rho = [spread(rho_ref, k) for k in range(groups)]
    phi = [spread(phi_ref, k) for k in range(groups)]

    pl.semaphore_wait(barrier, len(peers))

    for d in range(grid.nz - 1, 0, -1):
        remote(first.at[z], first.at[z], first_send, first_recv, at_sta(lax.rem(z + d, grid.nz), y))
    for load in g_loads:
        load.wait()
    wait_bytes(first.at[pl.ds(0, grid.nz - 1)], first_recv)

    for k in range(groups):
        for e in range(per):
            block = first[k * per + e].astype(F32)
            for p in range(2):
                for q in range(nq):
                    first_rows[k, q, p * per + e : p * per + e + 1, :] = block[p * nq + q : p * nq + q + 1, :]
        mine = pl.ds(y * nq, nq)
        vall[0, k, mine] = first_rows[k].astype(BF16)
        for d in y_order:
            remote(vall.at[0, k, mine], vall.at[0, k, mine], send.at[0, k, S_V], recv.at[0, k, S_V],
                   at_sta(z, y_peer(d)))

    def blocks_in(t):
        return n_own - (nq if t == 0 else 1)

    def columns(t, k, q):
        return jnp.stack([vall[t, k, i * nq + q].astype(F32) for i in range(ny)])

    def beta_squares(t, k):
        return beta_sq[t, k]

    def root(total, count):
        return jnp.sqrt(total * (1.0 / count) + EPS)

    def squares_of(values):
        total = jnp.sum(values[0] * values[0], axis=-1, keepdims=True)
        for value in values[1:]:
            total += jnp.sum(value * value, axis=-1, keepdims=True)
        total = lanes(total)
        return total + swap(total)

    seg = LANES // ny

    def pack(chunks):
        tile = chunks[0]
        lane = lax.broadcasted_iota(jnp.int32, tile.shape, 1)
        for i in range(1, ny):
            tile = jnp.where(lane >= i * seg, chunks[i], tile)
        return tile

    def unpack(tile):
        return jnp.stack([lanes(tile[:, i * seg : i * seg + 1]) for i in range(ny)])

    contract = (((1,), (1,)), ((), ()))

    slot = y * nq + quad

    def stage_a1(t, k):
        wait_bytes(vall.at[t, k, pl.ds(0, blocks_in(t))], recv.at[t, k, S_V])
        values = [columns(t, k, q) for q in range(nq)]
        product = jnp.zeros((ny * PART, 2 * rows_half), F32)
        for q in range(nq):
            left = values[q].reshape(ny * PART, width).astype(BF16)
            product += lax.dot_general(left, gmat[q], contract, preferred_element_type=F32)
        product = product.reshape(ny, PART, 2 * rows_half)
        turned = swap(product[..., rows_half:])
        image = product[..., :rows_half] + jnp.where(is_re(turned.shape), -turned, turned)
        if t == 0:
            scalars = jnp.zeros((ny, PART, LANES), F32)
            shape = image.shape
            event = event_of(k, shape)
            part_re = is_re(shape)
            per_src = station_ref.shape[1]
            for n in range(per_src):
                both = jnp.where(part_re, jnp.broadcast_to(station_ref[0, n : n + 1, :][None], shape),
                                 jnp.broadcast_to(station_ref[1, n : n + 1, :][None], shape))
                image -= jnp.where(event == src * per_src + n, alpha[k] * both, 0.0)
        else:
            scalars = encode(squares_of(values))
        a1_in[t, k, xc, 0:ny] = image.astype(BF16)
        a1_in[t, k, xc, ny] = pack(scalars).astype(BF16)
        here = a1_in.at[t, k, xc]
        for d in range(1, nxc):
            remote(here, here, send.at[t, k, S_A1], recv.at[t, k, S_A1], at_src(zh * nxc + lax.rem(xc + d, nxc)))

    def stage_a2(t, k):
        wait_bytes(a1_in.at[t, k, pl.ds(0, nxc - 1)], recv.at[t, k, S_A1])
        total = a1_in[t, k, 0].astype(F32)
        for i in range(1, nxc):
            total += a1_in[t, k, i].astype(F32)
        a2_in[t, k, zh, 0:ny] = total[0:ny].astype(BF16)
        a2_in[t, k, zh, ny] = encode(decode(total[ny])).astype(BF16)
        here = a2_in.at[t, k, zh]
        remote(here, here, send.at[t, k, S_A2], recv.at[t, k, S_A2], at_src((1 - zh) * nxc + xc))

    def stage_a3(t, k):
        wait_bytes(a2_in.at[t, k, 0], recv.at[t, k, S_A2])
        total = a2_in[t, k, 0].astype(F32) + a2_in[t, k, 1].astype(F32)
        vector = total[0:ny]
        if t > 0:
            alpha[k] = root(unpack(decode(total[ny])), cols_total)
            wait_bytes(beta_sq.at[t, k, pl.ds(0, ny - 1)], recv.at[t, k, S_BETA])
            beta = root(beta_squares(t, k), rows_total)
            vector = vector / alpha[k] - alpha[k] * (uhat[k] / beta)
        uhat[k] = vector
        turned = swap(vector)
        left = jnp.concatenate([vector, jnp.where(is_re(turned.shape), turned, -turned)], axis=-1)
        left = left.reshape(ny * PART, 2 * rows_half).astype(BF16)
        for i in range(nq):
            q = by_distance(i, True)
            back = jnp.dot(left, gmat[q], preferred_element_type=F32)
            b1_out[t, k, q] = back.reshape(ny, PART, width).astype(BF16)
            if i < nq - 1:
                remote(b1_out.at[t, k, q, y], b1_in.at[t, k, slot], send.at[t, k, S_B1], recv.at[t, k, S_B1],
                       at_sta(zhalf * nq + q, y))
            for d in y_order:
                remote(b1_out.at[t, k, q, y_peer(d)], b1_in.at[t, k, slot], send.at[t, k, S_B1],
                       recv.at[t, k, S_B1], at_sta(zhalf * nq + q, y_peer(d)))

            if i == 0:
                by_out[t, k] = squares_of([vector])
                for d in y_order:
                    remote(by_out.at[t, k, y_peer(d)], by_in.at[t, k, y], send.at[t, k, S_BY], recv.at[t, k, S_BY],
                           at_sta(z, y_peer(d)))

    def stage_squares(t, k):
        b1_in[t, k, slot] = b1_out[t, k, quad, y]
        wait_bytes(by_in.at[t, k, pl.ds(0, ny - 1)], recv.at[t, k, S_BY])
        squares = by_out[t, k, y]
        for d in range(1, ny):
            squares += by_in[t, k, y_peer(d)]
        bq_in[t, k, quad] = squares
        here = bq_in.at[t, k, quad]
        for i in range(nq - 1):
            remote(here, here, send.at[t, k, S_BQ], recv.at[t, k, S_BQ],
                   at_sta(zhalf * nq + by_distance(i, True), y))

    def stage_b3(t, k):
        wait_bytes(bq_in.at[t, k, pl.ds(0, nq - 1)], recv.at[t, k, S_BQ])
        squares = bq_in[t, k, 0]
        for i in range(1, nq):
            squares += bq_in[t, k, i]
        b3_out[t, k, :, width:] = encode(squares).astype(BF16)
        wait_bytes(b1_in.at[t, k, pl.ds(0, n_own - 1)], recv.at[t, k, S_B1])
        total = b1_in[t, k, 0].astype(F32)
        for i in range(1, n_own):
            total += b1_in[t, k, i].astype(F32)
        b3_out[t, k, :, 0:width] = total.astype(BF16)
        remote(b3_out.at[t, k], b3_in.at[t, k], send.at[t, k, S_B3], recv.at[t, k, S_B3],
               at_sta((1 - zhalf) * nq + quad, y))

    def to_half(ref, send_sem, recv_sem):
        for i in range(nq):
            q = by_distance(i, True)
            for d in y_order + [0]:
                if d or i < nq - 1:
                    remote(ref, ref, send_sem, recv_sem, at_sta(zhalf * nq + q, y_peer(d)))

    def stage_b4(t, k):
        before = vall[t, k, slot].astype(F32)
        if t > 0:
            before = before / coef[k, 0, y][:, 0:1]
        wait_bytes(b3_in.at[t, k], recv.at[t, k, S_B3])
        total = b3_out[t, k].astype(F32) + b3_in[t, k].astype(F32)
        squares = decode(total[:, width:])
        beta = root(squares, rows_total)[:, 0:1]
        after = total[:, :width] * (ratio / beta) - beta * before
        after = after.astype(BF16)
        vall[t + 1, k, slot] = after
        here = vall.at[t + 1, k, slot]
        if t < ITERS - 1:
            to_half(here, send.at[t + 1, k, S_V], recv.at[t + 1, k, S_V])
            beta_sq[t + 1, k, y] = squares
            for d in y_order:
                remote(beta_sq.at[t + 1, k, y], beta_sq.at[t + 1, k, y], send.at[t + 1, k, S_BETA],
                       recv.at[t + 1, k, S_BETA], at_sta(z, y_peer(d)))
        else:
            lane = lax.broadcasted_iota(jnp.int32, squares.shape, 1)
            fs1[k, slot] = jnp.where(lane < LANES // 2, squares_of([after.astype(F32)]), squares)
            to_half(fs1.at[k, slot], send.at[t + 1, k, 0], recv.at[t + 1, k, 0])
            for i in range(nq - 1):
                to = by_distance(i, True)
                remote(here, here, send.at[t, k, S_LAST], recv.at[t, k, S_LAST], at_sta(zhalf * nq + to, y))

    mine_k = lax.div(z, per)
    mine_row = lax.rem(z, per)

    def rotate(k, beta):
        rho_new = jnp.sqrt(rho[k] * rho[k] + beta * beta)
        cosine = rho[k] / rho_new
        sine = beta / rho_new
        coef[k, 0] = alpha[k]
        coef[k, 1] = cosine * phi[k] / rho_new
        coef[k, 2] = sine * alpha[k] / rho_new
        rho[k] = -cosine * alpha[k]
        phi[k] = sine * phi[k]

    def own_rows(t):
        block = vall[t, mine_k, pl.ds(y * nq, nq)].astype(F32)
        row = lax.broadcasted_iota(jnp.int32, block.shape, 1)
        result = []
        for p in range(2):
            picked = jnp.sum(jnp.where(row == p * per + mine_row, block, 0.0), axis=1, keepdims=True)
            result.append(jnp.concatenate([picked[q] for q in range(nq)], axis=-1))
        return result

    def step(t, rows):
        def scalar(i):
            return coef[mine_k, i, y, pl.ds(mine_row, 1), :][:, 0:1]

        alpha_own, step_sol, step_dir = scalar(0), scalar(1), scalar(2)
        for p in range(2):
            vector = rows[p] / alpha_own
            before = search_out[p]
            sol_out[p] = sol_out[p] + step_sol * before
            search_out[p] = vector - step_dir * before
            if t == ITERS:
                source_out[p] = vector

    for t in range(ITERS):
        for k in range(groups):
            stage_a1(t, k)
        for k in range(groups):
            stage_a2(t, k)
        for k in range(groups):
            stage_a3(t, k)
        for k in range(groups):
            stage_squares(t, k)
        if t > 0:
            for k in range(groups):
                rotate(k, root(beta_squares(t, k), rows_total))
            step(t, own_rows(t))
        for stage in (stage_b3, stage_b4):
            for k in range(groups):
                stage(t, k)

    row = lax.broadcasted_iota(jnp.int32, (PART, LANES), 0)
    lane = lax.broadcasted_iota(jnp.int32, (PART, LANES), 1)
    squares = jnp.zeros((PART, LANES), F32)
    betas = []
    for k in range(groups):
        wait_bytes(fs1.at[k, pl.ds(0, ny * nq - 1)], recv.at[ITERS, k, 0])
        beta_rows = []
        for i in range(ny):
            total = fs1[k, i * nq]
            beta_rows.append(lanes(total[:, LANES // 2 : LANES // 2 + 1]))
            for q in range(1, nq):
                total += fs1[k, i * nq + q]
            squares = jnp.where((lax.div(lane, seg) == i) & (lax.div(row, per) == k), lanes(total[:, 0:1]), squares)
        betas.append(root(jnp.stack(beta_rows), rows_total))
    fs2[src] = squares
    for d in range(1, n_src):
        remote(fs2.at[src], fs2.at[src], send.at[ITERS, 0, 1], recv.at[ITERS, 0, 1],
               at_src(lax.rem(src + d, n_src)))

    for k in range(groups):
        unorm[k] = uhat[k] / betas[k]
    per_src = station_ref.shape[1]
    for n in range(per_src):
        event = src * per_src + n
        at_y, at_z = lax.rem(event, ny), lax.div(event, ny)
        for p in range(2):
            station_out[p, n : n + 1, :] = unorm[
                lax.div(at_z, per), at_y, pl.ds(p * per + lax.rem(at_z, per), 1), :]
    for k in range(groups):
        wait_bytes(vall.at[ITERS, k, pl.ds(0, nq - 1)], recv.at[ITERS - 1, k, S_LAST])
    last_rows = own_rows(ITERS)

    wait_bytes(fs2.at[pl.ds(0, n_src - 1)], recv.at[ITERS, 0, 1])
    squares = fs2[0]
    for i in range(1, n_src):
        squares += fs2[i]
    for k in range(groups):
        kept = jnp.where(lax.div(row, per) == k, squares, 0.0)
        kept = kept + swap(kept)
        alpha[k] = root(jnp.stack([lanes(kept[:, i * seg : i * seg + 1]) for i in range(ny)]), cols_total)
        rotate(k, betas[k])
    step(ITERS, last_rows)

    def collect(values):
        shape = (ny, PART, n_events)
        lane = lax.broadcasted_iota(jnp.int32, shape, 2)
        total = jnp.zeros((1, n_events), F32)
        for k in range(groups):
            keep = (lane == event_of(k, shape)) & is_re(shape)
            kept = jnp.where(keep, values[k][..., 0:1], 0.0).reshape(ny * PART, n_events)
            total += jnp.sum(kept, axis=0, keepdims=True)
        return total

    alpha_out[...] = collect(alpha)
    rho_out[...] = collect(rho)
    phi_out[...] = collect(phi)

    wait_bytes(first.at[pl.ds(0, grid.nz - 1)], first_send)
    wait_bytes(fs2.at[pl.ds(0, n_src - 1)], send.at[ITERS, 0, 1])
    for k in range(groups):
        wait_bytes(fs1.at[k, pl.ds(0, ny * nq - 1)], send.at[ITERS, k, 0])
        for t in range(ITERS):
            wait_bytes(a1_in.at[t, k, pl.ds(0, nxc - 1)], send.at[t, k, S_A1])
            wait_bytes(a2_in.at[t, k, 0], send.at[t, k, S_A2])
            wait_bytes(by_in.at[t, k, pl.ds(0, ny - 1)], send.at[t, k, S_BY])
            wait_bytes(bq_in.at[t, k, pl.ds(0, nq - 1)], send.at[t, k, S_BQ])
            wait_bytes(vall.at[t, k, pl.ds(0, blocks_in(t))], send.at[t, k, S_V])
            wait_bytes(b1_in.at[t, k, pl.ds(0, n_own - 1)], send.at[t, k, S_B1])
            wait_bytes(b3_in.at[t, k], send.at[t, k, S_B3])
            if t > 0:
                wait_bytes(beta_sq.at[t, k, pl.ds(0, ny - 1)], send.at[t, k, S_BETA])
        wait_bytes(vall.at[ITERS, k, pl.ds(0, nq - 1)], send.at[ITERS - 1, k, S_LAST])


def deliver(n, *refs):
    copies = [pltpu.make_async_copy(refs[i], refs[n + i], refs[2 * n].at[i]) for i in range(n)]
    for copy in copies:
        copy.start()
    for copy in copies:
        copy.wait()


def shards(grid, *args):
    green_real, station, source = args[0], args[2], args[3]
    rows = green_real.shape[0]
    rows_total = rows * lax.axis_size("sta")
    cols_total = green_real.shape[1] * lax.axis_size("src")
    ny, nq, groups = grid.ny, grid.nq, grid.groups
    width = green_real.shape[1] // nq
    padded = width + LANES
    n_events = args[6].shape[0]
    args = list(args[:6]) + [a.reshape(1, n_events) for a in args[6:]]
    vmem = pl.BlockSpec(memory_space=pltpu.VMEM)
    hbm = pl.BlockSpec(memory_space=pltpu.HBM)

    def buf(*shape, kind=BF16):
        return pltpu.VMEM(shape, kind)

    scratch = [
        buf(*station.shape, kind=F32),
        buf(*source.shape, kind=F32),
        buf(1, n_events, kind=F32),
        buf(1, n_events, kind=F32),
        buf(1, n_events, kind=F32),
        buf(nq, 2 * rows, width),
        buf(grid.nz, 2 * nq, width),
        buf(groups, nq, PART, width, kind=F32),
        buf(ITERS + 1, groups, ny * nq, PART, width),
        buf(ITERS, groups, grid.nxc, ny + 1, PART, LANES),
        buf(ITERS, groups, grid.nzh, ny + 1, PART, LANES),
        buf(groups, ny * nq, PART, LANES, kind=F32),
        buf(grid.nzh * grid.nxc, PART, LANES, kind=F32),
        buf(ITERS, groups, nq, ny, PART, width),
        buf(ITERS, groups, ny * nq, PART, width),
        buf(ITERS, groups, ny, PART, LANES, kind=F32),
        buf(ITERS, groups, ny, PART, LANES, kind=F32),
        buf(ITERS, groups, nq, PART, LANES, kind=F32),
        buf(ITERS, groups, PART, padded),
        buf(ITERS, groups, PART, padded),
        buf(ITERS, groups, ny, PART, LANES, kind=F32),
        buf(groups, ny, PART, rows, kind=F32),
        buf(groups, ny, PART, rows, kind=F32),
        buf(groups, 3, ny, PART, LANES, kind=F32),
        pltpu.SemaphoreType.DMA((7 + 2 * nq,)),
        pltpu.SemaphoreType.DMA,
        pltpu.SemaphoreType.DMA,
        pltpu.SemaphoreType.DMA((ITERS + 1, groups, 9)),
        pltpu.SemaphoreType.DMA((ITERS + 1, groups, 9)),
    ]
    shapes = [station.shape, source.shape, source.shape, source.shape] + [(1, n_events)] * 3
    shapes = [jax.ShapeDtypeStruct(shape, F32) for shape in shapes]
    outs = pl.pallas_call(
        functools.partial(kernel, grid, rows_total, cols_total),
        out_shape=shapes,
        in_specs=[hbm] * 9,
        out_specs=[vmem] * 7,
        scratch_shapes=scratch,
        compiler_params=pltpu.CompilerParams(
            collective_id=0, has_side_effects=True),
        name="lsqr",
    )(*args)
    outs = pl.pallas_call(
        functools.partial(deliver, len(outs)),
        out_shape=shapes,
        in_specs=[vmem] * 7,
        out_specs=[hbm] * 7,
        scratch_shapes=[pltpu.SemaphoreType.DMA((7,))],
        name="deliver",
    )(*outs)
    return tuple(outs[:4]) + tuple(a.reshape(n_events) for a in outs[4:])


def build(mesh, grid):
    placed = (
        P("sta", "src"),
        P("sta", "src"),
        P(None, "src", "sta"),
        P(None, "sta", "src"),
        P(None, "sta", "src"),
        P(None, "sta", "src"),
        P(),
        P(),
        P(),
    )
    return jax.shard_map(
        functools.partial(shards, grid),
        mesh=mesh,
        in_specs=placed,
        out_specs=placed[2:],
        check_vma=False,
    )


def solution(mesh):
    return build(mesh, FULL)
```

```python
import functools

import jax
import jax.numpy as jnp
from jax import lax
from jax.experimental import pallas as pl
from jax.experimental.pallas import tpu as pltpu
from jax.sharding import PartitionSpec as P

ITERS = 3
EPS = 1e-06
MESH = pl.DeviceIdType.MESH
F32 = jnp.float32
BF16 = jnp.bfloat16
LANES = 128
PART = 8


class Grid:
    def __init__(self, ny, nq, nhalf, nzh, nx, ncore):
        self.ny, self.nq, self.nhalf = ny, nq, nhalf
        self.nzh, self.nx, self.ncore = nzh, nx, ncore
        self.nz = nq * nhalf
        self.nxc = nx * ncore
        self.groups = 2 * self.nz // PART
        self.per = self.nz // self.groups


FULL = Grid(4, 4, 2, 2, 4, 2)


def kernel(grid, rows_total, cols_total, *refs):
    (green_re, green_im, station_in, source_in, search_in, sol_in, alpha_in, rho_in, phi_in,
     station_out, source_out, search_out, sol_out, alpha_out, rho_out, phi_out,
     station_ref, source_ref, alpha_ref, rho_ref, phi_ref,
     gmat, first, first_rows, vall, a1_in, a2_in, fs1, fs2,
     b1_out, b1_in, by_out, by_in, bq_in, b3_out, b3_in, beta_sq,
     uhat, unorm, coef, load_sem, first_send, first_recv, send, recv) = refs
    ny, nq, nxc, groups, per = grid.ny, grid.nq, grid.nxc, grid.groups, grid.per
    n_src = grid.nzh * nxc
    width = source_ref.shape[-1] // nq
    rows_half = gmat.shape[1] // 2
    ratio = cols_total / rows_total
    S_A1, S_A2, S_B3, S_BETA, S_LAST, S_BY, S_BQ, S_V, S_B1 = *range(8), 7 + nq
    n_own = ny * nq

    sta = lax.axis_index("sta")
    src = lax.axis_index("src")
    y = lax.rem(sta, ny)
    z = lax.div(sta, ny)
    quad = lax.rem(z, nq)
    zhalf = lax.div(z, nq)
    zh = lax.div(src, nxc)
    xc = lax.rem(src, nxc)

    def at_sta(z_at, y_at):
        return {"sta": z_at * ny + y_at, "src": src}

    def at_src(src_to):
        return {"sta": sta, "src": src_to}

    def y_peer(d):
        return lax.rem(y + d, ny)

    def by_distance(i, far_first):
        sign = -1 if far_first else 1
        table = [sorted(range(nq), key=lambda q: sign * abs(q - p))[i] for p in range(nq)]
        value = jnp.int32(table[0])
        for p in range(1, nq):
            value = jnp.where(quad == p, table[p], value)
        return value

    y_order = sorted(range(1, ny), key=lambda d: -min(d, ny - d))
    peers = []
    for d in range(1, grid.nz):
        peers.append(at_sta(lax.rem(z + d, grid.nz), y))
    for d in range(1, ny):
        for e in range(nq):
            peers.append(at_sta(zhalf * nq + lax.rem(quad + e, nq), y_peer(d)))
    for d in range(1, n_src):
        peers.append(at_src(lax.rem(src + d, n_src)))
    barrier = pltpu.get_barrier_semaphore()
    for peer in peers:
        pl.semaphore_signal(barrier, inc=1, device_id=peer, device_id_type=MESH)

    loads = [
        pltpu.make_async_copy(a, b, load_sem.at[i])
        for i, (a, b) in enumerate((
            (source_in, source_ref), (station_in, station_ref), (alpha_in, alpha_ref), (rho_in, rho_ref),
            (phi_in, phi_ref), (search_in, search_out), (sol_in, sol_out)))
    ]
    g_loads = []
    for q in range(nq):
        cut = pl.ds(q * width, width)
        for p, green in enumerate((green_re, green_im)):
            g_loads.append(pltpu.make_async_copy(
                green.at[:, cut], gmat.at[q, pl.ds(p * rows_half, rows_half)],
                load_sem.at[len(loads) + 2 * q + p]))
    for load in loads + g_loads:
        load.start()
    for load in loads:
        load.wait()

    pieces = [source_ref[p, :, q * width : (q + 1) * width] for p in range(2) for q in range(nq)]
    first[z] = jnp.concatenate(pieces, axis=0).astype(BF16)

    def remote(src_at, dst_at, send_sem, recv_sem, to):
        pltpu.make_async_remote_copy(
            src_ref=src_at, dst_ref=dst_at, send_sem=send_sem, recv_sem=recv_sem,
            device_id=to, device_id_type=MESH).start()

    def wait_bytes(ref, sem):
        pltpu.make_async_copy(ref, ref, sem).wait()

    def is_re(shape):
        return lax.broadcasted_iota(jnp.int32, shape, len(shape) - 2) < per

    def swap(a):
        return pltpu.roll(a, per, a.ndim - 2)

    def encode(total):
        high = total.astype(BF16).astype(F32)
        return jnp.where(is_re(total.shape), high, total - high)

    def decode(pair):
        return pair + swap(pair)

    def lanes(a):
        return jnp.broadcast_to(a, a.shape[:-1] + (LANES,))

    def event_of(k, shape):
        zl = lax.rem(lax.broadcasted_iota(jnp.int32, shape, 1), per)
        return (k * per + zl) * ny + lax.broadcasted_iota(jnp.int32, shape, 0)

    n_events = alpha_ref.shape[-1]

    def spread(ref, k):
        shape = (ny, PART, n_events)
        lane = lax.broadcasted_iota(jnp.int32, shape, 2)
        row = jnp.broadcast_to(ref[...].reshape(1, 1, n_events), shape)
        return lanes(jnp.sum(jnp.where(lane == event_of(k, shape), row, 0.0), axis=-1, keepdims=True))

    alpha = [spread(alpha_ref, k) for k in range(groups)]
    rho = [spread(rho_ref, k) for k in range(groups)]
    phi = [spread(phi_ref, k) for k in range(groups)]

    pl.semaphore_wait(barrier, len(peers))

    for d in range(grid.nz - 1, 0, -1):
        remote(first.at[z], first.at[z], first_send, first_recv, at_sta(lax.rem(z + d, grid.nz), y))
    for load in g_loads:
        load.wait()
    wait_bytes(first.at[pl.ds(0, grid.nz - 1)], first_recv)

    for k in range(groups):
        for e in range(per):
            block = first[k * per + e].astype(F32)
            for p in range(2):
                for q in range(nq):
                    first_rows[k, q, p * per + e : p * per + e + 1, :] = block[p * nq + q : p * nq + q + 1, :]
        for q in range(nq):
            vall[0, k, q * ny + y] = first_rows[k, q].astype(BF16)
            here = vall.at[0, k, q * ny + y]
            for d in y_order:
                remote(here, here, send.at[0, k, S_V], recv.at[0, k, S_V + q], at_sta(z, y_peer(d)))

    def blocks_in(t):
        return n_own - (nq if t == 0 else 1)

    def columns(t, k, q):
        return vall[t, k, pl.ds(q * ny, ny)].astype(F32)

    def beta_squares(t, k):
        return beta_sq[t, k]

    def root(total, count):
        return jnp.sqrt(total * (1.0 / count) + EPS)

    def squares_of(values):
        total = jnp.sum(values[0] * values[0], axis=-1, keepdims=True)
        for value in values[1:]:
            total += jnp.sum(value * value, axis=-1, keepdims=True)
        total = lanes(total)
        return total + swap(total)

    seg = LANES // ny

    def pack(chunks):
        tile = chunks[0]
        lane = lax.broadcasted_iota(jnp.int32, tile.shape, 1)
        for i in range(1, ny):
            tile = jnp.where(lane >= i * seg, chunks[i], tile)
        return tile

    def unpack(tile):
        return jnp.stack([lanes(tile[:, i * seg : i * seg + 1]) for i in range(ny)])

    contract = (((1,), (1,)), ((), ()))

    slot = quad * ny + y

    def stage_a1(t, k):
        product = jnp.zeros((ny * PART, 2 * rows_half), F32)
        values = []
        for i in range(nq):
            q = by_distance(i, False)
            own_column = t == 0 or i == 0
            wait_bytes(vall.at[t, k, pl.ds(0, ny - 1 if own_column else ny)], recv.at[t, k, S_V + q])
            values.append(columns(t, k, q))
            left = values[i].reshape(ny * PART, width).astype(BF16)
            product += lax.dot_general(left, gmat[q], contract, preferred_element_type=F32)
        product = product.reshape(ny, PART, 2 * rows_half)
        turned = swap(product[..., rows_half:])
        image = product[..., :rows_half] + jnp.where(is_re(turned.shape), -turned, turned)
        if t == 0:
            scalars = jnp.zeros((ny, PART, LANES), F32)
            shape = image.shape
            event = event_of(k, shape)
            part_re = is_re(shape)
            per_src = station_ref.shape[1]
            for n in range(per_src):
                both = jnp.where(part_re, jnp.broadcast_to(station_ref[0, n : n + 1, :][None], shape),
                                 jnp.broadcast_to(station_ref[1, n : n + 1, :][None], shape))
                image -= jnp.where(event == src * per_src + n, alpha[k] * both, 0.0)
        else:
            scalars = encode(squares_of([columns(t, k, q) for q in range(nq)]))
        a1_in[t, k, xc, 0:ny] = image.astype(BF16)
        a1_in[t, k, xc, ny] = pack(scalars).astype(BF16)
        here = a1_in.at[t, k, xc]
        for d in range(1, nxc):
            remote(here, here, send.at[t, k, S_A1], recv.at[t, k, S_A1], at_src(zh * nxc + lax.rem(xc + d, nxc)))

    def stage_a2(t, k):
        wait_bytes(a1_in.at[t, k, pl.ds(0, nxc - 1)], recv.at[t, k, S_A1])
        total = a1_in[t, k, 0].astype(F32)
        for i in range(1, nxc):
            total += a1_in[t, k, i].astype(F32)
        a2_in[t, k, zh, 0:ny] = total[0:ny].astype(BF16)
        a2_in[t, k, zh, ny] = encode(decode(total[ny])).astype(BF16)
        here = a2_in.at[t, k, zh]
        remote(here, here, send.at[t, k, S_A2], recv.at[t, k, S_A2], at_src((1 - zh) * nxc + xc))

    def stage_a3(t, k):
        wait_bytes(a2_in.at[t, k, 0], recv.at[t, k, S_A2])
        total = a2_in[t, k, 0].astype(F32) + a2_in[t, k, 1].astype(F32)
        vector = total[0:ny]
        if t > 0:
            alpha[k] = root(unpack(decode(total[ny])), cols_total)
            wait_bytes(beta_sq.at[t, k, pl.ds(0, ny - 1)], recv.at[t, k, S_BETA])
            beta = root(beta_squares(t, k), rows_total)
            vector = vector / alpha[k] - alpha[k] * (uhat[k] / beta)
        uhat[k] = vector
        turned = swap(vector)
        left = jnp.concatenate([vector, jnp.where(is_re(turned.shape), turned, -turned)], axis=-1)
        left = left.reshape(ny * PART, 2 * rows_half).astype(BF16)
        for i in range(nq):
            q = by_distance(i, True)
            back = jnp.dot(left, gmat[q], preferred_element_type=F32)
            b1_out[t, k, q] = back.reshape(ny, PART, width).astype(BF16)
            if i < nq - 1:
                remote(b1_out.at[t, k, q, y], b1_in.at[t, k, quad, y], send.at[t, k, S_B1],
                       recv.at[t, k, S_B1 + quad], at_sta(zhalf * nq + q, y))
            for d in y_order:
                remote(b1_out.at[t, k, q, y_peer(d)], b1_in.at[t, k, quad, y], send.at[t, k, S_B1],
                       recv.at[t, k, S_B1 + quad], at_sta(zhalf * nq + q, y_peer(d)))

            if i == 0:
                by_out[t, k] = squares_of([vector])
                for d in y_order:
                    remote(by_out.at[t, k, y_peer(d)], by_in.at[t, k, y], send.at[t, k, S_BY], recv.at[t, k, S_BY],
                           at_sta(z, y_peer(d)))

    def stage_squares(t, k):
        wait_bytes(by_in.at[t, k, pl.ds(0, ny - 1)], recv.at[t, k, S_BY])
        squares = by_out[t, k, y]
        for d in range(1, ny):
            squares += by_in[t, k, y_peer(d)]
        bq_in[t, k, quad] = squares
        here = bq_in.at[t, k, quad]
        for i in range(nq - 1):
            remote(here, here, send.at[t, k, S_BQ], recv.at[t, k, S_BQ],
                   at_sta(zhalf * nq + by_distance(i, True), y))

    def stage_b3(t, k):
        wait_bytes(bq_in.at[t, k, pl.ds(0, nq - 1)], recv.at[t, k, S_BQ])
        squares = bq_in[t, k, 0]
        for i in range(1, nq):
            squares += bq_in[t, k, i]
        b3_out[t, k, :, width:] = encode(squares).astype(BF16)
        total = b1_out[t, k, quad, y].astype(F32)
        wait_bytes(b1_in.at[t, k, 0, pl.ds(0, ny - 1)], recv.at[t, k, S_B1 + quad])
        for d in range(1, ny):
            total += b1_in[t, k, quad, y_peer(d)].astype(F32)
        for i in range(1, nq):
            q = by_distance(i, False)
            wait_bytes(b1_in.at[t, k, 0], recv.at[t, k, S_B1 + q])
            for j in range(ny):
                total += b1_in[t, k, q, j].astype(F32)
        b3_out[t, k, :, 0:width] = total.astype(BF16)
        remote(b3_out.at[t, k], b3_in.at[t, k], send.at[t, k, S_B3], recv.at[t, k, S_B3],
               at_sta((1 - zhalf) * nq + quad, y))

    def to_half(ref, send_sem, recv_sem):
        for i in range(nq):
            q = by_distance(i, True)
            for d in y_order + [0]:
                if d or i < nq - 1:
                    remote(ref, ref, send_sem, recv_sem, at_sta(zhalf * nq + q, y_peer(d)))

    def stage_b4(t, k):
        before = vall[t, k, slot].astype(F32)
        if t > 0:
            before = before / coef[k, 0, y][:, 0:1]
        wait_bytes(b3_in.at[t, k], recv.at[t, k, S_B3])
        total = b3_out[t, k].astype(F32) + b3_in[t, k].astype(F32)
        squares = decode(total[:, width:])
        beta = root(squares, rows_total)[:, 0:1]
        after = total[:, :width] * (ratio / beta) - beta * before
        after = after.astype(BF16)
        vall[t + 1, k, slot] = after
        here = vall.at[t + 1, k, slot]
        if t < ITERS - 1:
            to_half(here, send.at[t + 1, k, S_V], recv.at[t + 1, k, S_V + quad])
            beta_sq[t + 1, k, y] = squares
            for d in y_order:
                remote(beta_sq.at[t + 1, k, y], beta_sq.at[t + 1, k, y], send.at[t + 1, k, S_BETA],
                       recv.at[t + 1, k, S_BETA], at_sta(z, y_peer(d)))
        else:
            lane = lax.broadcasted_iota(jnp.int32, squares.shape, 1)
            fs1[k, slot] = jnp.where(lane < LANES // 2, squares_of([after.astype(F32)]), squares)
            to_half(fs1.at[k, slot], send.at[t + 1, k, 0], recv.at[t + 1, k, 0])
            for i in range(nq - 1):
                to = by_distance(i, True)
                remote(here, here, send.at[t, k, S_LAST], recv.at[t, k, S_LAST], at_sta(zhalf * nq + to, y))

    mine_k = lax.div(z, per)
    mine_row = lax.rem(z, per)

    def rotate(k, beta):
        rho_new = jnp.sqrt(rho[k] * rho[k] + beta * beta)
        cosine = rho[k] / rho_new
        sine = beta / rho_new
        coef[k, 0] = alpha[k]
        coef[k, 1] = cosine * phi[k] / rho_new
        coef[k, 2] = sine * alpha[k] / rho_new
        rho[k] = -cosine * alpha[k]
        phi[k] = sine * phi[k]

    def own_rows(t):
        block = jnp.stack([vall[t, mine_k, q * ny + y].astype(F32) for q in range(nq)])
        row = lax.broadcasted_iota(jnp.int32, block.shape, 1)
        result = []
        for p in range(2):
            picked = jnp.sum(jnp.where(row == p * per + mine_row, block, 0.0), axis=1, keepdims=True)
            result.append(jnp.concatenate([picked[q] for q in range(nq)], axis=-1))
        return result

    def step(t, rows):
        def scalar(i):
            return coef[mine_k, i, y, pl.ds(mine_row, 1), :][:, 0:1]

        alpha_own, step_sol, step_dir = scalar(0), scalar(1), scalar(2)
        for p in range(2):
            vector = rows[p] / alpha_own
            before = search_out[p]
            sol_out[p] = sol_out[p] + step_sol * before
            search_out[p] = vector - step_dir * before
            if t == ITERS:
                source_out[p] = vector

    for t in range(ITERS):
        for k in range(groups):
            stage_a1(t, k)
        for k in range(groups):
            stage_a2(t, k)
        for k in range(groups):
            stage_a3(t, k)
        for k in range(groups):
            stage_squares(t, k)
        if t > 0:
            for k in range(groups):
                rotate(k, root(beta_squares(t, k), rows_total))
            step(t, own_rows(t))
        for stage in (stage_b3, stage_b4):
            for k in range(groups):
                stage(t, k)

    row = lax.broadcasted_iota(jnp.int32, (PART, LANES), 0)
    lane = lax.broadcasted_iota(jnp.int32, (PART, LANES), 1)
    squares = jnp.zeros((PART, LANES), F32)
    betas = []
    for k in range(groups):
        wait_bytes(fs1.at[k, pl.ds(0, ny * nq - 1)], recv.at[ITERS, k, 0])
        beta_rows = []
        for i in range(ny):
            total = fs1[k, i]
            beta_rows.append(lanes(total[:, LANES // 2 : LANES // 2 + 1]))
            for q in range(1, nq):
                total += fs1[k, q * ny + i]
            squares = jnp.where((lax.div(lane, seg) == i) & (lax.div(row, per) == k), lanes(total[:, 0:1]), squares)
        betas.append(root(jnp.stack(beta_rows), rows_total))
    high = squares.astype(BF16).astype(F32)
    fs2[src] = jnp.where(lax.rem(lane, seg) < seg // 2, high, squares - high).astype(BF16)
    for other in range(1, -1, -1):
        for d in range(nxc):
            if other or d:
                remote(fs2.at[src], fs2.at[src], send.at[ITERS, 0, 1], recv.at[ITERS, 0, 1],
                       at_src((1 - zh if other else zh) * nxc + lax.rem(xc + d, nxc)))

    for k in range(groups):
        unorm[k] = uhat[k] / betas[k]
    per_src = station_ref.shape[1]
    for n in range(per_src):
        event = src * per_src + n
        at_y, at_z = lax.rem(event, ny), lax.div(event, ny)
        for p in range(2):
            station_out[p, n : n + 1, :] = unorm[
                lax.div(at_z, per), at_y, pl.ds(p * per + lax.rem(at_z, per), 1), :]
    for k in range(groups):
        wait_bytes(vall.at[ITERS, k, pl.ds(0, nq - 1)], recv.at[ITERS - 1, k, S_LAST])
    last_rows = own_rows(ITERS)

    wait_bytes(fs2.at[pl.ds(0, n_src - 1)], recv.at[ITERS, 0, 1])
    squares = fs2[0].astype(F32)
    for i in range(1, n_src):
        squares += fs2[i].astype(F32)
    for k in range(groups):
        kept = jnp.where(lax.div(row, per) == k, squares, 0.0)
        kept = kept + swap(kept)
        alpha[k] = root(jnp.stack([lanes(kept[:, i * seg : i * seg + 1] + kept[:, i * seg + seg // 2 : i * seg + seg // 2 + 1])
                                   for i in range(ny)]), cols_total)
        rotate(k, betas[k])
    step(ITERS, last_rows)

    def collect(values):
        shape = (ny, PART, n_events)
        lane = lax.broadcasted_iota(jnp.int32, shape, 2)
        total = jnp.zeros((1, n_events), F32)
        for k in range(groups):
            keep = (lane == event_of(k, shape)) & is_re(shape)
            kept = jnp.where(keep, values[k][..., 0:1], 0.0).reshape(ny * PART, n_events)
            total += jnp.sum(kept, axis=0, keepdims=True)
        return total

    alpha_out[...] = collect(alpha)
    rho_out[...] = collect(rho)
    phi_out[...] = collect(phi)

    wait_bytes(first.at[pl.ds(0, grid.nz - 1)], first_send)
    wait_bytes(fs2.at[pl.ds(0, n_src - 1)], send.at[ITERS, 0, 1])
    for k in range(groups):
        wait_bytes(fs1.at[k, pl.ds(0, ny * nq - 1)], send.at[ITERS, k, 0])
        for t in range(ITERS):
            wait_bytes(a1_in.at[t, k, pl.ds(0, nxc - 1)], send.at[t, k, S_A1])
            wait_bytes(a2_in.at[t, k, 0], send.at[t, k, S_A2])
            wait_bytes(by_in.at[t, k, pl.ds(0, ny - 1)], send.at[t, k, S_BY])
            wait_bytes(bq_in.at[t, k, pl.ds(0, nq - 1)], send.at[t, k, S_BQ])
            wait_bytes(vall.at[t, k, pl.ds(0, blocks_in(t))], send.at[t, k, S_V])
            wait_bytes(vall.at[t, k, pl.ds(0, n_own - 1)], send.at[t, k, S_B1])
            wait_bytes(b3_in.at[t, k], send.at[t, k, S_B3])
            if t > 0:
                wait_bytes(beta_sq.at[t, k, pl.ds(0, ny - 1)], send.at[t, k, S_BETA])
        wait_bytes(vall.at[ITERS, k, pl.ds(0, nq - 1)], send.at[ITERS - 1, k, S_LAST])


def deliver(n, *refs):
    copies = [pltpu.make_async_copy(refs[i], refs[n + i], refs[2 * n].at[i]) for i in range(n)]
    for copy in copies:
        copy.start()
    for copy in copies:
        copy.wait()


def shards(grid, *args):
    green_real, station, source = args[0], args[2], args[3]
    rows = green_real.shape[0]
    rows_total = rows * lax.axis_size("sta")
    cols_total = green_real.shape[1] * lax.axis_size("src")
    ny, nq, groups = grid.ny, grid.nq, grid.groups
    width = green_real.shape[1] // nq
    padded = width + LANES
    n_events = args[6].shape[0]
    args = list(args[:6]) + [a.reshape(1, n_events) for a in args[6:]]
    vmem = pl.BlockSpec(memory_space=pltpu.VMEM)
    hbm = pl.BlockSpec(memory_space=pltpu.HBM)

    def buf(*shape, kind=BF16):
        return pltpu.VMEM(shape, kind)

    scratch = [
        buf(*station.shape, kind=F32),
        buf(*source.shape, kind=F32),
        buf(1, n_events, kind=F32),
        buf(1, n_events, kind=F32),
        buf(1, n_events, kind=F32),
        buf(nq, 2 * rows, width),
        buf(grid.nz, 2 * nq, width),
        buf(groups, nq, PART, width, kind=F32),
        buf(ITERS + 1, groups, ny * nq, PART, width),
        buf(ITERS, groups, grid.nxc, ny + 1, PART, LANES),
        buf(ITERS, groups, grid.nzh, ny + 1, PART, LANES),
        buf(groups, ny * nq, PART, LANES, kind=F32),
        buf(grid.nzh * grid.nxc, PART, LANES),
        buf(ITERS, groups, nq, ny, PART, width),
        buf(ITERS, groups, nq, ny, PART, width),
        buf(ITERS, groups, ny, PART, LANES, kind=F32),
        buf(ITERS, groups, ny, PART, LANES, kind=F32),
        buf(ITERS, groups, nq, PART, LANES, kind=F32),
        buf(ITERS, groups, PART, padded),
        buf(ITERS, groups, PART, padded),
        buf(ITERS, groups, ny, PART, LANES, kind=F32),
        buf(groups, ny, PART, rows, kind=F32),
        buf(groups, ny, PART, rows, kind=F32),
        buf(groups, 3, ny, PART, LANES, kind=F32),
        pltpu.SemaphoreType.DMA((7 + 2 * nq,)),
        pltpu.SemaphoreType.DMA,
        pltpu.SemaphoreType.DMA,
        pltpu.SemaphoreType.DMA((ITERS + 1, groups, 7 + 2 * nq)),
        pltpu.SemaphoreType.DMA((ITERS + 1, groups, 7 + 2 * nq)),
    ]
    shapes = [station.shape, source.shape, source.shape, source.shape] + [(1, n_events)] * 3
    shapes = [jax.ShapeDtypeStruct(shape, F32) for shape in shapes]
    outs = pl.pallas_call(
        functools.partial(kernel, grid, rows_total, cols_total),
        out_shape=shapes,
        in_specs=[hbm] * 9,
        out_specs=[vmem] * 7,
        scratch_shapes=scratch,
        compiler_params=pltpu.CompilerParams(
            collective_id=0, has_side_effects=True),
        name="lsqr",
    )(*args)
    outs = pl.pallas_call(
        functools.partial(deliver, len(outs)),
        out_shape=shapes,
        in_specs=[vmem] * 7,
        out_specs=[hbm] * 7,
        scratch_shapes=[pltpu.SemaphoreType.DMA((7,))],
        name="deliver",
    )(*outs)
    return tuple(outs[:4]) + tuple(a.reshape(n_events) for a in outs[4:])


def build(mesh, grid):
    placed = (
        P("sta", "src"),
        P("sta", "src"),
        P(None, "src", "sta"),
        P(None, "sta", "src"),
        P(None, "sta", "src"),
        P(None, "sta", "src"),
        P(),
        P(),
        P(),
    )
    return jax.shard_map(
        functools.partial(shards, grid),
        mesh=mesh,
        in_specs=placed,
        out_specs=placed[2:],
        check_vma=False,
    )


def solution(mesh):
    return build(mesh, FULL)
```

```python
import functools

import jax
import jax.numpy as jnp
from jax import lax
from jax.experimental import pallas as pl
from jax.experimental.pallas import tpu as pltpu
from jax.sharding import PartitionSpec as P

ITERS = 3
EPS = 1e-06
MESH = pl.DeviceIdType.MESH
F32 = jnp.float32
BF16 = jnp.bfloat16
LANES = 128
PART = 8


class Grid:
    def __init__(self, ny, nq, nhalf, nzh, nx, ncore):
        self.ny, self.nq, self.nhalf = ny, nq, nhalf
        self.nzh, self.nx, self.ncore = nzh, nx, ncore
        self.nz = nq * nhalf
        self.nxc = nx * ncore
        self.groups = 2 * self.nz // PART
        self.per = self.nz // self.groups


FULL = Grid(4, 4, 2, 2, 4, 2)


def kernel(grid, rows_total, cols_total, *refs):
    (green_re, green_im, station_in, source_in, search_in, sol_in, alpha_in, rho_in, phi_in,
     station_out, source_out, search_out, sol_out, alpha_out, rho_out, phi_out,
     station_ref, source_ref, alpha_ref, rho_ref, phi_ref,
     gmat, first, first_rows, vall, a1_in, a2_in, fs1, fs2,
     b1_out, b1_in, by_in, bq_in, b3_out, b3_in, beta_sq,
     uhat, unorm, coef, load_sem, first_send, first_recv, send, recv) = refs
    ny, nq, nxc, groups, per = grid.ny, grid.nq, grid.nxc, grid.groups, grid.per
    n_src = grid.nzh * nxc
    width = source_ref.shape[-1] // nq
    rows_half = gmat.shape[1] // 2
    ratio = cols_total / rows_total
    S_A1, S_A2, S_B3, S_BETA, S_LAST, S_BY, S_BQ, S_V, S_B1 = *range(8), 7 + nq
    n_own = ny * nq

    sta = lax.axis_index("sta")
    src = lax.axis_index("src")
    y = lax.rem(sta, ny)
    z = lax.div(sta, ny)
    quad = lax.rem(z, nq)
    zhalf = lax.div(z, nq)
    zh = lax.div(src, nxc)
    xc = lax.rem(src, nxc)

    def at_sta(z_at, y_at):
        return {"sta": z_at * ny + y_at, "src": src}

    def at_src(src_to):
        return {"sta": sta, "src": src_to}

    def y_peer(d):
        return lax.rem(y + d, ny)

    def by_distance(i, far_first):
        sign = -1 if far_first else 1
        table = [sorted(range(nq), key=lambda q: sign * abs(q - p))[i] for p in range(nq)]
        value = jnp.int32(table[0])
        for p in range(1, nq):
            value = jnp.where(quad == p, table[p], value)
        return value

    y_order = sorted(range(1, ny), key=lambda d: -min(d, ny - d))
    peers = []
    for d in range(1, grid.nz):
        peers.append(at_sta(lax.rem(z + d, grid.nz), y))
    for d in range(1, ny):
        for e in range(nq):
            peers.append(at_sta(zhalf * nq + lax.rem(quad + e, nq), y_peer(d)))
    for d in range(1, n_src):
        peers.append(at_src(lax.rem(src + d, n_src)))
    barrier = pltpu.get_barrier_semaphore()
    for peer in peers:
        pl.semaphore_signal(barrier, inc=1, device_id=peer, device_id_type=MESH)

    loads = [
        pltpu.make_async_copy(a, b, load_sem.at[i])
        for i, (a, b) in enumerate((
            (source_in, source_ref), (station_in, station_ref), (alpha_in, alpha_ref), (rho_in, rho_ref),
            (phi_in, phi_ref), (search_in, search_out), (sol_in, sol_out)))
    ]
    g_loads = []
    for q in range(nq):
        cut = pl.ds(q * width, width)
        for p, green in enumerate((green_re, green_im)):
            g_loads.append(pltpu.make_async_copy(
                green.at[:, cut], gmat.at[q, pl.ds(p * rows_half, rows_half)],
                load_sem.at[len(loads) + 2 * q + p]))
    for load in loads + g_loads:
        load.start()
    for load in loads:
        load.wait()

    pieces = [source_ref[p, :, q * width : (q + 1) * width] for p in range(2) for q in range(nq)]
    first[z] = jnp.concatenate(pieces, axis=0).astype(BF16)

    def remote(src_at, dst_at, send_sem, recv_sem, to):
        pltpu.make_async_remote_copy(
            src_ref=src_at, dst_ref=dst_at, send_sem=send_sem, recv_sem=recv_sem,
            device_id=to, device_id_type=MESH).start()

    def wait_bytes(ref, sem):
        pltpu.make_async_copy(ref, ref, sem).wait()

    def is_re(shape):
        return lax.broadcasted_iota(jnp.int32, shape, len(shape) - 2) < per

    def swap(a):
        return pltpu.roll(a, per, a.ndim - 2)

    def encode(total):
        high = total.astype(BF16).astype(F32)
        return jnp.where(is_re(total.shape), high, total - high)

    def decode(pair):
        return pair + swap(pair)

    def lanes(a):
        return jnp.broadcast_to(a, a.shape[:-1] + (LANES,))

    def event_of(k, shape):
        zl = lax.rem(lax.broadcasted_iota(jnp.int32, shape, 1), per)
        return (k * per + zl) * ny + lax.broadcasted_iota(jnp.int32, shape, 0)

    n_events = alpha_ref.shape[-1]

    def spread(ref, k):
        shape = (ny, PART, n_events)
        lane = lax.broadcasted_iota(jnp.int32, shape, 2)
        row = jnp.broadcast_to(ref[...].reshape(1, 1, n_events), shape)
        return lanes(jnp.sum(jnp.where(lane == event_of(k, shape), row, 0.0), axis=-1, keepdims=True))

    alpha = [spread(alpha_ref, k) for k in range(groups)]
    rho = [spread(rho_ref, k) for k in range(groups)]
    phi = [spread(phi_ref, k) for k in range(groups)]

    pl.semaphore_wait(barrier, len(peers))

    for d in range(grid.nz - 1, 0, -1):
        remote(first.at[z], first.at[z], first_send, first_recv, at_sta(lax.rem(z + d, grid.nz), y))
    for load in g_loads:
        load.wait()
    wait_bytes(first.at[pl.ds(0, grid.nz - 1)], first_recv)

    for k in range(groups):
        for e in range(per):
            block = first[k * per + e].astype(F32)
            for p in range(2):
                for q in range(nq):
                    first_rows[k, q, p * per + e : p * per + e + 1, :] = block[p * nq + q : p * nq + q + 1, :]
        for q in range(nq):
            vall[0, k, q * ny + y] = first_rows[k, q].astype(BF16)
            here = vall.at[0, k, q * ny + y]
            for d in y_order:
                remote(here, here, send.at[0, k, S_V], recv.at[0, k, S_V + q], at_sta(z, y_peer(d)))

    def blocks_in(t):
        return n_own - (nq if t == 0 else 1)

    def columns(t, k, q):
        return vall[t, k, pl.ds(q * ny, ny)].astype(F32)

    def beta_squares(t, k):
        return beta_sq[t, k]

    def root(total, count):
        return jnp.sqrt(total * (1.0 / count) + EPS)

    def squares_of(values):
        total = jnp.sum(values[0] * values[0], axis=-1, keepdims=True)
        for value in values[1:]:
            total += jnp.sum(value * value, axis=-1, keepdims=True)
        total = lanes(total)
        return total + swap(total)

    seg = LANES // ny

    def pack(chunks):
        tile = chunks[0]
        lane = lax.broadcasted_iota(jnp.int32, tile.shape, 1)
        for i in range(1, ny):
            tile = jnp.where(lane >= i * seg, chunks[i], tile)
        return tile

    def unpack(tile):
        return jnp.stack([lanes(tile[:, i * seg : i * seg + 1]) for i in range(ny)])

    contract = (((1,), (1,)), ((), ()))

    slot = quad * ny + y

    def stage_a1(t, k):
        product = jnp.zeros((ny * PART, 2 * rows_half), F32)
        values = []
        for i in range(nq):
            q = by_distance(i, False)
            own_column = t == 0 or i == 0
            wait_bytes(vall.at[t, k, pl.ds(0, ny - 1 if own_column else ny)], recv.at[t, k, S_V + q])
            values.append(columns(t, k, q))
            left = values[i].reshape(ny * PART, width).astype(BF16)
            product += lax.dot_general(left, gmat[q], contract, preferred_element_type=F32)
        product = product.reshape(ny, PART, 2 * rows_half)
        turned = swap(product[..., rows_half:])
        image = product[..., :rows_half] + jnp.where(is_re(turned.shape), -turned, turned)
        if t == 0:
            scalars = jnp.zeros((ny, PART, LANES), F32)
            shape = image.shape
            event = event_of(k, shape)
            part_re = is_re(shape)
            per_src = station_ref.shape[1]
            for n in range(per_src):
                both = jnp.where(part_re, jnp.broadcast_to(station_ref[0, n : n + 1, :][None], shape),
                                 jnp.broadcast_to(station_ref[1, n : n + 1, :][None], shape))
                image -= jnp.where(event == src * per_src + n, alpha[k] * both, 0.0)
        else:
            scalars = encode(squares_of([columns(t, k, q) for q in range(nq)]))
        a1_in[t, k, xc, 0:ny] = image.astype(BF16)
        a1_in[t, k, xc, ny] = pack(scalars).astype(BF16)
        here = a1_in.at[t, k, xc]
        for d in range(1, nxc):
            remote(here, here, send.at[t, k, S_A1], recv.at[t, k, S_A1], at_src(zh * nxc + lax.rem(xc + d, nxc)))

    def stage_a2(t, k):
        wait_bytes(a1_in.at[t, k, pl.ds(0, nxc - 1)], recv.at[t, k, S_A1])
        total = a1_in[t, k, 0].astype(F32)
        for i in range(1, nxc):
            total += a1_in[t, k, i].astype(F32)
        a2_in[t, k, zh, 0:ny] = total[0:ny].astype(BF16)
        a2_in[t, k, zh, ny] = encode(decode(total[ny])).astype(BF16)
        here = a2_in.at[t, k, zh]
        remote(here, here, send.at[t, k, S_A2], recv.at[t, k, S_A2], at_src((1 - zh) * nxc + xc))

    def stage_a3(t, k):
        wait_bytes(a2_in.at[t, k, 0], recv.at[t, k, S_A2])
        total = a2_in[t, k, 0].astype(F32) + a2_in[t, k, 1].astype(F32)
        vector = total[0:ny]
        if t > 0:
            alpha[k] = root(unpack(decode(total[ny])), cols_total)
            wait_bytes(beta_sq.at[t, k, pl.ds(0, ny - 1)], recv.at[t, k, S_BETA])
            beta = root(beta_squares(t, k), rows_total)
            vector = vector / alpha[k] - alpha[k] * (uhat[k] / beta)
        uhat[k] = vector
        bq_in[t, k, quad] = pack(squares_of([vector]))
        here = bq_in.at[t, k, quad]
        for i in range(nq - 1):
            remote(here, here, send.at[t, k, S_BQ], recv.at[t, k, S_BQ],
                   at_sta(zhalf * nq + by_distance(i, True), y))
        turned = swap(vector)
        left = jnp.concatenate([vector, jnp.where(is_re(turned.shape), turned, -turned)], axis=-1)
        left = left.reshape(ny * PART, 2 * rows_half).astype(BF16)
        for i in range(nq):
            q = by_distance(i, True)
            back = jnp.dot(left, gmat[q], preferred_element_type=F32)
            b1_out[t, k, q] = back.reshape(ny, PART, width).astype(BF16)
            if i < nq - 1:
                remote(b1_out.at[t, k, q, y], b1_in.at[t, k, quad, y], send.at[t, k, S_B1],
                       recv.at[t, k, S_B1 + quad], at_sta(zhalf * nq + q, y))
            for d in y_order:
                remote(b1_out.at[t, k, q, y_peer(d)], b1_in.at[t, k, quad, y], send.at[t, k, S_B1],
                       recv.at[t, k, S_B1 + quad], at_sta(zhalf * nq + q, y_peer(d)))


    def stage_squares(t, k):
        wait_bytes(bq_in.at[t, k, pl.ds(0, nq - 1)], recv.at[t, k, S_BQ])
        squares = bq_in[t, k, 0]
        for i in range(1, nq):
            squares += bq_in[t, k, i]
        by_in[t, k, y] = squares
        here = by_in.at[t, k, y]
        for d in y_order:
            remote(here, here, send.at[t, k, S_BY], recv.at[t, k, S_BY], at_sta(z, y_peer(d)))

    def stage_b3(t, k):
        wait_bytes(by_in.at[t, k, pl.ds(0, ny - 1)], recv.at[t, k, S_BY])
        total = by_in[t, k, 0]
        for i in range(1, ny):
            total += by_in[t, k, i]
        squares = jnp.zeros((PART, LANES), F32)
        for i in range(ny):
            squares = jnp.where(y == i, lanes(total[:, i * seg : i * seg + 1]), squares)
        b3_out[t, k, :, width:] = encode(squares).astype(BF16)
        total = b1_out[t, k, quad, y].astype(F32)
        wait_bytes(b1_in.at[t, k, 0, pl.ds(0, ny - 1)], recv.at[t, k, S_B1 + quad])
        for d in range(1, ny):
            total += b1_in[t, k, quad, y_peer(d)].astype(F32)
        for i in range(1, nq):
            q = by_distance(i, False)
            wait_bytes(b1_in.at[t, k, 0], recv.at[t, k, S_B1 + q])
            for j in range(ny):
                total += b1_in[t, k, q, j].astype(F32)
        b3_out[t, k, :, 0:width] = total.astype(BF16)
        remote(b3_out.at[t, k], b3_in.at[t, k], send.at[t, k, S_B3], recv.at[t, k, S_B3],
               at_sta((1 - zhalf) * nq + quad, y))

    def to_half(ref, send_sem, recv_sem):
        for i in range(nq):
            q = by_distance(i, True)
            for d in y_order + [0]:
                if d or i < nq - 1:
                    remote(ref, ref, send_sem, recv_sem, at_sta(zhalf * nq + q, y_peer(d)))

    def stage_b4(t, k):
        before = vall[t, k, slot].astype(F32)
        if t > 0:
            before = before / coef[k, 0, y][:, 0:1]
        wait_bytes(b3_in.at[t, k], recv.at[t, k, S_B3])
        total = b3_out[t, k].astype(F32) + b3_in[t, k].astype(F32)
        squares = decode(total[:, width:])
        beta = root(squares, rows_total)[:, 0:1]
        after = total[:, :width] * (ratio / beta) - beta * before
        after = after.astype(BF16)
        vall[t + 1, k, slot] = after
        here = vall.at[t + 1, k, slot]
        if t < ITERS - 1:
            to_half(here, send.at[t + 1, k, S_V], recv.at[t + 1, k, S_V + quad])
            beta_sq[t + 1, k, y] = squares
            for d in y_order:
                remote(beta_sq.at[t + 1, k, y], beta_sq.at[t + 1, k, y], send.at[t + 1, k, S_BETA],
                       recv.at[t + 1, k, S_BETA], at_sta(z, y_peer(d)))
        else:
            lane = lax.broadcasted_iota(jnp.int32, squares.shape, 1)
            fs1[k, slot] = jnp.where(lane < LANES // 2, squares_of([after.astype(F32)]), squares)
            to_half(fs1.at[k, slot], send.at[t + 1, k, 0], recv.at[t + 1, k, 0])
            for i in range(nq - 1):
                to = by_distance(i, True)
                remote(here, here, send.at[t, k, S_LAST], recv.at[t, k, S_LAST], at_sta(zhalf * nq + to, y))

    mine_k = lax.div(z, per)
    mine_row = lax.rem(z, per)

    def rotate(k, beta):
        rho_new = jnp.sqrt(rho[k] * rho[k] + beta * beta)
        cosine = rho[k] / rho_new
        sine = beta / rho_new
        coef[k, 0] = alpha[k]
        coef[k, 1] = cosine * phi[k] / rho_new
        coef[k, 2] = sine * alpha[k] / rho_new
        rho[k] = -cosine * alpha[k]
        phi[k] = sine * phi[k]

    def own_rows(t):
        block = jnp.stack([vall[t, mine_k, q * ny + y].astype(F32) for q in range(nq)])
        row = lax.broadcasted_iota(jnp.int32, block.shape, 1)
        result = []
        for p in range(2):
            picked = jnp.sum(jnp.where(row == p * per + mine_row, block, 0.0), axis=1, keepdims=True)
            result.append(jnp.concatenate([picked[q] for q in range(nq)], axis=-1))
        return result

    def step(t, rows):
        def scalar(i):
            return coef[mine_k, i, y, pl.ds(mine_row, 1), :][:, 0:1]

        alpha_own, step_sol, step_dir = scalar(0), scalar(1), scalar(2)
        for p in range(2):
            vector = rows[p] / alpha_own
            before = search_out[p]
            sol_out[p] = sol_out[p] + step_sol * before
            search_out[p] = vector - step_dir * before
            if t == ITERS:
                source_out[p] = vector

    for t in range(ITERS):
        for k in range(groups):
            stage_a1(t, k)
        for k in range(groups):
            stage_a2(t, k)
        for k in range(groups):
            stage_a3(t, k)
        for k in range(groups):
            stage_squares(t, k)
        if t > 0:
            for k in range(groups):
                rotate(k, root(beta_squares(t, k), rows_total))
            step(t, own_rows(t))
        for stage in (stage_b3, stage_b4):
            for k in range(groups):
                stage(t, k)

    row = lax.broadcasted_iota(jnp.int32, (PART, LANES), 0)
    lane = lax.broadcasted_iota(jnp.int32, (PART, LANES), 1)
    squares = jnp.zeros((PART, LANES), F32)
    betas = []
    for k in range(groups):
        wait_bytes(fs1.at[k, pl.ds(0, ny * nq - 1)], recv.at[ITERS, k, 0])
        beta_rows = []
        for i in range(ny):
            total = fs1[k, i]
            beta_rows.append(lanes(total[:, LANES // 2 : LANES // 2 + 1]))
            for q in range(1, nq):
                total += fs1[k, q * ny + i]
            squares = jnp.where((lax.div(lane, seg) == i) & (lax.div(row, per) == k), lanes(total[:, 0:1]), squares)
        betas.append(root(jnp.stack(beta_rows), rows_total))
    high = squares.astype(BF16).astype(F32)
    fs2[src] = jnp.where(lax.rem(lane, seg) < seg // 2, high, squares - high).astype(BF16)
    for other in range(1, -1, -1):
        for d in range(nxc):
            if other or d:
                remote(fs2.at[src], fs2.at[src], send.at[ITERS, 0, 1], recv.at[ITERS, 0, 1],
                       at_src((1 - zh if other else zh) * nxc + lax.rem(xc + d, nxc)))

    for k in range(groups):
        unorm[k] = uhat[k] / betas[k]
    per_src = station_ref.shape[1]
    for n in range(per_src):
        event = src * per_src + n
        at_y, at_z = lax.rem(event, ny), lax.div(event, ny)
        for p in range(2):
            station_out[p, n : n + 1, :] = unorm[
                lax.div(at_z, per), at_y, pl.ds(p * per + lax.rem(at_z, per), 1), :]
    for k in range(groups):
        wait_bytes(vall.at[ITERS, k, pl.ds(0, nq - 1)], recv.at[ITERS - 1, k, S_LAST])
    last_rows = own_rows(ITERS)

    wait_bytes(fs2.at[pl.ds(0, n_src - 1)], recv.at[ITERS, 0, 1])
    squares = fs2[0].astype(F32)
    for i in range(1, n_src):
        squares += fs2[i].astype(F32)
    for k in range(groups):
        kept = jnp.where(lax.div(row, per) == k, squares, 0.0)
        kept = kept + swap(kept)
        alpha[k] = root(jnp.stack([lanes(kept[:, i * seg : i * seg + 1] + kept[:, i * seg + seg // 2 : i * seg + seg // 2 + 1])
                                   for i in range(ny)]), cols_total)
        rotate(k, betas[k])
    step(ITERS, last_rows)

    def collect(values):
        shape = (ny, PART, n_events)
        lane = lax.broadcasted_iota(jnp.int32, shape, 2)
        total = jnp.zeros((1, n_events), F32)
        for k in range(groups):
            keep = (lane == event_of(k, shape)) & is_re(shape)
            kept = jnp.where(keep, values[k][..., 0:1], 0.0).reshape(ny * PART, n_events)
            total += jnp.sum(kept, axis=0, keepdims=True)
        return total

    alpha_out[...] = collect(alpha)
    rho_out[...] = collect(rho)
    phi_out[...] = collect(phi)

    wait_bytes(first.at[pl.ds(0, grid.nz - 1)], first_send)
    wait_bytes(fs2.at[pl.ds(0, n_src - 1)], send.at[ITERS, 0, 1])
    for k in range(groups):
        wait_bytes(fs1.at[k, pl.ds(0, ny * nq - 1)], send.at[ITERS, k, 0])
        for t in range(ITERS):
            wait_bytes(a1_in.at[t, k, pl.ds(0, nxc - 1)], send.at[t, k, S_A1])
            wait_bytes(a2_in.at[t, k, 0], send.at[t, k, S_A2])
            wait_bytes(by_in.at[t, k, pl.ds(0, ny - 1)], send.at[t, k, S_BY])
            wait_bytes(bq_in.at[t, k, pl.ds(0, nq - 1)], send.at[t, k, S_BQ])
            wait_bytes(vall.at[t, k, pl.ds(0, blocks_in(t))], send.at[t, k, S_V])
            wait_bytes(vall.at[t, k, pl.ds(0, n_own - 1)], send.at[t, k, S_B1])
            wait_bytes(b3_in.at[t, k], send.at[t, k, S_B3])
            if t > 0:
                wait_bytes(beta_sq.at[t, k, pl.ds(0, ny - 1)], send.at[t, k, S_BETA])
        wait_bytes(vall.at[ITERS, k, pl.ds(0, nq - 1)], send.at[ITERS - 1, k, S_LAST])


def deliver(n, *refs):
    copies = [pltpu.make_async_copy(refs[i], refs[n + i], refs[2 * n].at[i]) for i in range(n)]
    for copy in copies:
        copy.start()
    for copy in copies:
        copy.wait()


def shards(grid, *args):
    green_real, station, source = args[0], args[2], args[3]
    rows = green_real.shape[0]
    rows_total = rows * lax.axis_size("sta")
    cols_total = green_real.shape[1] * lax.axis_size("src")
    ny, nq, groups = grid.ny, grid.nq, grid.groups
    width = green_real.shape[1] // nq
    padded = width + LANES
    n_events = args[6].shape[0]
    args = list(args[:6]) + [a.reshape(1, n_events) for a in args[6:]]
    vmem = pl.BlockSpec(memory_space=pltpu.VMEM)
    hbm = pl.BlockSpec(memory_space=pltpu.HBM)

    def buf(*shape, kind=BF16):
        return pltpu.VMEM(shape, kind)

    scratch = [
        buf(*station.shape, kind=F32),
        buf(*source.shape, kind=F32),
        buf(1, n_events, kind=F32),
        buf(1, n_events, kind=F32),
        buf(1, n_events, kind=F32),
        buf(nq, 2 * rows, width),
        buf(grid.nz, 2 * nq, width),
        buf(groups, nq, PART, width, kind=F32),
        buf(ITERS + 1, groups, ny * nq, PART, width),
        buf(ITERS, groups, grid.nxc, ny + 1, PART, LANES),
        buf(ITERS, groups, grid.nzh, ny + 1, PART, LANES),
        buf(groups, ny * nq, PART, LANES, kind=F32),
        buf(grid.nzh * grid.nxc, PART, LANES),
        buf(ITERS, groups, nq, ny, PART, width),
        buf(ITERS, groups, nq, ny, PART, width),
        buf(ITERS, groups, ny, PART, LANES, kind=F32),
        buf(ITERS, groups, nq, PART, LANES, kind=F32),
        buf(ITERS, groups, PART, padded),
        buf(ITERS, groups, PART, padded),
        buf(ITERS, groups, ny, PART, LANES, kind=F32),
        buf(groups, ny, PART, rows, kind=F32),
        buf(groups, ny, PART, rows, kind=F32),
        buf(groups, 3, ny, PART, LANES, kind=F32),
        pltpu.SemaphoreType.DMA((7 + 2 * nq,)),
        pltpu.SemaphoreType.DMA,
        pltpu.SemaphoreType.DMA,
        pltpu.SemaphoreType.DMA((ITERS + 1, groups, 7 + 2 * nq)),
        pltpu.SemaphoreType.DMA((ITERS + 1, groups, 7 + 2 * nq)),
    ]
    shapes = [station.shape, source.shape, source.shape, source.shape] + [(1, n_events)] * 3
    shapes = [jax.ShapeDtypeStruct(shape, F32) for shape in shapes]
    outs = pl.pallas_call(
        functools.partial(kernel, grid, rows_total, cols_total),
        out_shape=shapes,
        in_specs=[hbm] * 9,
        out_specs=[vmem] * 7,
        scratch_shapes=scratch,
        compiler_params=pltpu.CompilerParams(
            collective_id=0, has_side_effects=True),
        name="lsqr",
    )(*args)
    outs = pl.pallas_call(
        functools.partial(deliver, len(outs)),
        out_shape=shapes,
        in_specs=[vmem] * 7,
        out_specs=[hbm] * 7,
        scratch_shapes=[pltpu.SemaphoreType.DMA((7,))],
        name="deliver",
    )(*outs)
    return tuple(outs[:4]) + tuple(a.reshape(n_events) for a in outs[4:])


def build(mesh, grid):
    placed = (
        P("sta", "src"),
        P("sta", "src"),
        P(None, "src", "sta"),
        P(None, "sta", "src"),
        P(None, "sta", "src"),
        P(None, "sta", "src"),
        P(),
        P(),
        P(),
    )
    return jax.shard_map(
        functools.partial(shards, grid),
        mesh=mesh,
        in_specs=placed,
        out_specs=placed[2:],
        check_vma=False,
    )


def solution(mesh):
    return build(mesh, FULL)
```

```python
import functools

import jax
import jax.numpy as jnp
from jax import lax
from jax.experimental import pallas as pl
from jax.experimental.pallas import tpu as pltpu
from jax.sharding import PartitionSpec as P

ITERS = 3
EPS = 1e-06
MESH = pl.DeviceIdType.MESH
F32 = jnp.float32
BF16 = jnp.bfloat16
LANES = 128
PART = 8


class Grid:
    def __init__(self, ny, nq, nhalf, nzh, nx, ncore):
        self.ny, self.nq, self.nhalf = ny, nq, nhalf
        self.nzh, self.nx, self.ncore = nzh, nx, ncore
        self.nz = nq * nhalf
        self.nxc = nx * ncore
        self.groups = 2 * self.nz // PART
        self.per = self.nz // self.groups


FULL = Grid(4, 4, 2, 2, 4, 2)


def kernel(grid, rows_total, cols_total, *refs):
    (green_re, green_im, station_in, source_in, search_in, sol_in, alpha_in, rho_in, phi_in,
     station_out, source_out, search_out, sol_out, alpha_out, rho_out, phi_out,
     station_ref, source_ref, alpha_ref, rho_ref, phi_ref,
     gmat, first, first_rows, vall, a1_in, a2_in, fs1, fs2,
     b1_out, b1_in, by_out, by_in, bq_in, b3_out, b3_in, beta_sq,
     uhat, unorm, coef, load_sem, first_send, first_recv, send, recv) = refs
    ny, nq, nxc, groups, per = grid.ny, grid.nq, grid.nxc, grid.groups, grid.per
    n_src = grid.nzh * nxc
    width = source_ref.shape[-1] // nq
    rows_half = gmat.shape[1] // 2
    ratio = cols_total / rows_total
    S_A1, S_A2, S_B3, S_BETA, S_LAST, S_BY, S_BQ, S_V, S_B1 = *range(8), 7 + nq
    n_own = ny * nq

    sta = lax.axis_index("sta")
    src = lax.axis_index("src")
    y = lax.rem(sta, ny)
    z = lax.div(sta, ny)
    quad = lax.rem(z, nq)
    zhalf = lax.div(z, nq)
    zh = lax.div(src, nxc)
    xc = lax.rem(src, nxc)

    def at_sta(z_at, y_at):
        return {"sta": z_at * ny + y_at, "src": src}

    def at_src(src_to):
        return {"sta": sta, "src": src_to}

    def y_peer(d):
        return lax.rem(y + d, ny)

    def by_distance(i, far_first):
        sign = -1 if far_first else 1
        table = [sorted(range(nq), key=lambda q: sign * abs(q - p))[i] for p in range(nq)]
        value = jnp.int32(table[0])
        for p in range(1, nq):
            value = jnp.where(quad == p, table[p], value)
        return value

    y_order = sorted(range(1, ny), key=lambda d: -min(d, ny - d))
    peers = []
    for d in range(1, grid.nz):
        peers.append(at_sta(lax.rem(z + d, grid.nz), y))
    for d in range(1, ny):
        for e in range(nq):
            peers.append(at_sta(zhalf * nq + lax.rem(quad + e, nq), y_peer(d)))
    for d in range(1, n_src):
        peers.append(at_src(lax.rem(src + d, n_src)))
    barrier = pltpu.get_barrier_semaphore()
    for peer in peers:
        pl.semaphore_signal(barrier, inc=1, device_id=peer, device_id_type=MESH)

    loads = [
        pltpu.make_async_copy(a, b, load_sem.at[i])
        for i, (a, b) in enumerate((
            (source_in, source_ref), (station_in, station_ref), (alpha_in, alpha_ref), (rho_in, rho_ref),
            (phi_in, phi_ref), (search_in, search_out), (sol_in, sol_out)))
    ]
    g_loads = []
    for q in range(nq):
        cut = pl.ds(q * width, width)
        for p, green in enumerate((green_re, green_im)):
            g_loads.append(pltpu.make_async_copy(
                green.at[:, cut], gmat.at[q, pl.ds(p * rows_half, rows_half)],
                load_sem.at[len(loads) + 2 * q + p]))
    for load in loads + g_loads:
        load.start()
    for load in loads:
        load.wait()

    pieces = [source_ref[p, :, q * width : (q + 1) * width] for p in range(2) for q in range(nq)]
    first[z] = jnp.concatenate(pieces, axis=0).astype(BF16)

    def remote(src_at, dst_at, send_sem, recv_sem, to):
        pltpu.make_async_remote_copy(
            src_ref=src_at, dst_ref=dst_at, send_sem=send_sem, recv_sem=recv_sem,
            device_id=to, device_id_type=MESH).start()

    def wait_bytes(ref, sem):
        pltpu.make_async_copy(ref, ref, sem).wait()

    def is_re(shape):
        return lax.broadcasted_iota(jnp.int32, shape, len(shape) - 2) < per

    def swap(a):
        return pltpu.roll(a, per, a.ndim - 2)

    def encode(total):
        high = total.astype(BF16).astype(F32)
        return jnp.where(is_re(total.shape), high, total - high)

    def decode(pair):
        return pair + swap(pair)

    def lanes(a):
        return jnp.broadcast_to(a, a.shape[:-1] + (LANES,))

    def event_of(k, shape):
        zl = lax.rem(lax.broadcasted_iota(jnp.int32, shape, 1), per)
        return (k * per + zl) * ny + lax.broadcasted_iota(jnp.int32, shape, 0)

    n_events = alpha_ref.shape[-1]

    def spread(ref, k):
        shape = (ny, PART, n_events)
        lane = lax.broadcasted_iota(jnp.int32, shape, 2)
        row = jnp.broadcast_to(ref[...].reshape(1, 1, n_events), shape)
        return lanes(jnp.sum(jnp.where(lane == event_of(k, shape), row, 0.0), axis=-1, keepdims=True))

    alpha = [spread(alpha_ref, k) for k in range(groups)]
    rho = [spread(rho_ref, k) for k in range(groups)]
    phi = [spread(phi_ref, k) for k in range(groups)]

    pl.semaphore_wait(barrier, len(peers))

    for d in range(grid.nz - 1, 0, -1):
        remote(first.at[z], first.at[z], first_send, first_recv, at_sta(lax.rem(z + d, grid.nz), y))
    for load in g_loads:
        load.wait()
    wait_bytes(first.at[pl.ds(0, grid.nz - 1)], first_recv)

    for k in range(groups):
        for e in range(per):
            block = first[k * per + e].astype(F32)
            for p in range(2):
                for q in range(nq):
                    first_rows[k, q, p * per + e : p * per + e + 1, :] = block[p * nq + q : p * nq + q + 1, :]
        for q in range(nq):
            vall[0, k, q * ny + y] = first_rows[k, q].astype(BF16)
            here = vall.at[0, k, q * ny + y]
            for d in y_order:
                remote(here, here, send.at[0, k, S_V], recv.at[0, k, S_V + q], at_sta(z, y_peer(d)))

    def blocks_in(t):
        return n_own - (nq if t == 0 else 1)

    def columns(t, k, q):
        return vall[t, k, pl.ds(q * ny, ny)].astype(F32)

    def beta_squares(t, k):
        return beta_sq[t, k]

    def root(total, count):
        return jnp.sqrt(total * (1.0 / count) + EPS)

    def squares_of(values):
        total = jnp.sum(values[0] * values[0], axis=-1, keepdims=True)
        for value in values[1:]:
            total += jnp.sum(value * value, axis=-1, keepdims=True)
        total = lanes(total)
        return total + swap(total)

    seg = LANES // ny

    def pack(chunks):
        tile = chunks[0]
        lane = lax.broadcasted_iota(jnp.int32, tile.shape, 1)
        for i in range(1, ny):
            tile = jnp.where(lane >= i * seg, chunks[i], tile)
        return tile

    def unpack(tile):
        return jnp.stack([lanes(tile[:, i * seg : i * seg + 1]) for i in range(ny)])

    contract = (((1,), (1,)), ((), ()))

    slot = quad * ny + y

    def stage_a1(t, k):
        product = jnp.zeros((ny * PART, 2 * rows_half), F32)
        values = []
        for i in range(nq):
            q = by_distance(i, False)
            own_column = t == 0 or i == 0
            wait_bytes(vall.at[t, k, pl.ds(0, ny - 1 if own_column else ny)], recv.at[t, k, S_V + q])
            values.append(columns(t, k, q))
            left = values[i].reshape(ny * PART, width).astype(BF16)
            product += lax.dot_general(left, gmat[q], contract, preferred_element_type=F32)
        product = product.reshape(ny, PART, 2 * rows_half)
        turned = swap(product[..., rows_half:])
        image = product[..., :rows_half] + jnp.where(is_re(turned.shape), -turned, turned)
        if t == 0:
            scalars = jnp.zeros((ny, PART, LANES), F32)
            shape = image.shape
            event = event_of(k, shape)
            part_re = is_re(shape)
            per_src = station_ref.shape[1]
            for n in range(per_src):
                both = jnp.where(part_re, jnp.broadcast_to(station_ref[0, n : n + 1, :][None], shape),
                                 jnp.broadcast_to(station_ref[1, n : n + 1, :][None], shape))
                image -= jnp.where(event == src * per_src + n, alpha[k] * both, 0.0)
        else:
            scalars = encode(squares_of([columns(t, k, q) for q in range(nq)]))
        a1_in[t, k, xc, 0:ny] = image.astype(BF16)
        a1_in[t, k, xc, ny] = pack(scalars).astype(BF16)
        here = a1_in.at[t, k, xc]
        for d in range(1, nxc):
            remote(here, here, send.at[t, k, S_A1], recv.at[t, k, S_A1], at_src(zh * nxc + lax.rem(xc + d, nxc)))

    def stage_a2(t, k):
        wait_bytes(a1_in.at[t, k, pl.ds(0, nxc - 1)], recv.at[t, k, S_A1])
        total = a1_in[t, k, 0].astype(F32)
        for i in range(1, nxc):
            total += a1_in[t, k, i].astype(F32)
        a2_in[t, k, zh, 0:ny] = total[0:ny].astype(BF16)
        a2_in[t, k, zh, ny] = encode(decode(total[ny])).astype(BF16)
        here = a2_in.at[t, k, zh]
        remote(here, here, send.at[t, k, S_A2], recv.at[t, k, S_A2], at_src((1 - zh) * nxc + xc))

    def stage_a3(t, k):
        wait_bytes(a2_in.at[t, k, 0], recv.at[t, k, S_A2])
        total = a2_in[t, k, 0].astype(F32) + a2_in[t, k, 1].astype(F32)
        vector = total[0:ny]
        if t > 0:
            alpha[k] = root(unpack(decode(total[ny])), cols_total)
            wait_bytes(beta_sq.at[t, k, pl.ds(0, ny - 1)], recv.at[t, k, S_BETA])
            beta = root(beta_squares(t, k), rows_total)
            vector = vector / alpha[k] - alpha[k] * (uhat[k] / beta)
        uhat[k] = vector
        turned = swap(vector)
        left = jnp.concatenate([vector, jnp.where(is_re(turned.shape), turned, -turned)], axis=-1)
        left = left.reshape(ny * PART, 2 * rows_half).astype(BF16)
        for i in range(nq):
            q = by_distance(i, True)
            back = jnp.dot(left, gmat[q], preferred_element_type=F32)
            b1_out[t, k, q] = back.reshape(ny, PART, width).astype(BF16)
            if i < nq - 1:
                remote(b1_out.at[t, k, q, y], b1_in.at[t, k, quad, y], send.at[t, k, S_B1],
                       recv.at[t, k, S_B1 + quad], at_sta(zhalf * nq + q, y))
            for d in y_order:
                remote(b1_out.at[t, k, q, y_peer(d)], b1_in.at[t, k, quad, y], send.at[t, k, S_B1],
                       recv.at[t, k, S_B1 + quad], at_sta(zhalf * nq + q, y_peer(d)))

            if i == 0:
                by_out[t, k] = squares_of([vector])
                for d in y_order:
                    remote(by_out.at[t, k, y_peer(d)], by_in.at[t, k, y], send.at[t, k, S_BY], recv.at[t, k, S_BY],
                           at_sta(z, y_peer(d)))

    def stage_squares(t, k):
        wait_bytes(by_in.at[t, k, pl.ds(0, ny - 1)], recv.at[t, k, S_BY])
        squares = by_out[t, k, y]
        for d in range(1, ny):
            squares += by_in[t, k, y_peer(d)]
        bq_in[t, k, z] = encode(squares).astype(BF16)
        here = bq_in.at[t, k, z]
        for d in range(1, grid.nz):
            remote(here, here, send.at[t, k, S_BQ], recv.at[t, k, S_BQ], at_sta(lax.rem(z + d, grid.nz), y))

    def stage_b3(t, k):
        total = b1_out[t, k, quad, y].astype(F32)
        wait_bytes(b1_in.at[t, k, 0, pl.ds(0, ny - 1)], recv.at[t, k, S_B1 + quad])
        for d in range(1, ny):
            total += b1_in[t, k, quad, y_peer(d)].astype(F32)
        for i in range(1, nq):
            q = by_distance(i, False)
            wait_bytes(b1_in.at[t, k, 0], recv.at[t, k, S_B1 + q])
            for j in range(ny):
                total += b1_in[t, k, q, j].astype(F32)
        b3_out[t, k] = total.astype(BF16)
        remote(b3_out.at[t, k], b3_in.at[t, k], send.at[t, k, S_B3], recv.at[t, k, S_B3],
               at_sta((1 - zhalf) * nq + quad, y))

    def to_half(ref, send_sem, recv_sem):
        for i in range(nq):
            q = by_distance(i, True)
            for d in y_order + [0]:
                if d or i < nq - 1:
                    remote(ref, ref, send_sem, recv_sem, at_sta(zhalf * nq + q, y_peer(d)))

    def stage_b4(t, k):
        before = vall[t, k, slot].astype(F32)
        if t > 0:
            before = before / coef[k, 0, y][:, 0:1]
        wait_bytes(b3_in.at[t, k], recv.at[t, k, S_B3])
        total = b3_out[t, k].astype(F32) + b3_in[t, k].astype(F32)
        wait_bytes(bq_in.at[t, k, pl.ds(0, grid.nz - 1)], recv.at[t, k, S_BQ])
        squares = bq_in[t, k, 0].astype(F32)
        for i in range(1, grid.nz):
            squares += bq_in[t, k, i].astype(F32)
        squares = decode(squares)
        beta = root(squares, rows_total)[:, 0:1]
        after = total * (ratio / beta) - beta * before
        after = after.astype(BF16)
        vall[t + 1, k, slot] = after
        here = vall.at[t + 1, k, slot]
        if t < ITERS - 1:
            to_half(here, send.at[t + 1, k, S_V], recv.at[t + 1, k, S_V + quad])
            beta_sq[t + 1, k, y] = squares
            for d in y_order:
                remote(beta_sq.at[t + 1, k, y], beta_sq.at[t + 1, k, y], send.at[t + 1, k, S_BETA],
                       recv.at[t + 1, k, S_BETA], at_sta(z, y_peer(d)))
        else:
            lane = lax.broadcasted_iota(jnp.int32, squares.shape, 1)
            fs1[k, slot] = jnp.where(lane < LANES // 2, squares_of([after.astype(F32)]), squares)
            to_half(fs1.at[k, slot], send.at[t + 1, k, 0], recv.at[t + 1, k, 0])
            for i in range(nq - 1):
                to = by_distance(i, True)
                remote(here, here, send.at[t, k, S_LAST], recv.at[t, k, S_LAST], at_sta(zhalf * nq + to, y))

    mine_k = lax.div(z, per)
    mine_row = lax.rem(z, per)

    def rotate(k, beta):
        rho_new = jnp.sqrt(rho[k] * rho[k] + beta * beta)
        cosine = rho[k] / rho_new
        sine = beta / rho_new
        coef[k, 0] = alpha[k]
        coef[k, 1] = cosine * phi[k] / rho_new
        coef[k, 2] = sine * alpha[k] / rho_new
        rho[k] = -cosine * alpha[k]
        phi[k] = sine * phi[k]

    def own_rows(t):
        block = jnp.stack([vall[t, mine_k, q * ny + y].astype(F32) for q in range(nq)])
        row = lax.broadcasted_iota(jnp.int32, block.shape, 1)
        result = []
        for p in range(2):
            picked = jnp.sum(jnp.where(row == p * per + mine_row, block, 0.0), axis=1, keepdims=True)
            result.append(jnp.concatenate([picked[q] for q in range(nq)], axis=-1))
        return result

    def step(t, rows):
        def scalar(i):
            return coef[mine_k, i, y, pl.ds(mine_row, 1), :][:, 0:1]

        alpha_own, step_sol, step_dir = scalar(0), scalar(1), scalar(2)
        for p in range(2):
            vector = rows[p] / alpha_own
            before = search_out[p]
            sol_out[p] = sol_out[p] + step_sol * before
            search_out[p] = vector - step_dir * before
            if t == ITERS:
                source_out[p] = vector

    for t in range(ITERS):
        for k in range(groups):
            stage_a1(t, k)
        for k in range(groups):
            stage_a2(t, k)
        for k in range(groups):
            stage_a3(t, k)
        for k in range(groups):
            stage_squares(t, k)
        if t > 0:
            for k in range(groups):
                rotate(k, root(beta_squares(t, k), rows_total))
            step(t, own_rows(t))
        for stage in (stage_b3, stage_b4):
            for k in range(groups):
                stage(t, k)

    row = lax.broadcasted_iota(jnp.int32, (PART, LANES), 0)
    lane = lax.broadcasted_iota(jnp.int32, (PART, LANES), 1)
    squares = jnp.zeros((PART, LANES), F32)
    betas = []
    for k in range(groups):
        wait_bytes(fs1.at[k, pl.ds(0, ny * nq - 1)], recv.at[ITERS, k, 0])
        beta_rows = []
        for i in range(ny):
            total = fs1[k, i]
            beta_rows.append(lanes(total[:, LANES // 2 : LANES // 2 + 1]))
            for q in range(1, nq):
                total += fs1[k, q * ny + i]
            squares = jnp.where((lax.div(lane, seg) == i) & (lax.div(row, per) == k), lanes(total[:, 0:1]), squares)
        betas.append(root(jnp.stack(beta_rows), rows_total))
    high = squares.astype(BF16).astype(F32)
    fs2[src] = jnp.where(lax.rem(lane, seg) < seg // 2, high, squares - high).astype(BF16)
    for other in range(1, -1, -1):
        for d in range(nxc):
            if other or d:
                remote(fs2.at[src], fs2.at[src], send.at[ITERS, 0, 1], recv.at[ITERS, 0, 1],
                       at_src((1 - zh if other else zh) * nxc + lax.rem(xc + d, nxc)))

    for k in range(groups):
        unorm[k] = uhat[k] / betas[k]
    per_src = station_ref.shape[1]
    for n in range(per_src):
        event = src * per_src + n
        at_y, at_z = lax.rem(event, ny), lax.div(event, ny)
        for p in range(2):
            station_out[p, n : n + 1, :] = unorm[
                lax.div(at_z, per), at_y, pl.ds(p * per + lax.rem(at_z, per), 1), :]
    for k in range(groups):
        wait_bytes(vall.at[ITERS, k, pl.ds(0, nq - 1)], recv.at[ITERS - 1, k, S_LAST])
    last_rows = own_rows(ITERS)

    wait_bytes(fs2.at[pl.ds(0, n_src - 1)], recv.at[ITERS, 0, 1])
    squares = fs2[0].astype(F32)
    for i in range(1, n_src):
        squares += fs2[i].astype(F32)
    for k in range(groups):
        kept = jnp.where(lax.div(row, per) == k, squares, 0.0)
        kept = kept + swap(kept)
        alpha[k] = root(jnp.stack([lanes(kept[:, i * seg : i * seg + 1] + kept[:, i * seg + seg // 2 : i * seg + seg // 2 + 1])
                                   for i in range(ny)]), cols_total)
        rotate(k, betas[k])
    step(ITERS, last_rows)

    def collect(values):
        shape = (ny, PART, n_events)
        lane = lax.broadcasted_iota(jnp.int32, shape, 2)
        total = jnp.zeros((1, n_events), F32)
        for k in range(groups):
            keep = (lane == event_of(k, shape)) & is_re(shape)
            kept = jnp.where(keep, values[k][..., 0:1], 0.0).reshape(ny * PART, n_events)
            total += jnp.sum(kept, axis=0, keepdims=True)
        return total

    alpha_out[...] = collect(alpha)
    rho_out[...] = collect(rho)
    phi_out[...] = collect(phi)

    wait_bytes(first.at[pl.ds(0, grid.nz - 1)], first_send)
    wait_bytes(fs2.at[pl.ds(0, n_src - 1)], send.at[ITERS, 0, 1])
    for k in range(groups):
        wait_bytes(fs1.at[k, pl.ds(0, ny * nq - 1)], send.at[ITERS, k, 0])
        for t in range(ITERS):
            wait_bytes(a1_in.at[t, k, pl.ds(0, nxc - 1)], send.at[t, k, S_A1])
            wait_bytes(a2_in.at[t, k, 0], send.at[t, k, S_A2])
            wait_bytes(by_in.at[t, k, pl.ds(0, ny - 1)], send.at[t, k, S_BY])
            wait_bytes(bq_in.at[t, k, pl.ds(0, grid.nz - 1)], send.at[t, k, S_BQ])
            wait_bytes(vall.at[t, k, pl.ds(0, blocks_in(t))], send.at[t, k, S_V])
            wait_bytes(vall.at[t, k, pl.ds(0, n_own - 1)], send.at[t, k, S_B1])
            wait_bytes(b3_in.at[t, k], send.at[t, k, S_B3])
            if t > 0:
                wait_bytes(beta_sq.at[t, k, pl.ds(0, ny - 1)], send.at[t, k, S_BETA])
        wait_bytes(vall.at[ITERS, k, pl.ds(0, nq - 1)], send.at[ITERS - 1, k, S_LAST])


def deliver(n, *refs):
    copies = [pltpu.make_async_copy(refs[i], refs[n + i], refs[2 * n].at[i]) for i in range(n)]
    for copy in copies:
        copy.start()
    for copy in copies:
        copy.wait()


def shards(grid, *args):
    green_real, station, source = args[0], args[2], args[3]
    rows = green_real.shape[0]
    rows_total = rows * lax.axis_size("sta")
    cols_total = green_real.shape[1] * lax.axis_size("src")
    ny, nq, groups = grid.ny, grid.nq, grid.groups
    width = green_real.shape[1] // nq
    n_events = args[6].shape[0]
    args = list(args[:6]) + [a.reshape(1, n_events) for a in args[6:]]
    vmem = pl.BlockSpec(memory_space=pltpu.VMEM)
    hbm = pl.BlockSpec(memory_space=pltpu.HBM)

    def buf(*shape, kind=BF16):
        return pltpu.VMEM(shape, kind)

    scratch = [
        buf(*station.shape, kind=F32),
        buf(*source.shape, kind=F32),
        buf(1, n_events, kind=F32),
        buf(1, n_events, kind=F32),
        buf(1, n_events, kind=F32),
        buf(nq, 2 * rows, width),
        buf(grid.nz, 2 * nq, width),
        buf(groups, nq, PART, width, kind=F32),
        buf(ITERS + 1, groups, ny * nq, PART, width),
        buf(ITERS, groups, grid.nxc, ny + 1, PART, LANES),
        buf(ITERS, groups, grid.nzh, ny + 1, PART, LANES),
        buf(groups, ny * nq, PART, LANES, kind=F32),
        buf(grid.nzh * grid.nxc, PART, LANES),
        buf(ITERS, groups, nq, ny, PART, width),
        buf(ITERS, groups, nq, ny, PART, width),
        buf(ITERS, groups, ny, PART, LANES, kind=F32),
        buf(ITERS, groups, ny, PART, LANES, kind=F32),
        buf(ITERS, groups, grid.nz, PART, LANES),
        buf(ITERS, groups, PART, width),
        buf(ITERS, groups, PART, width),
        buf(ITERS, groups, ny, PART, LANES, kind=F32),
        buf(groups, ny, PART, rows, kind=F32),
        buf(groups, ny, PART, rows, kind=F32),
        buf(groups, 3, ny, PART, LANES, kind=F32),
        pltpu.SemaphoreType.DMA((7 + 2 * nq,)),
        pltpu.SemaphoreType.DMA,
        pltpu.SemaphoreType.DMA,
        pltpu.SemaphoreType.DMA((ITERS + 1, groups, 7 + 2 * nq)),
        pltpu.SemaphoreType.DMA((ITERS + 1, groups, 7 + 2 * nq)),
    ]
    shapes = [station.shape, source.shape, source.shape, source.shape] + [(1, n_events)] * 3
    shapes = [jax.ShapeDtypeStruct(shape, F32) for shape in shapes]
    outs = pl.pallas_call(
        functools.partial(kernel, grid, rows_total, cols_total),
        out_shape=shapes,
        in_specs=[hbm] * 9,
        out_specs=[vmem] * 7,
        scratch_shapes=scratch,
        compiler_params=pltpu.CompilerParams(
            collective_id=0, has_side_effects=True),
        name="lsqr",
    )(*args)
    outs = pl.pallas_call(
        functools.partial(deliver, len(outs)),
        out_shape=shapes,
        in_specs=[vmem] * 7,
        out_specs=[hbm] * 7,
        scratch_shapes=[pltpu.SemaphoreType.DMA((7,))],
        name="deliver",
    )(*outs)
    return tuple(outs[:4]) + tuple(a.reshape(n_events) for a in outs[4:])


def build(mesh, grid):
    placed = (
        P("sta", "src"),
        P("sta", "src"),
        P(None, "src", "sta"),
        P(None, "sta", "src"),
        P(None, "sta", "src"),
        P(None, "sta", "src"),
        P(),
        P(),
        P(),
    )
    return jax.shard_map(
        functools.partial(shards, grid),
        mesh=mesh,
        in_specs=placed,
        out_specs=placed[2:],
        check_vma=False,
    )


def solution(mesh):
    return build(mesh, FULL)
```
